32 devices in a mesh: seq: 8 (over z, x), batch: 4 (over y, core).
Axes of the slice: x: 2, y: 2, z: 4, core: 2. Of those that a mesh axis runs over, the one named last changes fastest.
Arguments:
- inputs: float32 [4, 1024, 768], P('batch', 'seq'), may hold values from -6 to 6
- norm_gain: float32 [768], replicated, may hold values from 0.5 to 1.5
- input_projection_weight: float32 [768, 3072], replicated, may hold values from -0.21875 to 0.21875
- conv_weight: float32 [4, 1536], replicated, may hold values from -3 to 3
- conv_bias: float32 [1536], replicated, may hold values from -3 to 3
- x_proj: float32 [1536, 80], replicated, may hold values from -0.15625 to 0.15625
- step_proj: float32 [48, 1536], replicated, may hold values from -0.875 to 0.875
- step_bias: float32 [1536], replicated, may hold values from -3 to -1
- decay_code: int32 [1536], replicated, may hold values from 0 to 9
- decay_log: float32 [1536, 16], replicated, may hold values from -5 to -1.5
- skip_gain: float32 [1536], replicated, may hold values from 0.5 to 1.5
- output_projection_weight: float32 [1536, 768], replicated, may hold values from -0.15625 to 0.15625
- cotangent: float32 [4, 1024, 768], P('batch', 'seq'), may hold values from -6 to 6
Outputs:
- block_out: float32 [4, 1024, 768], P('batch', 'seq')
- input_grad: float32 [4, 1024, 768], P('batch', 'seq')
- norm_gain_grad: float32 [768], replicated
- in_proj_grad: float32 [768, 3072], replicated
- conv_weight_grad: float32 [4, 1536], replicated
- conv_bias_grad: float32 [1536], replicated
- x_proj_grad: float32 [1536, 80], replicated
- step_proj_grad: float32 [48, 1536], replicated
- step_bias_grad: float32 [1536], replicated
- decay_log_grad: float32 [1536, 16], replicated
- skip_gain_grad: float32 [1536], replicated
- out_proj_grad: float32 [1536, 768], replicated
The draws below stay inside these ranges and needn't reach their ends.
All inputs are finite; a program needn't handle non-finite values.
Results may differ from the reference program's by a relative error of at most 0.0003.
Values sent between devices are 32-bit elements; how exact they have to be, the bound alone decides.
A program may use at most 128 MiB of HBM per device.

```python
import jax
import jax.numpy as jnp
from jax import lax

D = 768
DI = 1536
N = 16
R = 48
KC = 4
QB = 32
SEQS = 4
LEN = 1024


def touch_ends(values, stream_key, low, largest):
    spot = [jax.random.randint(jax.random.fold_in(stream_key, axis), (), 0, length) for axis, length in enumerate(values.shape)]
    widest = values.shape.index(max(values.shape))
    neighbour = spot[:widest] + [(spot[widest] + 1) % values.shape[widest]] + spot[widest + 1:]
    return values.at[tuple(spot)].set(low).at[tuple(neighbour)].set(largest)


def block_levels(stream_key, extent, cuts, low, high):
    def one(axis_at, shards_of):
        draws = jax.random.uniform(jax.random.fold_in(jax.random.fold_in(stream_key, 6), axis_at), (shards_of,), jnp.float32, low / len(cuts), high / len(cuts))
        return jnp.repeat(jnp.exp(draws), extent[axis_at] // shards_of).reshape((-1,) + (1,) * (len(extent) - axis_at - 1))

    level = one(*cuts[0])
    for cut in cuts[1:]:
        level = level * one(*cut)
    return level


def centred(stream_key, extent, width, bound, shards=(), held_as=jnp.bfloat16):
    values = width * jax.random.normal(stream_key, extent, jnp.float32)
    if shards:
        values = values * block_levels(stream_key, extent, shards, -0.22, 0.18)
    return jnp.clip(values, -bound, bound).astype(held_as)


def setup_inputs(seed: int = 0) -> dict:
    key_of = jax.random.split(jax.random.key(seed), 14)
    return {
        "inputs": centred(key_of[0], (SEQS, LEN, D), 1.0, 6.0, ((0, 4), (1, 8)), jnp.float32),
        "norm_gain": jnp.clip(1.0 + 0.1 * jax.random.normal(key_of[1], (D,), jnp.float32), 0.5, 1.5),
        "input_projection_weight": centred(key_of[2], (D, 2 * DI), D ** -0.5, 0.21875, (), jnp.float32),
        "conv_weight": centred(key_of[3], (KC, DI), KC ** -0.5, 3.0, (), jnp.float32),
        "conv_bias": centred(key_of[4], (DI,), 0.5, 3.0, (), jnp.float32),
        "x_proj": centred(key_of[5], (DI, R + 2 * N), DI ** -0.5, 0.15625, (), jnp.float32),
        "step_proj": centred(key_of[6], (R, DI), R ** -0.5, 0.875, (), jnp.float32),
        "step_bias": jnp.clip(jax.random.uniform(key_of[7], (DI,), jnp.float32, -3.0, -1.0), -3.0, -1.0),
        "decay_code": touch_ends(jax.random.randint(key_of[8], (DI,), 0, 10), jax.random.fold_in(key_of[8], 1), 0, 9).astype(jnp.int32),
        "decay_log": jnp.clip(jax.random.uniform(key_of[9], (DI, N), jnp.float32, -5.0, -1.5), -5.0, -1.5),
        "skip_gain": jnp.clip(jax.random.uniform(key_of[10], (DI,), jnp.float32, 0.5, 1.5), 0.5, 1.5),
        "output_projection_weight": centred(key_of[11], (DI, D), DI ** -0.5, 0.15625, (), jnp.float32),
        "cotangent": centred(key_of[12], (SEQS, LEN, D), 1.0, 6.0, ((0, 4), (1, 8)), jnp.float32),
    }


MATMUL_ACCURACY = lax.Precision.HIGHEST
EPSILON = 1e-05

@jax.custom_vjp
def low(v):
    return lax.optimization_barrier(v.astype(jnp.bfloat16)).astype(jnp.float32)

@jax.custom_vjp
def low_back(v):
    return v

def low_keep(v):
    return (low(v), None)

def low_pass(kept, grad):
    return (grad,)

def back_keep(v):
    return (v, None)

def back_low(kept, grad):
    return (low(grad),)
low.defvjp(low_keep, low_pass)
low_back.defvjp(back_keep, back_low)

def selective(step, mixed, in_b, in_c, negative_decay_rate):
    count = step.shape[0]

    def token(state, row):
        step_t, mixed_t, b_t, c_t = row
        state = jnp.exp(step_t[:, :, None] * negative_decay_rate[None]) * state + (step_t * mixed_t)[:, :, None] * b_t[:, None, :]
        return (state, lax.optimization_barrier(jnp.sum(state * c_t[:, None, :], axis=-1)))

    def block_run(state, rows):
        return lax.scan(token, state, rows)
    rows = tuple((jnp.swapaxes(a, 0, 1).reshape(LEN // QB, QB, count, a.shape[-1]) for a in (step, mixed, in_b, in_c)))
    start = jnp.zeros((count, DI, N), jnp.float32)
    _, outputs = lax.scan(jax.checkpoint(block_run), start, rows)
    return jnp.swapaxes(outputs.reshape(LEN, count, DI), 0, 1)

def forward(offset, inputs, norm_gain, input_projection_weight, conv_weight, conv_bias, x_proj, step_proj, step_bias, decay_log, skip_gain, output_projection_weight):
    rms = lax.rsqrt(lax.optimization_barrier(jnp.mean(inputs * inputs, axis=-1, keepdims=True)) + EPSILON)
    normalized_input = inputs * rms * norm_gain
    mixer_and_gate = jnp.einsum('caw,wz->caz', normalized_input, input_projection_weight, precision=MATMUL_ACCURACY)
    hidden_x = mixer_and_gate[..., :DI]
    gate_z = mixer_and_gate[..., DI:]
    padded = jnp.pad(hidden_x, ((0, 0), (KC - 1, 0), (0, 0)))
    conv = conv_bias + jnp.zeros_like(hidden_x)
    for k in range(KC):
        conv = conv + conv_weight[k] * padded[:, k:k + LEN]
    mixed = jax.nn.silu(conv)
    proj = jnp.einsum('slc,ce->sle', mixed, x_proj, precision=MATMUL_ACCURACY)
    low_rank = proj[..., :R]
    in_b = proj[..., R:R + N]
    in_c = proj[..., R + N:]
    pre = jnp.einsum('slr,rc->slc', low_rank, step_proj, precision=MATMUL_ACCURACY) + step_bias - offset
    step = jax.nn.softplus(pre)
    negative_decay_rate = -jnp.exp(decay_log)
    result = selective(step, mixed, in_b, in_c, negative_decay_rate) + skip_gain * mixed
    gate_applied_output = result * jax.nn.silu(gate_z)
    return inputs + jnp.einsum('qiz,zk->qik', gate_applied_output, output_projection_weight, precision=MATMUL_ACCURACY)

def reference(inputs, norm_gain, input_projection_weight, conv_weight, conv_bias, x_proj, step_proj, step_bias, decay_code, decay_log, skip_gain, output_projection_weight, cotangent):
    offset = 0.5 * decay_code.astype(jnp.float32)

    def run(*values):
        return forward(offset, *values)
    block_out, pullback = jax.vjp(run, inputs, norm_gain, input_projection_weight, conv_weight, conv_bias, x_proj, step_proj, step_bias, decay_log, skip_gain, output_projection_weight)
    grads = pullback(cotangent)
    return (block_out, grads[0], grads[1], grads[2], grads[3], grads[4], grads[5], grads[6], grads[7], grads[8], grads[9], grads[10])
```

```python
import functools

import jax
import jax.numpy as jnp
from jax import lax
from jax.experimental import pallas as pl
from jax.experimental.pallas import tpu as pltpu
from jax.sharding import PartitionSpec as P

f32 = jnp.float32
MESH = pl.DeviceIdType.MESH
EPSILON = 1e-05
LOG2E=1.4426950408889634
LN2=0.6931471805599453

def wide(tile, reps):
    return jnp.concatenate([tile]*reps, axis=1) if reps>1 else tile
def rows(block, j, n):
    return jnp.broadcast_to(block[j:j+1], (n, block.shape[1]))

def pass_ac(step_ref, u_ref, d_ref, bb_ref, cc_ref, a2_ref, end_ref, lam_ref, dec_ref, lanes, LB):
    n=a2_ref.shape[0]; reps=LB//128
    a2=a2_ref[:, lanes]
    def chunk(i, carry):
        h,dec,acc=carry
        r=pl.multiple_of(i*8,8)
        s8=step_ref[pl.ds(r,8), lanes]; u8=u_ref[pl.ds(r,8), lanes]; d8=d_ref[pl.ds(r,8), lanes]
        for j in range(8):
            b=wide(bb_ref[r+j],reps); c=wide(cc_ref[r+j],reps)
            a=jnp.exp2(rows(s8,j,n)*a2)
            h=a*h+rows(u8,j,n)*b
            dec=dec*a
            acc=acc+dec*(rows(d8,j,n)*c)
        return h,dec,acc
    z=jnp.zeros((n,LB),f32)
    h,dec,acc=lax.fori_loop(0, step_ref.shape[0]//8, chunk, (z, z+1.0, z))
    end_ref[:, lanes]=h; lam_ref[:, lanes]=acc; dec_ref[:, lanes]=dec

def pass_b(step_ref,u_ref,bb_ref,cc_ref,d_ref,a2_ref,start_ref,y_ref,h_ref,cg_ref,lanes,LB,first):
    n=a2_ref.shape[0]; reps=LB//128
    a2=a2_ref[:, lanes]
    def chunk(i, h):
        r=pl.multiple_of(i*8,8)
        s8=step_ref[pl.ds(r,8), lanes]; u8=u_ref[pl.ds(r,8), lanes]; d8=d_ref[pl.ds(r,8), lanes]
        ys=[]
        for j in range(8):
            b=wide(bb_ref[r+j],reps); c=wide(cc_ref[r+j],reps)
            h_ref[r+j]=h
            a=jnp.exp2(rows(s8,j,n)*a2)
            h=a*h+rows(u8,j,n)*b
            ys.append(jnp.sum(c*h,axis=0,keepdims=True))
            w=rows(d8,j,n)*h
            p=sum(w[:,k*128:(k+1)*128] for k in range(reps))
            cg_ref[r+j]=p if first else cg_ref[r+j]+p
        y_ref[pl.ds(r,8), lanes]=jnp.concatenate(ys,axis=0)
        return h
    lax.fori_loop(0, step_ref.shape[0]//8, chunk, start_ref[:, lanes])

def pass_d(step_ref,u_ref,m_ref,bb_ref,cc_ref,d_ref,a2_ref,after_ref,h_ref,sg_ref,ms_ref,bg_ref,rate_ref,lanes,LB,first):
    n=a2_ref.shape[0]; reps=LB//128; T=step_ref.shape[0]
    a2=a2_ref[:, lanes]
    def chunk(i, carry):
        q,rate=carry
        r=pl.multiple_of(T-8-i*8,8)
        s8=step_ref[pl.ds(r,8), lanes]; u8=u_ref[pl.ds(r,8), lanes]; d8=d_ref[pl.ds(r,8), lanes]
        sg=[None]*8; lb=[None]*8
        for j in reversed(range(8)):
            b=wide(bb_ref[r+j],reps); c=wide(cc_ref[r+j],reps)
            st=rows(s8,j,n)
            a=jnp.exp2(st*a2)
            lam=rows(d8,j,n)*c+q
            q=a*lam
            dec=q*h_ref[r+j]
            lb[j]=jnp.sum(lam*b,axis=0,keepdims=True)
            sg[j]=jnp.sum(dec*a2,axis=0,keepdims=True)
            rate=rate+dec*st
            w=lam*rows(u8,j,n)
            p=sum(w[:,k*128:(k+1)*128] for k in range(reps))
            bg_ref[r+j]=p if first else bg_ref[r+j]+p
        lb8=jnp.concatenate(lb,axis=0); sg8=jnp.concatenate(sg,axis=0)
        sg_ref[pl.ds(r,8), lanes]=LN2*sg8+m_ref[pl.ds(r,8), lanes]*lb8
        ms_ref[pl.ds(r,8), lanes]=s8*lb8
        return q,rate
    q,rate=lax.fori_loop(0, T//8, chunk, (after_ref[:, lanes], jnp.zeros((n,LB),f32)))
    rate_ref[:, lanes]=rate

def bits_of(size): return size.bit_length()-1

def stage_plan(sizes, kind):
    s=[("seq",k) for k in range(bits_of(sizes["seq"]))]
    b=[("batch",k) for k in range(bits_of(sizes["batch"]))]
    core,y=b[0],b[1]; x=s[0]; z=s[1:]
    if kind=="xy": order=[(core,core),(x,y),(y,x)]+[(q,q) for q in z]
    else: order=[(core,core),(z[0],z[0]),(x,y),(y,x)]+[(q,q) for q in z[1:]]
    return order+[(q,q) for q in b[2:]]

class Place:
    def __init__(self):
        self.at={"seq":lax.axis_index("seq"),"batch":lax.axis_index("batch")}
        self.odd=self.at["batch"]%2
    def bit(self, d): return (self.at[d[0]]//(1<<d[1]))%2
    def stage(self, pair):
        to=dict(self.at); first,second=pair
        if first==second:
            v=self.bit(first); to[first[0]]=to[first[0]]+(1-2*v)*(1<<first[1])
        else:
            va,vb=self.bit(first),self.bit(second)
            to[first[0]]=to[first[0]]+(1-self.odd)*(1-2*va)*(1<<first[1])
            to[second[0]]=to[second[0]]+self.odd*(1-2*vb)*(1<<second[1])
            v=(1-self.odd)*va+self.odd*vb
        return (to["seq"],to["batch"]),v

def halvings(rows, stages):
    out=[]
    for _ in range(stages):
        ok=rows%16==0; out.append(ok); rows=rows//2 if ok else rows
    return out

class Chunk:
    def __init__(self, place, plan, acc, out, cols, recv, ss, rs):
        self.acc,self.out,self.cols,self.recv,self.ss,self.rs=acc,out,cols,recv,ss,rs
        rows=acc.shape[0]
        self.half=halvings(rows,len(plan)); self.K=len(plan)
        self.info=[place.stage(p) for p in plan]
        off=0; self.regs=[]; base=0
        for k in range(self.K):
            v=self.info[k][1]
            if self.half[k]:
                rows//=2
                keep=off+v*rows; send=off+(1-v)*rows
                self.regs.append((keep,send,rows,base)); off=keep
            else: self.regs.append((off,off,rows,base))
            base+=rows
        self.final=(off,rows)
        self.steps=[("r",k) for k in range(self.K)]+[("g",k) for k in reversed(range(self.K)) if self.half[k]]
        self.open=None; self.sends=[]; self.at=0
    def region(self, ref, off, rows): return ref.at[pl.ds(pl.multiple_of(off,8),rows), self.cols]
    def advance(self):
        if self.open is not None: self.finish()
        if self.at==self.K:
            off,rows=self.final
            self.move(rows, lambda r: self.put(self.out, off+r, self.acc[pl.ds(pl.multiple_of(off+r,8),8), self.cols]))
        if self.at<len(self.steps):
            kind,k=self.steps[self.at]
            keep,send,rows,base=self.regs[k]
            if kind=="r":
                src=self.region(self.acc,send,rows); dst=self.recv.at[pl.ds(base,rows)]
            else:
                src=dst=self.region(self.out,keep,rows)
            i=self.at
            cp=pltpu.make_async_remote_copy(src_ref=src,dst_ref=dst,send_sem=self.ss.at[i],recv_sem=self.rs.at[i],device_id=self.info[k][0],device_id_type=MESH)
            cp.start(); self.open=(cp,kind,k)
        self.at+=1
    def put(self, ref, off, v): ref[pl.ds(pl.multiple_of(off,8),8), self.cols]=v
    def move(self, rows, f):
        def body(i,_):
            f(i*8); return 0
        lax.fori_loop(0, rows//8, body, 0)
    def finish(self):
        cp,kind,k=self.open; self.open=None
        keep,send,rows,base=self.regs[k]
        cp.wait_recv()
        if kind=="r" and not self.half[k]: cp.wait_send()
        else: self.sends.append(cp)
        if kind=="r":
            def add(r):
                o=keep+r
                self.put(self.acc,o,self.acc[pl.ds(pl.multiple_of(o,8),8),self.cols]+self.recv[pl.ds(base+r,8)])
            self.move(rows, add)
    def done(self): return self.at>len(self.steps)
    def drain(self):
        for cp in self.sends: cp.wait_send()

def greet(place, plans):
    pairs=sorted({q for p in plans for q in p})
    bar=pltpu.get_barrier_semaphore()
    seen=sorted({d for p in pairs for d in p})
    for d in seen:
        to,_=place.stage((d,d))
        pl.semaphore_signal(bar,inc=1,device_id=to,device_id_type=MESH)
    pl.semaphore_wait(bar,len(seen))

def recv_rows(rows, stages):
    tot=0
    for ok in halvings(rows,stages):
        rows=rows//2 if ok else rows
        tot+=rows
    return tot

def ar_kernel(chunks, plans, n, order, *refs):
    ins,outs,refs=refs[:n],refs[n:2*n],refs[2*n:]
    recvs,ss,rs=refs[:len(chunks)],refs[-2],refs[-1]
    place=Place()
    greet(place, plans.values())
    cs=[Chunk(place,plans[kind],ins[o],outs[o],slice(c0,c0+w),recvs[i],ss.at[i],rs.at[i]) for i,(o,c0,w,kind) in enumerate(chunks)]
    t=0
    while not all(c.done() for c in cs):
        for i,c in enumerate(cs):
            if t>=i and not c.done(): c.advance()
        t+=1
    for c in cs: c.drain()

def all_reduce(sizes, arrays, chunks):
    plans={k:stage_plan(sizes,k) for k in {c[3] for c in chunks}}
    K=len(next(iter(plans.values())))
    V=pl.BlockSpec(memory_space=pltpu.VMEM)
    scratch=[pltpu.VMEM((recv_rows(arrays[o].shape[0],K),w),f32) for o,c0,w,kind in chunks]
    scratch+=[pltpu.SemaphoreType.DMA((len(chunks),2*K))]*2
    return pl.pallas_call(functools.partial(ar_kernel,chunks,plans,len(arrays),None),
        in_specs=[V]*len(arrays),out_specs=[V]*len(arrays),out_shape=[jax.ShapeDtypeStruct(a.shape,f32) for a in arrays],
        scratch_shapes=scratch,compiler_params=pltpu.CompilerParams(collective_id=1,has_side_effects=True,vmem_limit_bytes=62<<20))(*arrays)

VMEM = pl.BlockSpec(memory_space=pltpu.VMEM)


def local_call(kernel, outs, args, scratch=()):
    return pl.pallas_call(
        kernel,
        in_specs=[VMEM] * len(args),
        out_specs=[VMEM] * len(outs),
        out_shape=[jax.ShapeDtypeStruct(o, f32) for o in outs],
        scratch_shapes=list(scratch),
        compiler_params=pltpu.CompilerParams(vmem_limit_bytes=56 << 20),
    )(*args)


def lane_blocks(inner, width):
    return [slice(k, k + width) for k in range(0, inner, width)]


def ends_kernel(width, step, u, d, bb, cc, a2, end, lam, dec):
    for lanes in lane_blocks(a2.shape[1], width):
        pass_ac(step, u, d, bb, cc, a2, end, lam, dec, lanes, width)


def scans_kernel(width, step, u, m, d, bb, cc, a2, start, after, y, cg, sg, ms, bg, rate, h):
    for k, lanes in enumerate(lane_blocks(a2.shape[1], width)):
        pass_b(step, u, bb, cc, d, a2, start, y, h, cg, lanes, width, k == 0)
        pass_d(step, u, m, bb, cc, d, a2, after, h, sg, ms, bg, rate, lanes, width, k == 0)


def exchange_kernel(count, x_ref, o_ref, got, back, s1, r1, s2, r2):
    s, b = lax.axis_index("seq"), lax.axis_index("batch")
    across = count // 2
    width = x_ref.shape[2] // across
    bar = pltpu.get_barrier_semaphore()
    peers = [lax.rem(s + i, count) for i in range(1, count)]
    for p in peers:
        pl.semaphore_signal(bar, inc=1, device_id=(p, b), device_id_type=MESH)
    pl.semaphore_wait(bar, count - 1)

    def part(ref, p):
        return ref.at[:, pl.ds(pl.multiple_of(p // across * 8, 8), 8), pl.ds(pl.multiple_of(p % across * width, 128), width)]

    def copies(src, dst, ss, rs):
        out = []
        for i, p in enumerate(peers):
            out.append(pltpu.make_async_remote_copy(
                src_ref=src(p), dst_ref=dst, send_sem=ss.at[i], recv_sem=rs.at[i],
                device_id=(p, b), device_id_type=MESH))
            out[-1].start()
        return out

    first = copies(lambda p: part(x_ref, p), got.at[s], s1, r1)
    got[s] = part(x_ref, s)[...]
    for c in first:
        c.wait_recv()
    zero = jnp.zeros((8, width), f32)
    value = zero
    for q in range(count):
        back[q, 0] = value
        value = got[q, 0] + got[q, 2] * value
    value = zero
    for q in reversed(range(count)):
        back[q, 1] = value
        value = got[q, 1] + got[q, 2] * value
    second = copies(lambda p: back.at[p], part(o_ref, s), s2, r2)
    part(o_ref, s)[...] = back[s]
    for c in second:
        c.wait_recv()
    for c in first + second:
        c.wait_send()


def exchange(count, end, lam, dec):
    n, inner = end.shape
    if count % 2 or n != 16 or inner % (count // 2 * 128):
        return exchange_gathered(end, lam, dec)
    width = inner // (count // 2)
    sems = [pltpu.SemaphoreType.DMA((count - 1,))] * 4
    out = pl.pallas_call(
        functools.partial(exchange_kernel, count),
        in_specs=[VMEM], out_specs=VMEM,
        out_shape=jax.ShapeDtypeStruct((2, n, inner), f32),
        scratch_shapes=[pltpu.VMEM((count, 3, 8, width), f32), pltpu.VMEM((count, 2, 8, width), f32)] + sems,
        compiler_params=pltpu.CompilerParams(collective_id=2, has_side_effects=True),
    )(jnp.stack([end, lam, dec]))
    return out[0], out[1]


def exchange_gathered(end, lam, dec):
    ends, lams, decs = lax.all_gather((end, lam, dec), "seq")
    count, mine = lax.axis_size("seq"), lax.axis_index("seq")

    def ahead(q, value):
        return jnp.where(q < mine, ends[q] + decs[q] * value, value)

    def behind(i, value):
        q = count - 1 - i
        return jnp.where(q > mine, lams[q] + decs[q] * value, value)

    zero = jnp.zeros_like(end)
    return lax.fori_loop(0, count, ahead, zero), lax.fori_loop(0, count, behind, zero)


def shifted(x, axis, by):
    length = lax.axis_size(axis)
    return lax.ppermute(x, axis, [(i, i + by) for i in range(length) if 0 <= i + by < length])


def matmul(left, right, dims=((1,), (0,))):
    return lax.dot_general(left, right, (dims, ((), ())), precision=lax.Precision.HIGH, preferred_element_type=f32)


def silu_grad(value):
    sigma = jax.nn.sigmoid(value)
    return sigma * (1.0 + value * (1.0 - sigma))


def shards(sizes, inputs, norm_gain, w_in, conv_weight, conv_bias, x_proj, step_proj, step_bias, decay_code, decay_log,
           skip_gain, w_out, cotangent):
    seqs, group, width = inputs.shape
    assert seqs == 1
    inner = w_in.shape[1] // 2
    rank, states, taps = step_proj.shape[0], decay_log.shape[1], conv_weight.shape[0]
    x, g = inputs[0], cotangent[0]
    rms = lax.rsqrt(jnp.mean(x * x, axis=1, keepdims=True) + EPSILON)
    normed = x * rms * norm_gain
    both = matmul(normed, w_in)
    hidden, gate = both[:, :inner], both[:, inner:]
    padded = jnp.concatenate([shifted(hidden[group - taps + 1:], "seq", 1), hidden], axis=0)
    conv = conv_bias + sum(conv_weight[k] * padded[k:k + group] for k in range(taps))
    mixed = jax.nn.silu(conv)
    proj = matmul(mixed, x_proj)
    low_rank = proj[:, :rank]
    pre = matmul(low_rank, step_proj) + step_bias - 0.5 * decay_code.astype(f32)
    step = jax.nn.softplus(pre)
    rate = -jnp.exp(decay_log).T
    a2 = rate * LOG2E
    d_gated = matmul(g, w_out, ((1,), (1,)))
    gate_act = jax.nn.silu(gate)
    d_result = d_gated * gate_act
    spread = [jnp.broadcast_to(proj[:, k:k + states, None], (group, states, 128)) for k in (rank, rank + states)]
    u = step * mixed
    end, lam, dec = local_call(functools.partial(ends_kernel, 512), [(states, inner)] * 3, (step, u, d_result, *spread, a2))
    start, after = exchange(sizes["seq"], end, lam, dec)
    token, part, state = (group, inner), (group, states, 128), (states, inner)
    y, cg, step_grad, mixed_scan, bg, rate_sum = local_call(
        functools.partial(scans_kernel, 512), [token, part, token, token, part, state],
        (step, u, mixed, d_result, *spread, a2, start, after), [pltpu.VMEM((group, states, 512), f32)])
    result = y + skip_gain * mixed
    gated = result * gate_act
    block_out = x + matmul(gated, w_out)
    out_grad = matmul(gated, g, ((0,), (0,)))
    d_gate = d_gated * result * silu_grad(gate)
    skip_grad = jnp.sum(d_result * mixed, axis=0)
    pre_grad = step_grad * jax.nn.sigmoid(pre)
    bias_grad = jnp.sum(pre_grad, axis=0)
    step_proj_grad = matmul(low_rank, pre_grad, ((0,), (0,)))
    proj_grad = jnp.concatenate([matmul(pre_grad, step_proj, ((1,), (1,))), jnp.sum(bg, axis=2), jnp.sum(cg, axis=2)], axis=1)
    x_proj_grad_t = matmul(proj_grad, mixed, ((0,), (0,)))
    mixed_grad = mixed_scan + d_result * skip_gain + matmul(proj_grad, x_proj, ((1,), (1,)))
    conv_grad = mixed_grad * silu_grad(conv)
    tap_grads = [jnp.sum(conv_grad * padded[k:k + group], axis=0) for k in range(taps)]
    conv_bias_grad = jnp.sum(conv_grad, axis=0)
    behind = jnp.concatenate([conv_grad, shifted(conv_grad[:taps - 1], "seq", -1)], axis=0)
    x_grad = sum(conv_weight[k] * behind[taps - 1 - k:taps - 1 - k + group] for k in range(taps))
    both_grad = jnp.concatenate([x_grad, d_gate], axis=1)
    in_grad = matmul(normed, both_grad, ((0,), (0,)))
    normed_grad = matmul(both_grad, w_in, ((1,), (1,)))
    gain_grad = jnp.sum(normed_grad * x * rms, axis=0)
    weighted = normed_grad * norm_gain
    input_grad = rms * weighted - rms * rms * rms * x * jnp.mean(weighted * x, axis=1, keepdims=True) + g
    rows = jnp.stack(tap_grads + [conv_bias_grad, bias_grad, skip_grad, jnp.pad(gain_grad, (0, inner - width))])
    small = jnp.concatenate([x_proj_grad_t, step_proj_grad, rate_sum * rate, rows], axis=0)
    cells = small.size
    small = jnp.pad(small.reshape(-1), (0, 256 * 1024 - cells)).reshape(256, 1024)
    chunks = [(0, k, 768, "xy") for k in range(0, 2 * inner, 768)] + [(1, 0, width, "xy"), (2, 0, 1024, "xy")]
    in_sum, out_sum, small = all_reduce(sizes, [in_grad, out_grad, small], chunks)
    small = small.reshape(-1)[:cells].reshape(-1, inner)
    at = [0]

    def take(count):
        at[0] += count
        return small[at[0] - count:at[0]]

    x_proj_sum, step_proj_sum, decay_sum, taps_sum = take(x_proj.shape[1]).T, take(rank), take(states).T, take(taps)
    conv_bias_sum, bias_sum, skip_sum, gain_sum = (take(1)[0] for _ in range(4))
    return (block_out[None], input_grad[None], gain_sum[:width], in_sum, taps_sum, conv_bias_sum, x_proj_sum, step_proj_sum,
            bias_sum, decay_sum, skip_sum, out_sum)


def solution(mesh):
    tokens = P("batch", "seq", None)
    return jax.shard_map(
        functools.partial(shards, dict(mesh.shape)),
        mesh=mesh,
        in_specs=(tokens,) + (P(),) * 11 + (tokens,),
        out_specs=(tokens, tokens) + (P(),) * 10,
        check_vma=False,
    )
```

```python
import functools

import jax
import jax.numpy as jnp
from jax import lax
from jax.experimental import pallas as pl
from jax.experimental.pallas import tpu as pltpu
from jax.sharding import PartitionSpec as P

f32 = jnp.float32
MESH = pl.DeviceIdType.MESH
EPSILON = 1e-05
LOG2E=1.4426950408889634
LN2=0.6931471805599453

def wide(tile, reps):
    return jnp.concatenate([tile]*reps, axis=1) if reps>1 else tile
def rows(block, j, n):
    return jnp.broadcast_to(block[j:j+1], (n, block.shape[1]))

def pass_ac(step_ref, u_ref, d_ref, bb_ref, cc_ref, a2_ref, end_ref, lam_ref, dec_ref, lanes, LB):
    n=a2_ref.shape[0]; reps=LB//128
    a2=a2_ref[:, lanes]
    def chunk(i, carry):
        h,dec,acc=carry
        r=pl.multiple_of(i*8,8)
        s8=step_ref[pl.ds(r,8), lanes]; u8=u_ref[pl.ds(r,8), lanes]; d8=d_ref[pl.ds(r,8), lanes]
        for j in range(8):
            b=wide(bb_ref[r+j],reps); c=wide(cc_ref[r+j],reps)
            a=jnp.exp2(rows(s8,j,n)*a2)
            h=a*h+rows(u8,j,n)*b
            dec=dec*a
            acc=acc+dec*(rows(d8,j,n)*c)
        return h,dec,acc
    z=jnp.zeros((n,LB),f32)
    h,dec,acc=lax.fori_loop(0, step_ref.shape[0]//8, chunk, (z, z+1.0, z))
    end_ref[:, lanes]=h; lam_ref[:, lanes]=acc; dec_ref[:, lanes]=dec

def pass_b(step_ref,u_ref,bb_ref,cc_ref,d_ref,a2_ref,start_ref,y_ref,h_ref,cg_ref,lanes,LB,first):
    n=a2_ref.shape[0]; reps=LB//128
    a2=a2_ref[:, lanes]
    def chunk(i, h):
        r=pl.multiple_of(i*8,8)
        s8=step_ref[pl.ds(r,8), lanes]; u8=u_ref[pl.ds(r,8), lanes]; d8=d_ref[pl.ds(r,8), lanes]
        ys=[]
        for j in range(8):
            b=wide(bb_ref[r+j],reps); c=wide(cc_ref[r+j],reps)
            h_ref[r+j]=h
            a=jnp.exp2(rows(s8,j,n)*a2)
            h=a*h+rows(u8,j,n)*b
            ys.append(jnp.sum(c*h,axis=0,keepdims=True))
            w=rows(d8,j,n)*h
            p=sum(w[:,k*128:(k+1)*128] for k in range(reps))
            cg_ref[r+j]=p if first else cg_ref[r+j]+p
        y_ref[pl.ds(r,8), lanes]=jnp.concatenate(ys,axis=0)
        return h
    lax.fori_loop(0, step_ref.shape[0]//8, chunk, start_ref[:, lanes])

def pass_d(step_ref,u_ref,m_ref,bb_ref,cc_ref,d_ref,a2_ref,after_ref,h_ref,sg_ref,ms_ref,bg_ref,rate_ref,lanes,LB,first):
    n=a2_ref.shape[0]; reps=LB//128; T=step_ref.shape[0]
    a2=a2_ref[:, lanes]
    def chunk(i, carry):
        q,rate=carry
        r=pl.multiple_of(T-8-i*8,8)
        s8=step_ref[pl.ds(r,8), lanes]; u8=u_ref[pl.ds(r,8), lanes]; d8=d_ref[pl.ds(r,8), lanes]
        sg=[None]*8; lb=[None]*8
        for j in reversed(range(8)):
            b=wide(bb_ref[r+j],reps); c=wide(cc_ref[r+j],reps)
            st=rows(s8,j,n)
            a=jnp.exp2(st*a2)
            lam=rows(d8,j,n)*c+q
            q=a*lam
            dec=q*h_ref[r+j]
            lb[j]=jnp.sum(lam*b,axis=0,keepdims=True)
            sg[j]=jnp.sum(dec*a2,axis=0,keepdims=True)
            rate=rate+dec*st
            w=lam*rows(u8,j,n)
            p=sum(w[:,k*128:(k+1)*128] for k in range(reps))
            bg_ref[r+j]=p if first else bg_ref[r+j]+p
        lb8=jnp.concatenate(lb,axis=0); sg8=jnp.concatenate(sg,axis=0)
        sg_ref[pl.ds(r,8), lanes]=LN2*sg8+m_ref[pl.ds(r,8), lanes]*lb8
        ms_ref[pl.ds(r,8), lanes]=s8*lb8
        return q,rate
    q,rate=lax.fori_loop(0, T//8, chunk, (after_ref[:, lanes], jnp.zeros((n,LB),f32)))
    rate_ref[:, lanes]=rate

def bits_of(size): return size.bit_length()-1

def stage_plan(sizes, kind):
    s=[("seq",k) for k in range(bits_of(sizes["seq"]))]
    b=[("batch",k) for k in range(bits_of(sizes["batch"]))]
    core,y=b[0],b[1]; x=s[0]; z=s[1:]
    if kind=="xy": order=[(core,core),(x,y),(y,x)]+[(q,q) for q in z]
    else: order=[(core,core),(z[0],z[0]),(x,y),(y,x)]+[(q,q) for q in z[1:]]
    return order+[(q,q) for q in b[2:]]

class Place:
    def __init__(self):
        self.at={"seq":lax.axis_index("seq"),"batch":lax.axis_index("batch")}
        self.odd=self.at["batch"]%2
    def bit(self, d): return (self.at[d[0]]//(1<<d[1]))%2
    def stage(self, pair):
        to=dict(self.at); first,second=pair
        if first==second:
            v=self.bit(first); to[first[0]]=to[first[0]]+(1-2*v)*(1<<first[1])
        else:
            va,vb=self.bit(first),self.bit(second)
            to[first[0]]=to[first[0]]+(1-self.odd)*(1-2*va)*(1<<first[1])
            to[second[0]]=to[second[0]]+self.odd*(1-2*vb)*(1<<second[1])
            v=(1-self.odd)*va+self.odd*vb
        return (to["seq"],to["batch"]),v

def halvings(rows, stages):
    out=[]
    for _ in range(stages):
        ok=rows%16==0; out.append(ok); rows=rows//2 if ok else rows
    return out

class Chunk:
    def __init__(self, place, plan, acc, out, cols, recv, ss, rs):
        self.acc,self.out,self.cols,self.recv,self.ss,self.rs=acc,out,cols,recv,ss,rs
        rows=acc.shape[0]
        self.half=halvings(rows,len(plan)); self.K=len(plan)
        self.info=[place.stage(p) for p in plan]
        off=0; self.regs=[]; base=0
        for k in range(self.K):
            v=self.info[k][1]
            if self.half[k]:
                rows//=2
                keep=off+v*rows; send=off+(1-v)*rows
                self.regs.append((keep,send,rows,base)); off=keep
            else: self.regs.append((off,off,rows,base))
            base+=rows
        self.final=(off,rows)
        self.steps=[("r",k) for k in range(self.K)]+[("g",k) for k in reversed(range(self.K)) if self.half[k]]
        self.open=None; self.sends=[]; self.at=0
    def region(self, ref, off, rows): return ref.at[pl.ds(pl.multiple_of(off,8),rows), self.cols]
    def advance(self):
        if self.open is not None: self.finish()
        if self.at==self.K:
            off,rows=self.final
            self.move(rows, lambda r: self.put(self.out, off+r, self.acc[pl.ds(pl.multiple_of(off+r,8),8), self.cols]))
        if self.at<len(self.steps):
            kind,k=self.steps[self.at]
            keep,send,rows,base=self.regs[k]
            if kind=="r":
                src=self.region(self.acc,send,rows); dst=self.recv.at[pl.ds(base,rows)]
            else:
                src=dst=self.region(self.out,keep,rows)
            i=self.at
            cp=pltpu.make_async_remote_copy(src_ref=src,dst_ref=dst,send_sem=self.ss.at[i],recv_sem=self.rs.at[i],device_id=self.info[k][0],device_id_type=MESH)
            cp.start(); self.open=(cp,kind,k)
        self.at+=1
    def put(self, ref, off, v): ref[pl.ds(pl.multiple_of(off,8),8), self.cols]=v
    def move(self, rows, f):
        def body(i,_):
            f(i*8); return 0
        lax.fori_loop(0, rows//8, body, 0)
    def finish(self):
        cp,kind,k=self.open; self.open=None
        keep,send,rows,base=self.regs[k]
        cp.wait_recv()
        if kind=="r" and not self.half[k]: cp.wait_send()
        else: self.sends.append(cp)
        if kind=="r":
            def add(r):
                o=keep+r
                self.put(self.acc,o,self.acc[pl.ds(pl.multiple_of(o,8),8),self.cols]+self.recv[pl.ds(base+r,8)])
            self.move(rows, add)
    def done(self): return self.at>len(self.steps)
    def drain(self):
        for cp in self.sends: cp.wait_send()

def greet(place, plans):
    pairs=sorted({q for p in plans for q in p})
    bar=pltpu.get_barrier_semaphore()
    seen=sorted({d for p in pairs for d in p})
    for d in seen:
        to,_=place.stage((d,d))
        pl.semaphore_signal(bar,inc=1,device_id=to,device_id_type=MESH)
    pl.semaphore_wait(bar,len(seen))

def recv_rows(rows, stages):
    tot=0
    for ok in halvings(rows,stages):
        rows=rows//2 if ok else rows
        tot+=rows
    return tot

def ar_kernel(chunks, plans, n, order, *refs):
    ins,outs,refs=refs[:n],refs[n:2*n],refs[2*n:]
    recvs,ss,rs=refs[:len(chunks)],refs[-2],refs[-1]
    place=Place()
    greet(place, plans.values())
    cs=[Chunk(place,plans[kind],ins[o],outs[o],slice(c0,c0+w),recvs[i],ss.at[i],rs.at[i]) for i,(o,c0,w,kind) in enumerate(chunks)]
    t=0
    while not all(c.done() for c in cs):
        for i,c in enumerate(cs):
            if t>=i and not c.done(): c.advance()
        t+=1
    for c in cs: c.drain()

def all_reduce(sizes, arrays, chunks):
    plans={k:stage_plan(sizes,k) for k in {c[3] for c in chunks}}
    K=len(next(iter(plans.values())))
    V=pl.BlockSpec(memory_space=pltpu.VMEM)
    scratch=[pltpu.VMEM((recv_rows(arrays[o].shape[0],K),w),f32) for o,c0,w,kind in chunks]
    scratch+=[pltpu.SemaphoreType.DMA((len(chunks),2*K))]*2
    return pl.pallas_call(functools.partial(ar_kernel,chunks,plans,len(arrays),None),
        in_specs=[V]*len(arrays),out_specs=[V]*len(arrays),out_shape=[jax.ShapeDtypeStruct(a.shape,f32) for a in arrays],
        scratch_shapes=scratch,compiler_params=pltpu.CompilerParams(collective_id=1,has_side_effects=True,vmem_limit_bytes=62<<20))(*arrays)

VMEM = pl.BlockSpec(memory_space=pltpu.VMEM)


def local_call(kernel, outs, args, scratch=()):
    return pl.pallas_call(
        kernel,
        in_specs=[VMEM] * len(args),
        out_specs=[VMEM] * len(outs),
        out_shape=[jax.ShapeDtypeStruct(o, f32) for o in outs],
        scratch_shapes=list(scratch),
        compiler_params=pltpu.CompilerParams(vmem_limit_bytes=56 << 20),
    )(*args)


def lane_blocks(inner, width):
    return [slice(k, k + width) for k in range(0, inner, width)]


def scan_kernel(width, count, step, u, m, d, bb, cc, a2, y, cg, sg, ms, bg, rate, h, ends, edges, *carry):
    meet(carry_peers(count), lax.axis_index("batch"), pltpu.get_barrier_semaphore())
    blocks = lane_blocks(a2.shape[1], width)
    for lanes in blocks:
        pass_ac(step, u, d, bb, cc, a2, ends.at[0], ends.at[1], ends.at[2], lanes, width)
    carry_exchange(count, ends, edges, *carry)
    for k, lanes in enumerate(blocks):
        pass_b(step, u, bb, cc, d, a2, edges.at[0], y, h, cg, lanes, width, k == 0)
        pass_d(step, u, m, bb, cc, d, a2, edges.at[1], h, sg, ms, bg, rate, lanes, width, k == 0)


def meet(seqs, b, bar):
    for p in seqs:
        pl.semaphore_signal(bar, inc=1, device_id=(p, b), device_id_type=MESH)
    pl.semaphore_wait(bar, len(seqs))


def carry_peers(count):
    s = lax.axis_index("seq")
    if tiled(count):
        return [lax.rem(s + i, count) for i in range(1, count)]
    return [s + (1 - 2 * (s // k % 2)) * k for k in powers(count)]


def powers(count):
    return [1 << k for k in range(count.bit_length() - 1)]


def tiled(count):
    return count in (2, 4, 6, 8, 12, 24)


def carry_scratch(count, n, inner):
    if tiled(count):
        w = inner // (count // 2)
        return [pltpu.VMEM((count, 3, 8, w), f32), pltpu.VMEM((count, 2, 8, w), f32)] + [pltpu.SemaphoreType.DMA((count - 1,))] * 4
    k = len(powers(count))
    return [pltpu.VMEM((k, 3, n, inner), f32), pltpu.VMEM((2, n, inner), f32)] + [pltpu.SemaphoreType.DMA((k,))] * 4


def carry_exchange(count, ends, edges, got, back, s1, r1, s2, r2):
    if tiled(count):
        carry_tiles(count, ends, edges, got, back, s1, r1, s2, r2)
    else:
        carry_doubling(count, ends, edges, got, back, s1, r1)


def carry_doubling(count, ends, edges, got, decays, ss, rs):
    s, b = lax.axis_index("seq"), lax.axis_index("batch")
    edges[...] = jnp.zeros_like(edges)
    decays[...] = jnp.ones_like(decays)
    for k, p in enumerate(carry_peers(count)):
        copy = pltpu.make_async_remote_copy(
            src_ref=ends, dst_ref=got.at[k], send_sem=ss.at[k], recv_sem=rs.at[k], device_id=(p, b), device_id_type=MESH)
        copy.start()
        copy.wait()
        later = s // (1 << k) % 2

        @pl.when(later == 1)
        def _():
            edges[0] += decays[0] * got[k, 0]
            decays[0] *= got[k, 2]
            ends[0] += ends[2] * got[k, 0]
            ends[1] = got[k, 1] + got[k, 2] * ends[1]

        @pl.when(later == 0)
        def _():
            edges[1] += decays[1] * got[k, 1]
            decays[1] *= got[k, 2]
            ends[1] += ends[2] * got[k, 1]
            ends[0] = got[k, 0] + got[k, 2] * ends[0]

        ends[2] *= got[k, 2]


def carry_tiles(count, ends, edges, got, back, s1, r1, s2, r2):
    s, b = lax.axis_index("seq"), lax.axis_index("batch")
    across = count // 2
    width = ends.shape[2] // across
    peers = carry_peers(count)

    def part(ref, p):
        return ref.at[:, pl.ds(pl.multiple_of(p // across * 8, 8), 8), pl.ds(pl.multiple_of(p % across * width, 128), width)]

    def copies(src, dst, ss, rs):
        out = []
        for i, p in enumerate(peers):
            out.append(pltpu.make_async_remote_copy(
                src_ref=src(p), dst_ref=dst, send_sem=ss.at[i], recv_sem=rs.at[i],
                device_id=(p, b), device_id_type=MESH))
            out[-1].start()
        return out

    first = copies(lambda p: part(ends, p), got.at[s], s1, r1)
    got[s] = part(ends, s)[...]
    for c in first:
        c.wait_recv()
    value = jnp.zeros((8, width), f32)
    for q in range(count):
        back[q, 0] = value
        value = got[q, 0] + got[q, 2] * value
    value = jnp.zeros((8, width), f32)
    for q in reversed(range(count)):
        back[q, 1] = value
        value = got[q, 1] + got[q, 2] * value
    second = copies(lambda p: back.at[p], part(edges, s), s2, r2)
    part(edges, s)[...] = back[s]
    for c in second:
        c.wait_recv()
    for c in first + second:
        c.wait_send()


def scans(count, step, u, mixed, d_result, bb, cc, a2):
    group, inner = step.shape
    n = a2.shape[0]
    token, part, state = [jax.ShapeDtypeStruct(v, f32) for v in ((group, inner), (group, n, 128), (n, inner))]
    return pl.pallas_call(
        functools.partial(scan_kernel, 512, count),
        in_specs=[VMEM] * 7, out_specs=[VMEM] * 6,
        out_shape=[token, part, token, token, part, state],
        scratch_shapes=[pltpu.VMEM((group, n, 512), f32), pltpu.VMEM((3, n, inner), f32), pltpu.VMEM((2, n, inner), f32), *carry_scratch(count, n, inner)],
        compiler_params=pltpu.CompilerParams(collective_id=2, has_side_effects=True, vmem_limit_bytes=56 << 20),
    )(step, u, mixed, d_result, bb, cc, a2)


def shifted(x, axis, by):
    length = lax.axis_size(axis)
    return lax.ppermute(x, axis, [(i, i + by) for i in range(length) if 0 <= i + by < length])


def matmul(left, right, dims=((1,), (0,))):
    return lax.dot_general(left, right, (dims, ((), ())), precision=lax.Precision.HIGH, preferred_element_type=f32)


def silu_grad(value):
    sigma = jax.nn.sigmoid(value)
    return sigma * (1.0 + value * (1.0 - sigma))


def shards(sizes, inputs, norm_gain, w_in, conv_weight, conv_bias, x_proj, step_proj, step_bias, decay_code, decay_log,
           skip_gain, w_out, cotangent):
    seqs, group, width = inputs.shape
    assert seqs == 1
    inner = w_in.shape[1] // 2
    rank, states, taps = step_proj.shape[0], decay_log.shape[1], conv_weight.shape[0]
    x, g = inputs[0], cotangent[0]
    rms = lax.rsqrt(jnp.mean(x * x, axis=1, keepdims=True) + EPSILON)
    normed = x * rms * norm_gain
    both = matmul(normed, w_in)
    hidden, gate = both[:, :inner], both[:, inner:]
    padded = jnp.concatenate([shifted(hidden[group - taps + 1:], "seq", 1), hidden], axis=0)
    conv = conv_bias + sum(conv_weight[k] * padded[k:k + group] for k in range(taps))
    mixed = jax.nn.silu(conv)
    proj = matmul(mixed, x_proj)
    low_rank = proj[:, :rank]
    pre = matmul(low_rank, step_proj) + step_bias - 0.5 * decay_code.astype(f32)
    step = jax.nn.softplus(pre)
    rate = -jnp.exp(decay_log).T
    a2 = rate * LOG2E
    d_gated = matmul(g, w_out, ((1,), (1,)))
    gate_act = jax.nn.silu(gate)
    d_result = d_gated * gate_act
    spread = [jnp.broadcast_to(proj[:, k:k + states, None], (group, states, 128)) for k in (rank, rank + states)]
    u = step * mixed
    y, cg, step_grad, mixed_scan, bg, rate_sum = scans(sizes["seq"], step, u, mixed, d_result, *spread, a2)
    result = y + skip_gain * mixed
    gated = result * gate_act
    block_out = x + matmul(gated, w_out)
    out_grad = matmul(gated, g, ((0,), (0,)))
    d_gate = d_gated * result * silu_grad(gate)
    skip_grad = jnp.sum(d_result * mixed, axis=0)
    pre_grad = step_grad * jax.nn.sigmoid(pre)
    bias_grad = jnp.sum(pre_grad, axis=0)
    step_proj_grad = matmul(low_rank, pre_grad, ((0,), (0,)))
    proj_grad = jnp.concatenate([matmul(pre_grad, step_proj, ((1,), (1,))), jnp.sum(bg, axis=2), jnp.sum(cg, axis=2)], axis=1)
    x_proj_grad_t = matmul(proj_grad, mixed, ((0,), (0,)))
    mixed_grad = mixed_scan + d_result * skip_gain + matmul(proj_grad, x_proj, ((1,), (1,)))
    conv_grad = mixed_grad * silu_grad(conv)
    tap_grads = [jnp.sum(conv_grad * padded[k:k + group], axis=0) for k in range(taps)]
    conv_bias_grad = jnp.sum(conv_grad, axis=0)
    behind = jnp.concatenate([conv_grad, shifted(conv_grad[:taps - 1], "seq", -1)], axis=0)
    x_grad = sum(conv_weight[k] * behind[taps - 1 - k:taps - 1 - k + group] for k in range(taps))
    both_grad = jnp.concatenate([x_grad, d_gate], axis=1)
    in_grad = matmul(normed, both_grad, ((0,), (0,)))
    normed_grad = matmul(both_grad, w_in, ((1,), (1,)))
    gain_grad = jnp.sum(normed_grad * x * rms, axis=0)
    weighted = normed_grad * norm_gain
    input_grad = rms * weighted - rms * rms * rms * x * jnp.mean(weighted * x, axis=1, keepdims=True) + g
    rows = jnp.stack(tap_grads + [conv_bias_grad, bias_grad, skip_grad, jnp.pad(gain_grad, (0, inner - width))])
    small = jnp.concatenate([x_proj_grad_t, step_proj_grad, rate_sum * rate, rows], axis=0)
    cells = small.size
    small = jnp.pad(small.reshape(-1), (0, 256 * 1024 - cells)).reshape(256, 1024)
    chunks = [(0, k, 768, "xy") for k in range(0, 2 * inner, 768)] + [(1, 0, width, "xy"), (2, 0, 1024, "xy")]
    in_sum, out_sum, small = all_reduce(sizes, [in_grad, out_grad, small], chunks)
    small = small.reshape(-1)[:cells].reshape(-1, inner)
    at = [0]

    def take(count):
        at[0] += count
        return small[at[0] - count:at[0]]

    x_proj_sum, step_proj_sum, decay_sum, taps_sum = take(x_proj.shape[1]).T, take(rank), take(states).T, take(taps)
    conv_bias_sum, bias_sum, skip_sum, gain_sum = (take(1)[0] for _ in range(4))
    return (block_out[None], input_grad[None], gain_sum[:width], in_sum, taps_sum, conv_bias_sum, x_proj_sum, step_proj_sum,
            bias_sum, decay_sum, skip_sum, out_sum)


def solution(mesh):
    tokens = P("batch", "seq", None)
    return jax.shard_map(
        functools.partial(shards, dict(mesh.shape)),
        mesh=mesh,
        in_specs=(tokens,) + (P(),) * 11 + (tokens,),
        out_specs=(tokens, tokens) + (P(),) * 10,
        check_vma=False,
    )
```

```python
import functools

import jax
import jax.numpy as jnp
from jax import lax
from jax.experimental import pallas as pl
from jax.experimental.pallas import tpu as pltpu
from jax.sharding import PartitionSpec as P

f32 = jnp.float32
bf16 = jnp.bfloat16
MESH = pl.DeviceIdType.MESH
EPSILON = 1e-05
LOG2E = 1.4426950408889634
LN2 = 0.6931471805599453
LANES = 128
SCAN = 512
WBLOCK = 256
SLOTS = 4
SMALL = (256, 1024)


def mult(value, by):
    return value if isinstance(value, int) else pl.multiple_of(value, by)


def split(value):
    high = value.astype(bf16)
    return high, (value - high.astype(f32)).astype(bf16)


def dot(a, b, dims):
    return lax.dot_general(a, b, (dims, ((), ())), preferred_element_type=f32)


def matmul(a, b, dims=((1,), (0,))):
    (ah, al), (bh, bl) = split(a), split(b)
    return dot(ah, bh, dims) + dot(al, bh, dims) + dot(ah, bl, dims)


def stacked(value):
    return jnp.concatenate(split(value), axis=0)


def rows_matmul(both, b, dims):
    rows = both.shape[0] // 2
    bh, bl = split(b)
    wide = dot(both, bh, dims)
    return wide[:rows] + wide[rows:] + dot(both[:rows], bl, dims)


def sigmoid(v):
    return 1.0 / (1.0 + jnp.exp(-v))


def loop(count, body):
    def step(i, _):
        body(i)
        return 0

    lax.fori_loop(0, count, step, 0)


class Place:
    def __init__(self, sizes):
        self.sizes = sizes
        self.s, self.b = lax.axis_index("seq"), lax.axis_index("batch")
        self.at = {"seq": self.s, "batch": self.b}
        self.x, self.c, self.y = self.s % 2, self.b % 2, self.b // 2
        self.odd = self.c
        self.q = self.x + 2 * self.y

    def near(self, dx, dy, dc):
        seq = self.s + dx * (1 - 2 * self.x)
        batch = self.b + dc * (1 - 2 * self.c) + 2 * dy * (1 - 2 * self.y)
        return (seq, batch), self.q + dx * (1 - 2 * self.x) + 2 * dy * (1 - 2 * self.y)

    def bit(self, d):
        return self.at[d[0]] // (1 << d[1]) % 2

    def stage(self, pair):
        to = dict(self.at)
        first, second = pair
        if first == second:
            v = self.bit(first)
            to[first[0]] = to[first[0]] + (1 - 2 * v) * (1 << first[1])
        else:
            va, vb = self.bit(first), self.bit(second)
            to[first[0]] = to[first[0]] + (1 - self.odd) * (1 - 2 * va) * (1 << first[1])
            to[second[0]] = to[second[0]] + self.odd * (1 - 2 * vb) * (1 << second[1])
            v = (1 - self.odd) * va + self.odd * vb
        return (to["seq"], to["batch"]), v


class Links:
    def __init__(self, send, recv):
        self.send, self.recv, self.used, self.open = send, recv, 0, []

    def copy(self, src, dst, to, start=True):
        i = self.used
        self.used += 1
        c = pltpu.make_async_remote_copy(
            src_ref=src, dst_ref=dst, send_sem=self.send.at[i], recv_sem=self.recv.at[i], device_id=to, device_id_type=MESH
        )
        if start:
            c.start()
            self.open.append(c)
        return c

    def sent(self, copy):
        copy.wait_send()
        self.open = [c for c in self.open if c is not copy]

    def drain(self):
        for c in self.open:
            c.wait_send()
        self.open = []


GROUP = [(dx, dy, dc) for dx in (0, 1) for dy in (0, 1) for dc in (0, 1) if dx + dy + dc]


def log2(size):
    return size.bit_length() - 1


def all_bits(sizes):
    s = [("seq", k) for k in range(log2(sizes["seq"]))]
    b = [("batch", k) for k in range(log2(sizes["batch"]))]
    return s, b


def small_plan(sizes):
    s, b = all_bits(sizes)
    return [(b[0], b[0]), (s[0], b[1]), (b[1], s[0])] + [(q, q) for q in s[1:] + b[2:]]


def halvings(rows, stages):
    out = []
    for _ in range(stages):
        ok = rows % 16 == 0
        out.append(ok)
        rows = rows // 2 if ok else rows
    return out


def landing_rows(rows, stages):
    total = 0
    for ok in halvings(rows, stages):
        rows = rows // 2 if ok else rows
        total += rows
    return total


def reduce_rows(place, links, plan, acc, land, whole):
    rows = acc.shape[0]
    half = halvings(rows, len(plan))
    off, base, kept = 0, 0, []
    for pair, ok in zip(plan, half):
        to, v = place.stage(pair)
        if ok:
            rows //= 2
            keep, give = off + v * rows, off + (1 - v) * rows
        else:
            keep = give = off
        copy = links.copy(acc.at[pl.ds(mult(give, 8), rows)], land.at[pl.ds(base, rows)], to)
        yield
        copy.wait_recv()
        if not ok:
            links.sent(copy)

        def add(i, keep=keep, base=base):
            at = pl.ds(mult(keep + i * 8, 8), 8)
            acc[at] = acc[at] + land[pl.ds(mult(base + i * 8, 8), 8)]

        loop(rows // 8, add)
        base += rows
        if ok:
            kept.append((to, keep, rows))
        off = keep

    def place_row(i):
        whole(off + i * 8, 8)[...] = acc[pl.ds(mult(off + i * 8, 8), 8)]

    loop(rows // 8, place_row)
    for to, keep, rows in reversed(kept):
        part = whole(keep, rows)
        copy = links.copy(part, part, to)
        yield
        copy.wait_recv()


def tiled(count):
    return count in (2, 4, 6, 8, 12, 24)


def carry_peers(count, s):
    if tiled(count):
        return [lax.rem(s + i, count) for i in range(1, count)]
    return [s + (1 - 2 * (s // (1 << k) % 2)) * (1 << k) for k in range(log2(count))]


def carry_scratch(count, n, inner):
    if tiled(count):
        w = inner // (count // 2)
        return [pltpu.VMEM((count, 3, 8, w), f32), pltpu.VMEM((count, 2, 8, w), f32)]
    return [pltpu.VMEM((log2(count), 3, n, inner), f32), pltpu.VMEM((2, n, inner), f32)]


def carry_doubling(place, links, ends, edges, got, decays):
    edges[...] = jnp.zeros_like(edges)
    decays[...] = jnp.ones_like(decays)
    for k, p in enumerate(carry_peers(place.sizes["seq"], place.s)):
        copy = links.copy(ends, got.at[k], (p, place.b))
        copy.wait_recv()
        links.sent(copy)
        later = place.bit(("seq", k))

        @pl.when(later == 1)
        def _():
            edges[0] += decays[0] * got[k, 0]
            decays[0] *= got[k, 2]
            ends[0] += ends[2] * got[k, 0]
            ends[1] = got[k, 1] + got[k, 2] * ends[1]

        @pl.when(later == 0)
        def _():
            edges[1] += decays[1] * got[k, 1]
            decays[1] *= got[k, 2]
            ends[1] += ends[2] * got[k, 1]
            ends[0] = got[k, 0] + got[k, 2] * ends[0]

        ends[2] *= got[k, 2]


def carry_tiles(place, links, ends, edges, got, back):
    count, s, b = place.sizes["seq"], place.s, place.b
    across = count // 2
    width = ends.shape[2] // across
    peers = carry_peers(count, s)

    def part(ref, p):
        return ref.at[:, pl.ds(mult(p // across * 8, 8), 8), pl.ds(mult(p % across * width, LANES), width)]

    first = [links.copy(part(ends, p), got.at[s], (p, b)) for p in peers]
    got[s] = part(ends, s)[...]
    for c in first:
        c.wait_recv()
    value = jnp.zeros((8, width), f32)
    for p in range(count):
        back[p, 0] = value
        value = got[p, 0] + got[p, 2] * value
    value = jnp.zeros((8, width), f32)
    for p in reversed(range(count)):
        back[p, 1] = value
        value = got[p, 1] + got[p, 2] * value
    second = [links.copy(back.at[p], part(edges, s), (p, b)) for p in peers]
    part(edges, s)[...] = back[s]
    for c in second:
        c.wait_recv()


def carry(place, links, *refs):
    (carry_tiles if tiled(place.sizes["seq"]) else carry_doubling)(place, links, *refs)


def wide(tile):
    return jnp.concatenate([tile] * (SCAN // LANES), axis=1)


def spread(row, n):
    return jnp.broadcast_to(row, (n, row.shape[1]))


def fold(value):
    return sum(value[:, k : k + LANES] for k in range(0, value.shape[1], LANES))


def scan_ends(m, lanes):
    a2 = m.a2[:, lanes]
    n = a2.shape[0]

    def chunk(i, held):
        h, dec, acc = held
        at = pl.ds(pl.multiple_of(i * 8, 8), 8)
        s8, u8, d8 = m.step[at, lanes], m.u[at, lanes], m.d_res[at, lanes]
        for j in range(8):
            t = pl.ds(pl.multiple_of((i * 8 + j) * n, 8), n)
            b, c = wide(m.bb[t]), wide(m.cc[t])
            a = jnp.exp2(spread(s8[j : j + 1], n) * a2)
            h = a * h + spread(u8[j : j + 1], n) * b
            dec = dec * a
            acc = acc + dec * (spread(d8[j : j + 1], n) * c)
        return h, dec, acc

    zero = jnp.zeros_like(a2)
    h, dec, acc = lax.fori_loop(0, m.step.shape[0] // 8, chunk, (zero, zero + 1.0, zero))
    m.ends[0, :, lanes], m.ends[1, :, lanes], m.ends[2, :, lanes] = h, acc, dec


def scan_out(m, lanes):
    a2 = m.a2[:, lanes]
    n = a2.shape[0]

    def chunk(i, h):
        at = pl.ds(pl.multiple_of(i * 8, 8), 8)
        s8, u8 = m.step[at, lanes], m.u[at, lanes]
        ys = []
        for j in range(8):
            t = pl.ds(pl.multiple_of((i * 8 + j) * n, 8), n)
            b, c = wide(m.bb[t]), wide(m.cc[t])
            h = jnp.exp2(spread(s8[j : j + 1], n) * a2) * h + spread(u8[j : j + 1], n) * b
            ys.append(jnp.sum(c * h, axis=0, keepdims=True))
        m.y[at, lanes] = jnp.concatenate(ys, axis=0)
        return h

    lax.fori_loop(0, m.step.shape[0] // 8, chunk, m.edges[0, :, lanes])


def scan_back(m, lanes, first):
    a2 = m.a2[:, lanes]
    n = a2.shape[0]
    tokens = m.step.shape[0]

    def ahead(i, h):
        at = pl.ds(pl.multiple_of(i * 8, 8), 8)
        s8, u8, d8 = m.step[at, lanes], m.u[at, lanes], m.d_res[at, lanes]
        for j in range(8):
            t = pl.ds(pl.multiple_of((i * 8 + j) * n, 8), n)
            m.h[i * 8 + j] = h
            h = jnp.exp2(spread(s8[j : j + 1], n) * a2) * h + spread(u8[j : j + 1], n) * wide(m.bb[t])
            part = fold(spread(d8[j : j + 1], n) * h)
            m.cg[t] = part if first else m.cg[t] + part
        return h

    lax.fori_loop(0, tokens // 8, ahead, m.edges[0, :, lanes])

    def behind(i, held):
        q, rate = held
        r = tokens // 8 - 1 - i
        at = pl.ds(pl.multiple_of(r * 8, 8), 8)
        s8, u8, d8 = m.step[at, lanes], m.u[at, lanes], m.d_res[at, lanes]
        sg, lb = [None] * 8, [None] * 8
        for j in reversed(range(8)):
            t = pl.ds(pl.multiple_of((r * 8 + j) * n, 8), n)
            st = spread(s8[j : j + 1], n)
            lam = spread(d8[j : j + 1], n) * wide(m.cc[t]) + q
            q = jnp.exp2(st * a2) * lam
            dec = q * m.h[r * 8 + j]
            lb[j] = jnp.sum(lam * wide(m.bb[t]), axis=0, keepdims=True)
            sg[j] = jnp.sum(dec * a2, axis=0, keepdims=True)
            rate = rate + dec * st
            part = fold(lam * spread(u8[j : j + 1], n))
            m.bg[t] = part if first else m.bg[t] + part
        lb8, sg8 = jnp.concatenate(lb, axis=0), jnp.concatenate(sg, axis=0)
        m.sg[at, lanes] = LN2 * sg8 + m.mixed[at, lanes] * lb8
        m.ms[at, lanes] = s8 * lb8
        return q, rate

    _, rate = lax.fori_loop(0, tokens // 8, behind, (m.edges[1, :, lanes], jnp.zeros_like(a2)))
    m.rate[:, lanes] = rate


class Refs:
    pass


ARGS = ["x", "g", "gain", "w_in", "conv_w", "conv_b", "x_proj", "step_proj", "step_b", "code", "a2", "skip", "w_out"]
OUTS = ["block_out", "input_grad", "in_sum", "out_sum", "small_sum"]


def scratch(sizes, tokens, width, inner, n, rank):
    full = (tokens, inner)
    quarter, part = inner // 4, width // 2
    zs = log2(sizes["seq"]) - 1 + log2(sizes["batch"]) - 2
    v = lambda *shape: pltpu.VMEM(shape, f32)
    sh = {name: v(*full) for name in ("gate", "d_res", "conv", "mixed", "pre", "step", "u", "y", "gated", "d_gate", "sg", "ms", "x_grad")}
    sh.update(
        normed=v(tokens, width), hid=v(8 + tokens, inner), cgr=v(tokens + 8, inner), proj=v(tokens, LANES),
        wbuf=v(SLOTS, width, WBLOCK), w_out_v=v(inner, width), acc=v(tokens, width),
        bb=v(tokens * n, LANES), cc=v(tokens * n, LANES), bg=v(tokens * n, LANES), cg=v(tokens * n, LANES),
        h=v(tokens, n, SCAN), rate=v(n, inner), ends=v(3, n, inner), edges=v(2, n, inner),
        ng=v(8, tokens, part), gg=v(8, tokens, part),
        late0=v(8, tokens, quarter), late1=v(8, tokens, quarter), late2=v(8, tokens, quarter),
        tile0=v(quarter, part), tile1=v(part, quarter), tile2=v(part, quarter),
        land0=v(landing_rows(quarter, zs), part), land1=v(landing_rows(part, zs), quarter), land2=v(landing_rows(part, zs), quarter),
        small=v(*SMALL), small_land=v(landing_rows(SMALL[0], len(small_plan(sizes))), SMALL[1]),
    )
    sh["got"], sh["back"] = carry_scratch(sizes["seq"], n, inner)
    sh["send"], sh["recv"] = [pltpu.SemaphoreType.DMA((160,))] * 2
    sh["wsem"] = pltpu.SemaphoreType.DMA((SLOTS,))
    sh["osem"] = pltpu.SemaphoreType.DMA
    return sh


def stream(m, blocks, use):
    def fetch(i, slot):
        cols = pl.ds(mult(i * WBLOCK, WBLOCK), WBLOCK)
        return pltpu.make_async_copy(m.w_in.at[:, cols], m.wbuf.at[slot], m.wsem.at[slot])

    first, last = blocks
    for k in range(SLOTS - 1):
        fetch(first + k, k).start()

    def body(i):
        slot = lax.rem(i, SLOTS)
        fetch(first + i, slot).wait()

        @pl.when(i + SLOTS - 1 < last - first)
        def _():
            fetch(first + i + SLOTS - 1, lax.rem(i + SLOTS - 1, SLOTS)).start()

        use(i, m.wbuf[slot])

    loop(last - first, body)


def tile_chain(place, links, m, k, value, left, right, zplan, out, region):
    late, tile, land = getattr(m, f"late{k}"), getattr(m, f"tile{k}"), getattr(m, f"land{k}")
    quarter = late.shape[2]
    c, q = place.c, place.q
    core, _ = place.near(0, 0, 1)

    def cut(quart):
        return value.at[:, pl.ds(mult(quart * quarter, LANES), quarter)]

    def pass_on(quart):
        slot = late.at[quart * 2 + c]
        return links.copy(slot, slot, core)

    sent = []
    for dx, dy in ((1, 0), (0, 1), (1, 1)):
        to, quart = place.near(dx, dy, 0)
        sent.append((links.copy(cut(quart), late.at[q * 2 + c], to), quart))
    late[q * 2 + c] = cut(q)[...]
    passed = [pass_on(q)]
    yield
    for copy, quart in sent:
        copy.wait_recv()
        passed.append(pass_on(quart))
    yield
    for copy in passed:
        copy.wait_recv()
    for i in range(4):
        part = matmul(left(i), right(i), ((0,), (0,)))
        tile[...] = part if i == 0 else tile[...] + part
    yield from reduce_rows(place, links, zplan, tile, land, lambda row, rows: region(q, c, row, rows))

    def mine(quart):
        return region(quart, c, 0, tile.shape[0])

    def give(quart, to):
        part = mine(quart)
        return links.copy(part, part, to)

    first, q1 = place.near(1 - c, c, 0)
    second, q2 = place.near(c, 1 - c, 0)
    _, q3 = place.near(1, 1, 0)
    a, b, across = give(q, first), give(q, second), [give(q, core)]
    yield
    a.wait_recv()
    d = give(q1, second)
    across.append(give(q1, core))
    yield
    b.wait_recv()
    across.append(give(q2, core))
    yield
    d.wait_recv()
    across.append(give(q3, core))
    yield
    for copy in across:
        copy.wait_recv()


def block_kernel(sizes, names, *refs):
    m = Refs()
    for name, ref in zip(ARGS + OUTS + names, refs):
        setattr(m, name, ref)
    place = Place(sizes)
    links = Links(m.send, m.recv)
    s, b, c, q = place.s, place.b, place.c, place.q
    count = sizes["seq"]
    tokens, width = m.x.shape
    inner, n = m.a2.shape[1], m.a2.shape[0]
    rank = m.step_proj.shape[0]
    taps = m.conv_w.shape[0]
    part = width // 2
    last = s == count - 1

    bar = pltpu.get_barrier_semaphore()
    greet = [place.near(*d)[0] for d in GROUP] + [(p, b) for p in carry_peers(count, s)]
    greet += [(lax.rem(s + 1, count), b), (lax.rem(s + count - 1, count), b)]
    for to in greet:
        pl.semaphore_signal(bar, inc=1, device_id=to, device_id_type=MESH)
    fetch_out = pltpu.make_async_copy(m.w_out, m.w_out_v, m.osem)
    fetch_out.start()

    x = m.x[...]
    rms = lax.rsqrt(jnp.mean(x * x, axis=1, keepdims=True) + EPSILON)
    m.normed[...] = x * rms * m.gain[...]
    pl.semaphore_wait(bar, len(greet))
    slot = q * 2 + c
    early = []
    for d in GROUP:
        to, _ = place.near(*d)
        half = pl.ds(mult((c + d[2] * (1 - 2 * c)) * part, LANES), part)
        early.append(links.copy(m.normed.at[:, half], m.ng.at[slot], to))
        early.append(links.copy(m.g.at[:, half], m.gg.at[slot], to))
    own = pl.ds(mult(c * part, LANES), part)
    m.ng[slot] = m.normed[:, own]
    m.gg[slot] = m.g[:, own]

    left = stacked(m.normed[...])
    half_blocks = inner // WBLOCK

    def to_hidden(i, w):
        m.hid[pl.ds(8, tokens), pl.ds(mult(i * WBLOCK, WBLOCK), WBLOCK)] = rows_matmul(left, w, ((1,), (0,)))

    stream(m, (0, half_blocks), to_hidden)
    halo = links.copy(m.hid.at[pl.ds(tokens, 8)], m.hid.at[pl.ds(0, 8)], (lax.rem(s + 1, count), b), start=False)

    @pl.when(jnp.logical_not(last))
    def _():
        halo.start()

    def to_gate(i, w):
        m.gate[:, pl.ds(mult(i * WBLOCK, WBLOCK), WBLOCK)] = rows_matmul(left, w, ((1,), (0,)))

    stream(m, (half_blocks, 2 * half_blocks), to_gate)

    fetch_out.wait()
    g_left = stacked(m.g[...])

    def to_d_res(i):
        cols = pl.ds(mult(i * WBLOCK, WBLOCK), WBLOCK)
        d = rows_matmul(g_left, m.w_out_v[cols], ((1,), (1,)))
        z = m.gate[:, cols]
        sg = sigmoid(z)
        m.d_res[:, cols] = d * (z * sg)
        m.d_gate[:, cols] = d * (sg * (1.0 + z * (1.0 - sg)))

    loop(half_blocks, to_d_res)

    @pl.when(s > 0)
    def _():
        halo.wait_recv()

    @pl.when(s == 0)
    def _():
        m.hid[pl.ds(0, 8)] = jnp.zeros((8, inner), f32)

    def convolve(i):
        at = pl.ds(mult(i * 8, 8), 8)
        window = m.hid[pl.ds(mult(i * 8, 8), 16)]
        v = m.conv_b[...]
        for k in range(taps):
            o = 8 - taps + 1 + k
            v = v + m.conv_w[k : k + 1] * window[o : o + 8]
        m.conv[at] = v
        m.mixed[at] = v * sigmoid(v)

    loop(tokens // 8, convolve)

    proj = matmul(m.mixed[...], m.x_proj[...], ((1,), (1,)))
    m.proj[:, : proj.shape[1]] = proj
    low_rank = proj[:, :rank]
    for j in range(n):
        at = pl.ds(j, tokens, stride=n)
        m.bb[at] = jnp.broadcast_to(proj[:, rank + j : rank + j + 1], (tokens, LANES))
        m.cc[at] = jnp.broadcast_to(proj[:, rank + n + j : rank + n + j + 1], (tokens, LANES))
    low_left = stacked(low_rank)

    def to_step(i):
        cols = pl.ds(mult(i * WBLOCK, WBLOCK), WBLOCK)
        pre = rows_matmul(low_left, m.step_proj[:, cols], ((1,), (0,))) + (m.step_b[:, cols] - 0.5 * m.code[:, cols].astype(f32))
        step = jnp.maximum(pre, 0.0) + jnp.log1p(jnp.exp(-jnp.abs(pre)))
        m.pre[:, cols] = pre
        m.step[:, cols] = step
        m.u[:, cols] = step * m.mixed[:, cols]

    loop(half_blocks, to_step)

    blocks = [slice(k, k + SCAN) for k in range(0, inner, SCAN)]
    for lanes in blocks:
        scan_ends(m, lanes)
    carry(place, links, m.ends, m.edges, m.got, m.back)
    for lanes in blocks:
        scan_out(m, lanes)

    def to_gated(i):
        at = pl.ds(mult(i * 8, 8), 8)
        result = m.y[at] + m.skip[...] * m.mixed[at]
        z = m.gate[at]
        m.gated[at] = result * (z * sigmoid(z))
        m.d_gate[at] = m.d_gate[at] * result

    loop(tokens // 8, to_gated)

    s_bits, b_bits = all_bits(sizes)
    zplan = [(k, k) for k in s_bits[1:] + b_bits[2:]]
    quarter = inner // 4

    def pair(ref):
        return lambda i: ref[pl.ds(2 * i, 2)].reshape(2 * tokens, ref.shape[2])

    def out_region(quart, half, row, rows):
        return m.out_sum.at[pl.ds(mult(quart * quarter + row, 8), rows), pl.ds(mult(half * part, LANES), part)]

    def in_region(base):
        return lambda quart, half, row, rows: m.in_sum.at[
            pl.ds(mult(half * part + row, 8), rows), pl.ds(mult(base + quart * quarter, LANES), quarter)]

    def chain(k, value, left, right, region):
        return tile_chain(place, links, m, k, value, pair(left), pair(right), zplan, None, region)

    chains = []

    def go(*which):
        for w in which:
            if w < len(chains) and chains[w] is not None:
                try:
                    next(chains[w])
                except StopIteration:
                    chains[w] = None

    chains.append(chain(0, m.gated, m.late0, m.gg, out_region))
    go(0)
    chains.append(chain(1, m.d_gate, m.ng, m.late1, in_region(inner)))
    go(1)

    scan_back(m, blocks[0], True)
    go(0, 1)
    for e in early:
        e.wait_recv()
    scan_back(m, blocks[1], False)
    go(0)
    scan_back(m, blocks[2], False)
    go(1)

    column = lax.broadcasted_iota(jnp.int32, (tokens, LANES), 1)

    def collect(ref, base, total):
        for j in range(n):
            rows = jnp.sum(ref[pl.ds(j, tokens, stride=n)], axis=1, keepdims=True)
            total = total + jnp.where(column == base + j, rows, 0.0)
        return total

    bc_grad = collect(m.cg, rank + n, collect(m.bg, rank, jnp.zeros((tokens, LANES), f32)))

    def to_pre_grad(i, total):
        at = pl.ds(pl.multiple_of(i * 8, 8), 8)
        v = m.sg[at] * sigmoid(m.pre[at])
        m.sg[at] = v
        return total[0] + v, total[1] + m.d_res[at] * m.mixed[at]

    zero = jnp.zeros((8, inner), f32)
    total = lax.fori_loop(0, tokens // 8, to_pre_grad, (zero, zero))
    bias_grad, skip_grad = (jnp.sum(v, axis=0, keepdims=True) for v in total)
    pre_grad = m.sg[...]
    low_grad = matmul(pre_grad, m.step_proj[...], ((1,), (1,)))
    proj_grad = jnp.concatenate([low_grad, bc_grad[:, rank : rank + 2 * n]], axis=1)

    def put_small(row, value):
        rows = value.shape[0]
        cut, top = SMALL[1], 80
        m.small[row : row + rows] = value[:, :cut]
        over = inner - cut
        if row < top:
            m.small[2 * top + row : 2 * top + row + rows, :over] = value[:, cut:]
        else:
            m.small[top + row : top + row + rows, over:] = value[:, cut:]

    go(0)
    put_small(0, matmul(proj_grad, m.mixed[...], ((0,), (0,))))
    put_small(rank + 2 * n, matmul(m.proj[:, :rank], pre_grad, ((0,), (0,))))
    put_small(2 * rank + 2 * n, m.rate[...] * m.a2[...] * LN2)
    go(1)

    pg_left = stacked(proj_grad)

    def to_mixed_grad(i):
        cols = pl.ds(mult(i * WBLOCK, WBLOCK), WBLOCK)
        d = rows_matmul(pg_left, m.x_proj[:, cols], ((1,), (0,)))
        v = m.conv[:, cols]
        sg = sigmoid(v)
        d = d + m.ms[:, cols] + m.d_res[:, cols] * m.skip[:, cols]
        m.cgr[pl.ds(0, tokens), cols] = d * (sg * (1.0 + v * (1.0 - sg)))

    loop(half_blocks, to_mixed_grad)
    halo_back = links.copy(m.cgr.at[pl.ds(0, 8)], m.cgr.at[pl.ds(tokens, 8)], (lax.rem(s + count - 1, count), b), start=False)

    @pl.when(s > 0)
    def _():
        halo_back.start()

    def to_taps(i, total):
        at = pl.ds(pl.multiple_of(i * 8, 8), 8)
        window = m.hid[pl.ds(pl.multiple_of(i * 8, 8), 16)]
        v = m.cgr[at]
        o = 8 - taps + 1
        return tuple(t + v * window[o + k : o + k + 8] for k, t in enumerate(total[:-1])) + (total[-1] + v,)

    total = lax.fori_loop(0, tokens // 8, to_taps, (zero,) * (taps + 1))
    tap_rows = [jnp.sum(v, axis=0, keepdims=True) for v in total]
    go(0)

    @pl.when(jnp.logical_not(last))
    def _():
        halo_back.wait_recv()

    @pl.when(last)
    def _():
        m.cgr[pl.ds(tokens, 8)] = jnp.zeros((8, inner), f32)

    def to_x_grad(i):
        window = m.cgr[pl.ds(mult(i * 8, 8), 16)]
        v = m.conv_w[0:1] * window[taps - 1 : taps + 7]
        for k in range(1, taps):
            o = taps - 1 - k
            v = v + m.conv_w[k : k + 1] * window[o : o + 8]
        m.x_grad[pl.ds(mult(i * 8, 8), 8)] = v

    loop(tokens // 8, to_x_grad)
    chains.append(chain(2, m.x_grad, m.ng, m.late2, in_region(0)))
    go(2, 1)

    m.acc[...] = jnp.zeros_like(m.acc)

    def to_normed(ref):
        def use(i, w):
            d = stacked(ref[:, pl.ds(mult(i * WBLOCK, WBLOCK), WBLOCK)])
            m.acc[...] = m.acc[...] + rows_matmul(d, w, ((1,), (1,)))

        return use

    stream(m, (0, half_blocks), to_normed(m.x_grad))
    go(0, 2, 1)
    stream(m, (half_blocks, 2 * half_blocks), to_normed(m.d_gate))
    x = m.x[...]
    rms = lax.rsqrt(jnp.mean(x * x, axis=1, keepdims=True) + EPSILON)
    normed_grad = m.acc[...]
    gain_grad = jnp.sum(normed_grad * x * rms, axis=0, keepdims=True)
    weighted = normed_grad * m.gain[...]
    m.input_grad[...] = rms * weighted - rms * rms * rms * x * jnp.mean(weighted * x, axis=1, keepdims=True) + m.g[...]
    rows = tap_rows + [bias_grad, skip_grad, jnp.concatenate([gain_grad, jnp.zeros((1, inner - width), f32)], axis=1)]
    put_small(2 * rank + 3 * n, jnp.concatenate(rows, axis=0))
    end = 2 * rank + 3 * n + 8
    m.small[end:160] = jnp.zeros((160 - end, SMALL[1]), f32)
    m.small[240:256] = jnp.zeros((16, SMALL[1]), f32)
    m.small[80 + end : 240, SMALL[1] // 2 :] = jnp.zeros((160 - end, SMALL[1] // 2), f32)
    chains.append(reduce_rows(place, links, small_plan(sizes), m.small, m.small_land, lambda row, rows: m.small_sum.at[pl.ds(mult(row, 8), rows)]))
    go(3, 0, 2, 1)

    gl = stacked(m.gated[...])

    def to_out(i):
        cols = pl.ds(mult(i * WBLOCK, WBLOCK), WBLOCK)
        m.block_out[:, cols] = m.x[:, cols] + rows_matmul(gl, m.w_out_v[:, cols], ((1,), (0,)))

    loop(width // WBLOCK, to_out)
    while any(v is not None for v in chains):
        go(0, 1, 3, 2)

    @pl.when(jnp.logical_not(last))
    def _():
        halo.wait_send()

    @pl.when(s > 0)
    def _():
        halo_back.wait_send()

    links.drain()


def unpack_kernel(rank, n, a_v, b_v, c_v, d_v, small, a_o, b_o, c_o, d_o, x_proj_o, step_proj_o, decay_o, rows_o, sems):
    copies = [pltpu.make_async_copy(v, o, sems.at[i]) for i, (v, o) in enumerate(((a_v, a_o), (b_v, b_o), (c_v, c_o), (d_v, d_o)))]
    for c in copies:
        c.start()

    def take(row, rows):
        over = SMALL[1] // 2
        if row < 80:
            tail = small[160 + row : 160 + row + rows, :over]
        else:
            tail = small[80 + row : 80 + row + rows, over:]
        return jnp.concatenate([small[row : row + rows], tail], axis=1)

    x_proj_o[...] = take(0, rank + 2 * n)
    step_proj_o[...] = take(rank + 2 * n, rank)
    decay_o[...] = take(2 * rank + 2 * n, n)
    rows_o[...] = take(2 * rank + 3 * n, 8)
    for c in copies:
        c.wait()


VMEM = pl.BlockSpec(memory_space=pltpu.VMEM)
ANY = pl.BlockSpec(memory_space=pl.ANY)


def shards(sizes, inputs, norm_gain, w_in, conv_weight, conv_bias, x_proj, step_proj, step_bias, decay_code, decay_log,
           skip_gain, w_out, cotangent):
    seqs, tokens, width = inputs.shape
    assert seqs == 1 and sizes["batch"] == 4 and sizes["seq"] % 2 == 0
    inner = w_in.shape[1] // 2
    rank, n, taps = step_proj.shape[0], decay_log.shape[1], conv_weight.shape[0]
    row = lambda v: v.reshape(1, -1)
    sh = scratch(sizes, tokens, width, inner, n, rank)
    args = dict(
        x=inputs[0], g=cotangent[0], gain=row(norm_gain), w_in=w_in, conv_w=conv_weight, conv_b=row(conv_bias), x_proj=x_proj.T,
        step_proj=step_proj, step_b=row(step_bias), code=row(decay_code), a2=(-LOG2E * jnp.exp(decay_log)).T, skip=row(skip_gain),
        w_out=w_out)
    held = [pltpu.VMEM(v, f32) for v in ((tokens, width), (tokens, width), (width, 2 * inner), (inner, width), SMALL)]
    sums = pl.pallas_call(
        functools.partial(block_kernel, sizes, list(sh)),
        in_specs=[ANY if a in ("w_in", "w_out") else VMEM for a in ARGS],
        out_specs=[VMEM] * 5,
        out_shape=held,
        scratch_shapes=list(sh.values()),
        compiler_params=pltpu.CompilerParams(collective_id=1, has_side_effects=True, vmem_limit_bytes=VLIMIT << 20),
        name="block",
    )(*(args[a] for a in ARGS))
    wanted = [v.shape for v in sums[:4]] + [(rank + 2 * n, inner), (rank, inner), (n, inner), (8, inner)]
    block_out, input_grad, in_sum, out_sum, x_proj_sum, step_proj_sum, decay_sum, rows = pl.pallas_call(
        functools.partial(unpack_kernel, rank, n),
        in_specs=[VMEM] * 5,
        out_specs=[ANY] * 4 + [VMEM] * 4,
        out_shape=[jax.ShapeDtypeStruct(v, f32) for v in wanted],
        scratch_shapes=[pltpu.SemaphoreType.DMA((4,))],
        compiler_params=pltpu.CompilerParams(vmem_limit_bytes=VLIMIT2 << 20),
        name="unpack",
    )(*sums)
    return (block_out[None], input_grad[None], rows[7, :width], in_sum, rows[:taps], rows[taps], x_proj_sum.T, step_proj_sum,
            rows[taps + 1], decay_sum.T, rows[taps + 2], out_sum)


VLIMIT, VLIMIT2 = 47, 8


def solution(mesh):
    rows = P("batch", "seq", None)
    return jax.shard_map(
        functools.partial(shards, dict(mesh.shape)),
        mesh=mesh,
        in_specs=(rows,) + (P(),) * 11 + (rows,),
        out_specs=(rows, rows) + (P(),) * 10,
        check_vma=False,
    )
```

```python
import functools

import jax
import jax.numpy as jnp
from jax import lax
from jax.experimental import pallas as pl
from jax.experimental.pallas import tpu as pltpu
from jax.sharding import PartitionSpec as P

f32 = jnp.float32
bf16 = jnp.bfloat16
MESH = pl.DeviceIdType.MESH
EPSILON = 1e-05
LOG2E = 1.4426950408889634
LN2 = 0.6931471805599453
LANES = 128
SCAN = 512
WBLOCK = 256
SLOTS = 4
SMALL = (256, 1024)
PARTS = {"o": 2, "i": 4, "x": 4}
SPREAD = {"o0": "T3", "x0": "T3"}
COPIES = 250
ORDER = [
    "gated", "back0", "back1", "back2", "i", "o", "pre", "i", "i3", "i2", "o", "i0", "o0", "i1", "o1", "mixg",
    "xg", "taps", "mid", "ng0", "i3", "i2", "i0", "i1", "ng1", "inp", "bo", "i3", "o0", "o1", "i2", "i0",
    "i1", "s", "x", "x", "i3", "x1", "x2", "x3", "s", "x0", "i2", "i0", "i1", "o0", "o1", "i3",
    "i2", "i0", "i1", "i3", "s", "x1", "x2", "o0", "x3", "o1", "x0", "i2", "i0", "i1", "i3", "i3",
    "s", "x1", "x2", "x3", "o0", "x0", "o1", "i2", "i2", "s", "i0", "i0", "i3", "i1", "i1", "i3",
    "x1", "o0", "x2", "o0", "x3", "o1", "s", "i2", "x0", "i0", "i1", "x1", "i2", "i0", "i1", "o0",
    "x2", "x3", "s", "x0", "o1", "o1", "x1", "x0", "x0", "x2", "x3", "s", "x0", "x1", "x1", "o0",
    "x2", "x2", "x3", "x3", "o1", "o0", "x0", "o1", "x1", "s", "x0", "x1", "x2", "x3", "s", "x2",
    "x3",
]


def mult(value, by):
    return value if isinstance(value, int) else pl.multiple_of(value, by)


def split(value):
    high = value.astype(bf16)
    return high, (value - high.astype(f32)).astype(bf16)


def dot(a, b, dims):
    return lax.dot_general(a, b, (dims, ((), ())), preferred_element_type=f32)


def matmul(a, b, dims=((1,), (0,))):
    (ah, al), (bh, bl) = split(a), split(b)
    return dot(ah, bh, dims) + dot(al, bh, dims) + dot(ah, bl, dims)


def stacked(value):
    return jnp.concatenate(split(value), axis=0)


def rows_matmul(both, b, dims):
    rows = both.shape[0] // 2
    bh, bl = split(b)
    wide = dot(both, bh, dims)
    return wide[:rows] + wide[rows:] + dot(both[:rows], bl, dims)


def sigmoid(v):
    return 1.0 / (1.0 + jnp.exp(-v))


def loop(count, body):
    def step(i, _):
        body(i)
        return 0

    lax.fori_loop(0, count, step, 0)


class Place:
    def __init__(self, sizes):
        self.sizes = sizes
        self.s, self.b = lax.axis_index("seq"), lax.axis_index("batch")
        self.at = {"seq": self.s, "batch": self.b}
        self.x, self.c, self.y = self.s % 2, self.b % 2, self.b // 2
        self.odd = self.c

    def near(self, dx, dy, dc):
        dx, dy = dx * (1 - 2 * self.x), dy * (1 - 2 * self.y)
        return (self.s + dx, self.b + dc * (1 - 2 * self.c) + 2 * dy), (self.x + dx, self.y + dy)

    def bit(self, d):
        return self.at[d[0]] // (1 << d[1]) % 2

    def stage(self, pair):
        to = dict(self.at)
        first, second = pair
        if first == second:
            v = self.bit(first)
            to[first[0]] = to[first[0]] + (1 - 2 * v) * (1 << first[1])
        else:
            va, vb = self.bit(first), self.bit(second)
            to[first[0]] = to[first[0]] + (1 - self.odd) * (1 - 2 * va) * (1 << first[1])
            to[second[0]] = to[second[0]] + self.odd * (1 - 2 * vb) * (1 << second[1])
            v = (1 - self.odd) * va + self.odd * vb
        return (to["seq"], to["batch"]), v


class Links:
    def __init__(self, send, recv):
        self.send, self.recv, self.used, self.open = send, recv, 0, []

    def copy(self, src, dst, to, start=True):
        i = self.used
        self.used += 1
        c = pltpu.make_async_remote_copy(
            src_ref=src, dst_ref=dst, send_sem=self.send.at[i], recv_sem=self.recv.at[i], device_id=to, device_id_type=MESH
        )
        if start:
            c.start()
            self.open.append(c)
        return c

    def sent(self, copy):
        copy.wait_send()
        self.open = [c for c in self.open if c is not copy]

    def drain(self):
        for c in self.open:
            c.wait_send()
        self.open = []


GROUP = [(1, 0, 0), (1, 0, 1), (0, 1, 0), (0, 1, 1), (0, 0, 1)]


def log2(size):
    return size.bit_length() - 1


def all_bits(sizes):
    s = [("seq", k) for k in range(log2(sizes["seq"]))]
    b = [("batch", k) for k in range(log2(sizes["batch"]))]
    return s, b


def small_plan(sizes):
    s, b = all_bits(sizes)
    return [(b[0], b[0]), (s[0], b[1]), (b[1], s[0])] + [(q, q) for q in s[1:] + b[2:]]


def halvings(rows, stages):
    out = []
    for _ in range(stages):
        ok = rows % 16 == 0
        out.append(ok)
        rows = rows // 2 if ok else rows
    return out


def landing_rows(rows, stages):
    total = 0
    for ok in halvings(rows, stages):
        rows = rows // 2 if ok else rows
        total += rows
    return total


def reduce_rows(place, links, plan, acc, land, kept):
    rows = acc.shape[0]
    off, base = 0, 0
    for pair, ok in zip(plan, halvings(rows, len(plan))):
        to, v = place.stage(pair)
        parent = off
        if ok:
            rows //= 2
            off, give = off + v * rows, off + (1 - v) * rows
        else:
            give = off
        copy = links.copy(acc.at[pl.ds(mult(give, 8), rows)], land.at[pl.ds(base, rows)], to)
        yield
        copy.wait_recv()
        if not ok:
            links.sent(copy)

        def add(i, off=off, base=base):
            at = pl.ds(mult(off + i * 8, 8), 8)
            acc[at] = acc[at] + land[pl.ds(mult(base + i * 8, 8), 8)]

        loop(rows // 8, add)
        base += rows
        if ok:
            kept.append((to, parent, off, rows))
    return off, rows


def place_rows(acc, off, rows, whole):
    def one(i):
        whole(off + i * 8, 8)[...] = acc[pl.ds(mult(off + i * 8, 8), 8)]

    loop(rows // 8, one)


def small_chain(place, links, plan, acc, land, out):
    whole = lambda row, rows: out.at[pl.ds(mult(row, 8), rows)]
    kept = []
    off, rows = yield from reduce_rows(place, links, plan, acc, land, kept)
    place_rows(acc, off, rows, whole)
    for to, _, off, rows in reversed(kept):
        copy = links.copy(whole(off, rows), whole(off, rows), to)
        yield
        copy.wait_recv()


def tiled(count):
    return count in (2, 4, 6, 8, 12, 24)


def carry_peers(count, s):
    if tiled(count):
        return [lax.rem(s + i, count) for i in range(1, count)]
    return [s + (1 - 2 * (s // (1 << k) % 2)) * (1 << k) for k in range(log2(count))]


def carry_scratch(count, n, inner):
    v = lambda *shape: pltpu.VMEM(shape, f32)
    if tiled(count):
        w = inner // (count // 2)
        return dict(got=v(count, 2, 8, w), back=v(count, 2, 8, w), got_sum=v(count, 1, w), tile_dec=v(count, 8, w))
    return dict(got=v(2 * log2(count), 2, n, inner), back=v(2, n, inner), tot=v(2, n, inner))


def carry(place, links, m, way):
    return (carry_tiles if tiled(place.sizes["seq"]) else carry_doubling)(place, links, m, way)


def carry_doubling(place, links, m, way):
    bits = log2(place.sizes["seq"])
    m.edges[way] = jnp.zeros_like(m.edges[way])
    m.back[way] = jnp.ones_like(m.back[way])
    m.tot[0] = m.ends[way]
    m.tot[1] = jnp.exp2(m.a2[...] * m.sums[...])
    for k, p in enumerate(carry_peers(place.sizes["seq"], place.s)):
        got = m.got.at[way * bits + k]
        copy = links.copy(m.tot, got, (p, place.b))
        copy.wait_recv()
        links.sent(copy)
        later = place.bit(("seq", k))

        @pl.when(later == 1 - way)
        def _():
            m.edges[way] += m.back[way] * got[0]
            m.back[way] *= got[1]
            m.tot[0] += m.tot[1] * got[0]

        @pl.when(later == way)
        def _():
            m.tot[0] = got[0] + got[1] * m.tot[0]

        m.tot[1] *= got[1]
    yield
    yield


def carry_tiles(place, links, m, way):
    count, s, b = place.sizes["seq"], place.s, place.b
    across = count // 2
    width = m.ends.shape[2] // across
    peers = carry_peers(count, s)

    def cut(ref, p):
        return ref.at[pl.ds(mult(p // across * 8, 8), 8), pl.ds(mult(p % across * width, LANES), width)]

    def cut_sum(p):
        return m.sums.at[:, pl.ds(mult(p % across * width, LANES), width)]

    first = [links.copy(cut(m.ends.at[way], p), m.got.at[s, way], (p, b)) for p in peers]
    m.got[s, way] = cut(m.ends.at[way], s)[...]
    if way == 0:
        first += [links.copy(cut_sum(p), m.got_sum.at[s], (p, b)) for p in peers]
        m.got_sum[s] = cut_sum(s)[...]
    yield
    for c in first:
        c.wait_recv()
    if way == 0:
        a2 = cut(m.a2, s)[...]
        for p in range(count):
            m.tile_dec[p] = jnp.exp2(a2 * m.got_sum[p])
    value = jnp.zeros((8, width), f32)
    for p in reversed(range(count)) if way else range(count):
        m.back[p, way] = value
        value = m.got[p, way] + m.tile_dec[p] * value
    second = [links.copy(m.back.at[p, way], cut(m.edges.at[way], s), (p, b)) for p in peers]
    cut(m.edges.at[way], s)[...] = m.back[s, way]
    yield
    for c in second:
        c.wait_recv()


def wide(tile):
    return jnp.concatenate([tile] * (SCAN // LANES), axis=1)


def spread(row, n):
    return jnp.broadcast_to(row, (n, row.shape[1]))


def fold(value):
    return sum(value[:, k : k + LANES] for k in range(0, value.shape[1], LANES))


def scan_ends(m, lanes):
    a2 = m.a2[:, lanes]
    n = a2.shape[0]

    def chunk(i, h):
        at = pl.ds(pl.multiple_of(i * 8, 8), 8)
        s8, u8 = m.step[at, lanes], m.u[at, lanes]
        for j in range(8):
            b = wide(m.bb[pl.ds(pl.multiple_of((i * 8 + j) * n, 8), n)])
            h = jnp.exp2(spread(s8[j : j + 1], n) * a2) * h + spread(u8[j : j + 1], n) * b
        return h

    m.ends[0, :, lanes] = lax.fori_loop(0, m.step.shape[0] // 8, chunk, jnp.zeros_like(a2))


def scan_lams(m, lanes):
    a2 = m.a2[:, lanes]
    n = a2.shape[0]

    def chunk(i, held):
        dec, acc = held
        at = pl.ds(pl.multiple_of(i * 8, 8), 8)
        s8, d8 = m.step[at, lanes], m.d_res[at, lanes]
        for j in range(8):
            c = wide(m.cc[pl.ds(pl.multiple_of((i * 8 + j) * n, 8), n)])
            dec = dec * jnp.exp2(spread(s8[j : j + 1], n) * a2)
            acc = acc + dec * (spread(d8[j : j + 1], n) * c)
        return dec, acc

    zero = jnp.zeros_like(a2)
    m.ends[1, :, lanes] = lax.fori_loop(0, m.step.shape[0] // 8, chunk, (zero + 1.0, zero))[1]


def scan_out(m, lanes):
    a2 = m.a2[:, lanes]
    n = a2.shape[0]

    def chunk(i, h):
        at = pl.ds(pl.multiple_of(i * 8, 8), 8)
        s8, u8 = m.step[at, lanes], m.u[at, lanes]
        ys = []
        for j in range(8):
            t = pl.ds(pl.multiple_of((i * 8 + j) * n, 8), n)
            b, c = wide(m.bb[t]), wide(m.cc[t])
            h = jnp.exp2(spread(s8[j : j + 1], n) * a2) * h + spread(u8[j : j + 1], n) * b
            ys.append(jnp.sum(c * h, axis=0, keepdims=True))
        m.y[at, lanes] = jnp.concatenate(ys, axis=0)
        return h

    lax.fori_loop(0, m.step.shape[0] // 8, chunk, m.edges[0, :, lanes])


def scan_back(m, lanes, first):
    a2 = m.a2[:, lanes]
    n = a2.shape[0]
    tokens = m.step.shape[0]

    def ahead(i, h):
        at = pl.ds(pl.multiple_of(i * 8, 8), 8)
        s8, u8, d8 = m.step[at, lanes], m.u[at, lanes], m.d_res[at, lanes]
        for j in range(8):
            t = pl.ds(pl.multiple_of((i * 8 + j) * n, 8), n)
            m.h[i * 8 + j] = h
            h = jnp.exp2(spread(s8[j : j + 1], n) * a2) * h + spread(u8[j : j + 1], n) * wide(m.bb[t])
            part = fold(spread(d8[j : j + 1], n) * h)
            m.cg[t] = part if first else m.cg[t] + part
        return h

    lax.fori_loop(0, tokens // 8, ahead, m.edges[0, :, lanes])

    def behind(i, held):
        q, rate = held
        r = tokens // 8 - 1 - i
        at = pl.ds(pl.multiple_of(r * 8, 8), 8)
        s8, u8, d8 = m.step[at, lanes], m.u[at, lanes], m.d_res[at, lanes]
        sg, lb = [None] * 8, [None] * 8
        for j in reversed(range(8)):
            t = pl.ds(pl.multiple_of((r * 8 + j) * n, 8), n)
            st = spread(s8[j : j + 1], n)
            lam = spread(d8[j : j + 1], n) * wide(m.cc[t]) + q
            q = jnp.exp2(st * a2) * lam
            dec = q * m.h[r * 8 + j]
            lb[j] = jnp.sum(lam * wide(m.bb[t]), axis=0, keepdims=True)
            sg[j] = jnp.sum(dec * a2, axis=0, keepdims=True)
            rate = rate + dec * st
            part = fold(lam * spread(u8[j : j + 1], n))
            m.bg[t] = part if first else m.bg[t] + part
        lb8, sg8 = jnp.concatenate(lb, axis=0), jnp.concatenate(sg, axis=0)
        m.sg[at, lanes] = LN2 * sg8 + m.mixed[at, lanes] * lb8
        m.gate[at, lanes] = s8 * lb8
        return q, rate

    _, rate = lax.fori_loop(0, tokens // 8, behind, (m.edges[1, :, lanes], jnp.zeros_like(a2)))
    m.rate[:, lanes] = rate


class Refs:
    pass


FETCH = ["x", "gain", "g", "w_out", "conv_w", "conv_b", "x_proj", "step_proj", "step_b", "code", "a2", "skip"]
ARGS = [v + "_h" for v in FETCH] + ["w_in"]
OUTS = ["block_out", "input_grad", "in_sum", "out_sum", "small_sum"]


def pieces(key):
    return (PARTS[key], 1) if key == "o" else {1: (1, 1), 2: (1, 2), 4: (2, 2)}[PARTS[key]]


def scratch(sizes, tokens, width, inner, n, rank, taps):
    full = (tokens, inner)
    half, part = inner // 2, width // 2
    stages = log2(sizes["seq"])
    v = lambda *shape: pltpu.VMEM(shape, f32)
    sh = {name: v(*full) for name in ("gate", "d_res", "conv", "mixed", "pre", "step", "u", "y", "d_gate", "sg")}
    sh.update(
        x=v(tokens, width), g=v(tokens, width), vec=v(4, inner), gain=v(width // LANES, LANES),
        conv_b=v(inner // LANES, LANES), step_b=v(inner // LANES, LANES), skip=v(inner // LANES, LANES),
        code=pltpu.VMEM((inner // LANES, LANES), jnp.int32), conv_w=v(taps, inner), x_proj=v(rank + 2 * n, inner),
        step_proj=v(rank, inner), a2=v(n, inner), w_out=v(inner, width),
        normed=v(tokens, width), hid=v(8 + tokens, inner), cgr=v(tokens + 8, inner), proj=v(tokens, LANES),
        wbuf=v(SLOTS, width, WBLOCK), acc=v(tokens, width),
        bb=v(tokens * n, LANES), cc=v(tokens * n, LANES), bg=v(tokens * n, LANES), cg=v(tokens * n, LANES),
        h=v(tokens, n, SCAN), rate=v(n, inner), ends=v(2, n, inner), edges=v(2, n, inner), sums=v(1, inner),
        ng=v(4, tokens, part), gg=v(4, tokens, part),
        small=v(*SMALL), small_land=v(landing_rows(SMALL[0], len(small_plan(sizes))), SMALL[1]),
    )
    for key in "oix":
        rows, cols = (half, part) if key == "o" else (part, half)
        down, over = pieces(key)
        sh["late_" + key] = v(4, tokens, half)
        for k in range(down * over):
            sh[f"tile_{key}{k}"] = v(rows // down, cols // over)
            sh[f"land_{key}{k}"] = v(landing_rows(rows // down, stages), cols // over)
    sh.update(carry_scratch(sizes["seq"], n, inner))
    sh["send"], sh["recv"] = [pltpu.SemaphoreType.DMA((COPIES,))] * 2
    sh["wsem"] = pltpu.SemaphoreType.DMA((SLOTS,))
    sh["isem"] = pltpu.SemaphoreType.DMA((len(FETCH),))
    return sh


def stream(m, first, last):
    def fetch(i, slot):
        cols = pl.ds(mult((first + i) * WBLOCK, WBLOCK), WBLOCK)
        return pltpu.make_async_copy(m.w_in.at[:, cols], m.wbuf.at[slot], m.wsem.at[slot])

    ahead = SLOTS - 1
    for k in range(ahead):
        fetch(k, k).start()

    def run(use):
        def body(i):
            slot = lax.rem(i, SLOTS)
            fetch(i, slot).wait()

            @pl.when(i + ahead < last - first)
            def _():
                fetch(i + ahead, lax.rem(i + ahead, SLOTS)).start()

            use(i, m.wbuf[slot])

        loop(last - first, body)

    return run


def late_chain(place, links, m, key, value, left, right):
    late = getattr(m, "late_" + key)
    half = late.shape[2]
    mine = place.y if key == "o" else place.x
    to, _ = place.near(0, 1, 0) if key == "o" else place.near(1, 0, 0)
    core, _ = place.near(0, 0, 1)

    def cut(which):
        return value.at[:, pl.ds(mult(which * half, LANES), half)]

    def pass_on(which):
        slot = late.at[which * 2 + place.c]
        return links.copy(slot, slot, core)

    sent = links.copy(cut(1 - mine), late.at[mine * 2 + place.c], to)
    late[mine * 2 + place.c] = cut(mine)[...]
    passed = [pass_on(mine)]
    yield
    sent.wait_recv()
    passed.append(pass_on(1 - mine))
    yield
    for copy in passed:
        copy.wait_recv()
    down, over = pieces(key)
    for i in range(2):
        part = matmul(left(i), right(i), ((0,), (0,)))
        rows, cols = part.shape[0] // down, part.shape[1] // over
        for k in range(down * over):
            tile = getattr(m, f"tile_{key}{k}")
            r, c = k // over * rows, k % over * cols
            cell = part[r : r + rows, c : c + cols]
            tile[...] = cell if i == 0 else tile[...] + cell


def piece_chain(place, links, m, key, k, zplan, out, base):
    acc, land = getattr(m, f"tile_{key}{k}"), getattr(m, f"land_{key}{k}")
    rows, cols = acc.shape
    over = pieces(key)[1]
    r0, c0 = k // over * rows, k % over * cols
    half, part = out.shape[0] // 2 if key == "o" else out.shape[1] // 4, m.x.shape[1] // 2
    bit = ("seq", 0) if key == "o" else ("batch", 1)
    x, y, c = place.x, place.y, place.c
    core, _ = place.near(0, 0, 1)

    def region(at, row, count):
        xx, yy = at
        if key == "o":
            top, side = yy * half + r0 + xx * (rows // 2) + row, c * part + c0
        else:
            top, side = c * part + r0 + yy * (rows // 2) + row, base + xx * half + c0
        return out.at[pl.ds(mult(top, 8), count), pl.ds(mult(side, LANES), cols)]

    kept = []
    off, count = yield from reduce_rows(place, links, [(bit, bit)] + zplan, acc, land, kept)
    edge = kept[0][2]
    place_rows(acc, off, count, lambda row, n: region((x, y), row - edge, n))
    row = off - edge
    held, across = [(x, y)], []

    def give(at, to):
        ref = region(at, row, count)
        return links.copy(ref, ref, to)

    steps = list(reversed(kept[1:]))
    kind = SPREAD.get(key + str(k), "T1")
    steps.insert({"T1": len(steps), "T2": 0, "T3": 1}[kind], None)
    for i, step in enumerate(steps):
        last = i == len(steps) - 1
        if step is not None:
            to, parent, _, size = step
            copies = [give(at, to) for at in held]
            yield
            for copy in copies:
                copy.wait_recv()
            row, count = parent - edge, 2 * size
            continue
        first, at_a = place.near(1 - c, c, 0)
        second, at_b = place.near(c, 1 - c, 0)
        _, at_d = place.near(1, 1, 0)
        a, b = give((x, y), first), give((x, y), second)
        held = [(x, y), at_a, at_b, at_d]

        def onward(at):
            if last:
                across.append(give(at, core))

        onward((x, y))
        yield
        a.wait_recv()
        d = give(at_a, second)
        onward(at_a)
        yield
        b.wait_recv()
        onward(at_b)
        yield
        d.wait_recv()
        onward(at_d)
    if not across:
        across = [give(at, core) for at in held]
    yield
    for copy in across:
        copy.wait_recv()


def block_kernel(sizes, names, *refs):
    m = Refs()
    for name, ref in zip(ARGS + OUTS + names, refs):
        setattr(m, name, ref)
    place = Place(sizes)
    links = Links(m.send, m.recv)
    s, b, c = place.s, place.b, place.c
    count = sizes["seq"]
    tokens, width = m.x.shape
    inner, n = m.a2.shape[1], m.a2.shape[0]
    rank = m.step_proj.shape[0]
    taps = m.conv_w.shape[0]
    half, part = inner // 2, width // 2
    blocks_of_half = inner // WBLOCK
    last = s == count - 1

    fetched = {}
    for i, name in enumerate(FETCH):
        fetched[name] = pltpu.make_async_copy(getattr(m, name + "_h"), getattr(m, name), m.isem.at[i])
    for name in FETCH[:3]:
        fetched[name].start()
    to_hidden = stream(m, 0, blocks_of_half)
    for name in FETCH[3:]:
        fetched[name].start()
    bar = pltpu.get_barrier_semaphore()
    greet = [place.near(*d)[0] for d in GROUP] + [(p, b) for p in carry_peers(count, s)]
    greet += [(lax.rem(s + 1, count), b), (lax.rem(s + count - 1, count), b)]
    for to in greet:
        pl.semaphore_signal(bar, inc=1, device_id=to, device_id_type=MESH)

    fetched["x"].wait()
    fetched["gain"].wait()

    def to_row(name, k):
        ref = getattr(m, name)
        for j in range(ref.shape[0]):
            m.vec[k : k + 1, j * LANES : (j + 1) * LANES] = ref[j : j + 1]

    to_row("gain", 3)
    x = m.x[...]
    rms = lax.rsqrt(jnp.mean(x * x, axis=1, keepdims=True) + EPSILON)
    m.normed[...] = x * rms * m.vec[3:4, :width]
    fetched["g"].wait()
    pl.semaphore_wait(bar, len(greet))
    early = []
    for d in GROUP:
        to, _ = place.near(*d)
        cols = pl.ds(mult((c + d[2] * (1 - 2 * c)) * part, LANES), part)
        if not d[1]:
            early.append(links.copy(m.normed.at[:, cols], m.ng.at[place.x * 2 + c], to))
        if not d[0]:
            early.append(links.copy(m.g.at[:, cols], m.gg.at[place.y * 2 + c], to))
    own = pl.ds(mult(c * part, LANES), part)
    m.ng[place.x * 2 + c] = m.normed[:, own]
    m.gg[place.y * 2 + c] = m.g[:, own]

    left = stacked(m.normed[...])

    def hidden_block(i, w):
        m.hid[pl.ds(8, tokens), pl.ds(mult(i * WBLOCK, WBLOCK), WBLOCK)] = rows_matmul(left, w, ((1,), (0,)))

    to_hidden(hidden_block)
    to_gate = stream(m, blocks_of_half, 2 * blocks_of_half)
    halo = links.copy(m.hid.at[pl.ds(tokens, 8)], m.hid.at[pl.ds(0, 8)], (lax.rem(s + 1, count), b), start=False)

    @pl.when(jnp.logical_not(last))
    def _():
        halo.start()

    for name in FETCH[3:]:
        fetched[name].wait()
    m.step_b[...] = m.step_b[...] - 0.5 * m.code[...].astype(f32)
    for k, name in enumerate(("conv_b", "step_b", "skip")):
        to_row(name, k)
    m.a2[...] = -LOG2E * jnp.exp(m.a2[...])
    g_left = stacked(m.g[...])

    def d_gated_block(i):
        cols = pl.ds(mult(i * WBLOCK, WBLOCK), WBLOCK)
        m.d_res[:, cols] = rows_matmul(g_left, m.w_out[cols], ((1,), (1,)))

    loop(blocks_of_half, d_gated_block)

    @pl.when(s > 0)
    def _():
        halo.wait_recv()

    @pl.when(s == 0)
    def _():
        m.hid[pl.ds(0, 8)] = jnp.zeros((8, inner), f32)

    def convolve(i):
        window = m.hid[pl.ds(mult(i * 8, 8), 16)]
        v = m.vec[0:1]
        for k in range(taps):
            o = 8 - taps + 1 + k
            v = v + m.conv_w[k : k + 1] * window[o : o + 8]
        at = pl.ds(mult(i * 8, 8), 8)
        m.conv[at] = v
        m.mixed[at] = v * sigmoid(v)

    loop(tokens // 8, convolve)

    proj = matmul(m.mixed[...], m.x_proj[...], ((1,), (1,)))
    m.proj[:, : proj.shape[1]] = proj
    for j in range(n):
        at = pl.ds(j, tokens, stride=n)
        m.bb[at] = jnp.broadcast_to(proj[:, rank + j : rank + j + 1], (tokens, LANES))
        m.cc[at] = jnp.broadcast_to(proj[:, rank + n + j : rank + n + j + 1], (tokens, LANES))
    low_left = stacked(proj[:, :rank])

    def step_block(i):
        cols = pl.ds(mult(i * WBLOCK, WBLOCK), WBLOCK)
        pre = rows_matmul(low_left, m.step_proj[:, cols], ((1,), (0,))) + m.vec[1:2, cols]
        step = jnp.maximum(pre, 0.0) + jnp.log1p(jnp.exp(-jnp.abs(pre)))
        m.pre[:, cols] = pre
        m.step[:, cols] = step
        m.u[:, cols] = step * m.mixed[:, cols]
        m.sums[:, cols] = jnp.sum(step, axis=0, keepdims=True)

    loop(blocks_of_half, step_block)

    blocks = [slice(k, k + SCAN) for k in range(0, inner, SCAN)]
    for lanes in blocks:
        scan_ends(m, lanes)
    ahead = carry(place, links, m, 0)
    next(ahead)

    def gate_block(i, w):
        cols = pl.ds(mult(i * WBLOCK, WBLOCK), WBLOCK)
        z = rows_matmul(left, w, ((1,), (0,)))
        sg = sigmoid(z)
        act = z * sg
        d = m.d_res[:, cols]
        m.gate[:, cols] = act
        m.d_res[:, cols] = d * act
        m.d_gate[:, cols] = d * (sg * (1.0 + z * (1.0 - sg)))

    to_gate(gate_block)
    next(ahead)
    for lanes in blocks:
        scan_lams(m, lanes)
    behind = carry(place, links, m, 1)
    next(behind)
    for _ in ahead:
        pass
    for lanes in blocks:
        scan_out(m, lanes)
    next(behind)

    def gated_rows(i):
        at = pl.ds(mult(i * 8, 8), 8)
        result = m.y[at] + m.vec[2:3] * m.mixed[at]
        m.y[at] = result * m.gate[at]
        m.d_gate[at] = m.d_gate[at] * result

    loop(tokens // 8, gated_rows)

    s_bits, b_bits = all_bits(sizes)
    zplan = [(k, k) for k in s_bits[1:] + b_bits[2:]]
    chains, started, v = {}, set(), Refs()

    def pair(ref):
        return lambda i: ref[pl.ds(2 * i, 2)].reshape(2 * tokens, ref.shape[2])

    def go(name):
        started.add(name)
        try:
            next(chains[name])
        except StopIteration:
            del chains[name]
            if name in "oix":
                where = {"o": (m.out_sum, 0), "i": (m.in_sum, inner), "x": (m.in_sum, 0)}[name]
                for k in range(PARTS[name]):
                    chains[name + str(k)] = piece_chain(place, links, m, name, k, zplan, *where)

    def late(key, value, left, right):
        chains[key] = late_chain(place, links, m, key, value, pair(left), pair(right))
        go(key)

    column = lax.broadcasted_iota(jnp.int32, (tokens, LANES), 1)
    zero = jnp.zeros((8, inner), f32)

    def collect(ref, base, total):
        for j in range(n):
            rows = jnp.sum(ref[pl.ds(j, tokens, stride=n)], axis=1, keepdims=True)
            total = total + jnp.where(column == base + j, rows, 0.0)
        return total

    def put_small(row, value):
        rows = value.shape[0]
        cut, top = SMALL[1], 80
        m.small[row : row + rows] = value[:, :cut]
        over = inner - cut
        if row < top:
            m.small[2 * top + row : 2 * top + row + rows, :over] = value[:, cut:]
        else:
            m.small[top + row : top + row + rows, over:] = value[:, cut:]

    def gated():
        late("o", m.y, m.late_o, m.gg)
        late("i", m.d_gate, m.ng, m.late_i)
        for _ in behind:
            pass

    def back(k):
        scan_back(m, blocks[k], k == 0)
        if k == 0:
            for e in early:
                e.wait_recv()

    def pre():
        bc_grad = collect(m.cg, rank + n, collect(m.bg, rank, jnp.zeros((tokens, LANES), f32)))

        def rows(i, total):
            at = pl.ds(pl.multiple_of(i * 8, 8), 8)
            p = m.sg[at] * sigmoid(m.pre[at])
            m.sg[at] = p
            return total[0] + p, total[1] + m.d_res[at] * m.mixed[at]

        total = lax.fori_loop(0, tokens // 8, rows, (zero, zero))
        v.bias_grad, v.skip_grad = (jnp.sum(t, axis=0, keepdims=True) for t in total)
        low_grad = matmul(m.sg[...], m.step_proj[...], ((1,), (1,)))
        v.proj_grad = jnp.concatenate([low_grad, bc_grad[:, rank : rank + 2 * n]], axis=1)

    def mixg():
        pg_left = stacked(v.proj_grad)

        def block(i):
            cols = pl.ds(mult(i * WBLOCK, WBLOCK), WBLOCK)
            d = rows_matmul(pg_left, m.x_proj[:, cols], ((1,), (0,)))
            z = m.conv[:, cols]
            sg = sigmoid(z)
            d = d + m.gate[:, cols] + m.d_res[:, cols] * m.vec[2:3, cols]
            m.cgr[pl.ds(0, tokens), cols] = d * (sg * (1.0 + z * (1.0 - sg)))

        loop(blocks_of_half, block)
        v.halo_back = links.copy(
            m.cgr.at[pl.ds(0, 8)], m.cgr.at[pl.ds(tokens, 8)], (lax.rem(s + count - 1, count), b), start=False)

        @pl.when(s > 0)
        def _():
            v.halo_back.start()

    def xg():
        @pl.when(jnp.logical_not(last))
        def _():
            v.halo_back.wait_recv()

        @pl.when(last)
        def _():
            m.cgr[pl.ds(tokens, 8)] = jnp.zeros((8, inner), f32)

        def rows(i):
            window = m.cgr[pl.ds(mult(i * 8, 8), 16)]
            z = m.conv_w[0:1] * window[taps - 1 : taps + 7]
            for k in range(1, taps):
                o = taps - 1 - k
                z = z + m.conv_w[k : k + 1] * window[o : o + 8]
            m.gate[pl.ds(mult(i * 8, 8), 8)] = z

        loop(tokens // 8, rows)
        late("x", m.gate, m.ng, m.late_x)

    def taps_():
        def rows(i, total):
            at = pl.ds(pl.multiple_of(i * 8, 8), 8)
            window = m.hid[pl.ds(pl.multiple_of(i * 8, 8), 16)]
            z = m.cgr[at]
            o = 8 - taps + 1
            return tuple(t + z * window[o + k : o + k + 8] for k, t in enumerate(total[:-1])) + (total[-1] + z,)

        total = lax.fori_loop(0, tokens // 8, rows, (zero,) * (taps + 1))
        v.tap_rows = [jnp.sum(t, axis=0, keepdims=True) for t in total]

    def mid():
        put_small(0, matmul(v.proj_grad, m.mixed[...], ((0,), (0,))))
        put_small(rank + 2 * n, matmul(m.proj[:, :rank], m.sg[...], ((0,), (0,))))
        put_small(2 * rank + 2 * n, m.rate[...] * m.a2[...] * LN2)

    def normed_block(ref):
        def use(i, w):
            d = stacked(ref[:, pl.ds(mult(i * WBLOCK, WBLOCK), WBLOCK)])
            m.acc[...] = m.acc[...] + rows_matmul(d, w, ((1,), (1,)))

        return use

    def ng0():
        m.acc[...] = jnp.zeros_like(m.acc)
        stream(m, blocks_of_half, 2 * blocks_of_half)(normed_block(m.d_gate))

    def ng1():
        stream(m, 0, blocks_of_half)(normed_block(m.gate))

    def inp():
        x = m.x[...]
        rms = lax.rsqrt(jnp.mean(x * x, axis=1, keepdims=True) + EPSILON)
        normed_grad = m.acc[...]
        gain_grad = jnp.sum(normed_grad * x * rms, axis=0, keepdims=True)
        weighted = normed_grad * m.vec[3:4, :width]
        m.input_grad[...] = rms * weighted - rms * rms * rms * x * jnp.mean(weighted * x, axis=1, keepdims=True) + m.g[...]
        rows = v.tap_rows + [v.bias_grad, v.skip_grad, jnp.concatenate([gain_grad, jnp.zeros((1, inner - width), f32)], axis=1)]
        put_small(2 * rank + 3 * n, jnp.concatenate(rows, axis=0))
        end = 2 * rank + 3 * n + 8
        m.small[end:160] = jnp.zeros((160 - end, SMALL[1]), f32)
        m.small[240:256] = jnp.zeros((16, SMALL[1]), f32)
        m.small[80 + end : 240, SMALL[1] // 2 :] = jnp.zeros((160 - end, SMALL[1] // 2), f32)
        chains["s"] = small_chain(place, links, small_plan(sizes), m.small, m.small_land, m.small_sum)
        go("s")

    def bo():
        gl = stacked(m.y[...])

        def block(i):
            cols = pl.ds(mult(i * WBLOCK, WBLOCK), WBLOCK)
            m.block_out[:, cols] = m.x[:, cols] + rows_matmul(gl, m.w_out[:, cols], ((1,), (0,)))

        loop(width // WBLOCK, block)

    work = {
        "gated": gated, "back0": lambda: back(0), "back1": lambda: back(1), "back2": lambda: back(2), "pre": pre, "mixg": mixg,
        "xg": xg, "taps": taps_, "mid": mid, "ng0": ng0, "ng1": ng1, "inp": inp, "bo": bo,
    }
    for name in ORDER:
        if name in work:
            work.pop(name)()
        elif name in chains:
            go(name)
    assert not work
    while chains:
        for name in list(chains):
            go(name)

    @pl.when(jnp.logical_not(last))
    def _():
        halo.wait_send()

    @pl.when(s > 0)
    def _():
        v.halo_back.wait_send()

    links.drain()


def unpack_kernel(rank, n, a_v, b_v, c_v, d_v, small, a_o, b_o, c_o, d_o, x_proj_o, step_proj_o, decay_o, rows_o, sems):
    copies = []
    for v, o, cuts in ((c_v, c_o, 8), (d_v, d_o, 4), (a_v, a_o, 1), (b_v, b_o, 1)):
        rows = v.shape[0] // cuts
        for k in range(cuts):
            at = pl.ds(k * rows, rows)
            copies.append(pltpu.make_async_copy(v.at[at], o.at[at], sems.at[len(copies)]))
    for c in copies:
        c.start()

    def take(row, rows):
        over = SMALL[1] // 2
        if row < 80:
            tail = small[160 + row : 160 + row + rows, :over]
        else:
            tail = small[80 + row : 80 + row + rows, over:]
        return jnp.concatenate([small[row : row + rows], tail], axis=1)

    x_proj_o[...] = take(0, rank + 2 * n)
    step_proj_o[...] = take(rank + 2 * n, rank)
    decay_o[...] = take(2 * rank + 2 * n, n)
    rows_o[...] = take(2 * rank + 3 * n, 8)
    for c in copies:
        c.wait()


VMEM = pl.BlockSpec(memory_space=pltpu.VMEM)
ANY = pl.BlockSpec(memory_space=pl.ANY)


def shards(sizes, inputs, norm_gain, w_in, conv_weight, conv_bias, x_proj, step_proj, step_bias, decay_code, decay_log,
           skip_gain, w_out, cotangent):
    seqs, tokens, width = inputs.shape
    assert seqs == 1 and sizes["batch"] == 4 and sizes["seq"] % 2 == 0
    inner = w_in.shape[1] // 2
    rank, n, taps = step_proj.shape[0], decay_log.shape[1], conv_weight.shape[0]
    sh = scratch(sizes, tokens, width, inner, n, rank, taps)
    tall = lambda u: u.reshape(-1, LANES)
    args = dict(
        x=inputs[0], g=cotangent[0], gain=tall(norm_gain), conv_w=conv_weight, conv_b=tall(conv_bias), x_proj=x_proj.T,
        step_proj=step_proj, step_b=tall(step_bias), code=tall(decay_code), a2=decay_log.T, skip=tall(skip_gain), w_out=w_out)
    held = [pltpu.VMEM(v, f32) for v in ((tokens, width), (tokens, width), (width, 2 * inner), (inner, width), SMALL)]
    sums = pl.pallas_call(
        functools.partial(block_kernel, sizes, list(sh)),
        in_specs=[ANY] * len(ARGS),
        out_specs=[VMEM] * 5,
        out_shape=held,
        scratch_shapes=list(sh.values()),
        compiler_params=pltpu.CompilerParams(collective_id=1, has_side_effects=True, vmem_limit_bytes=VLIMIT << 19),
        name="block",
    )(*(args[a] for a in FETCH), w_in)
    wanted = [v.shape for v in sums[:4]] + [(rank + 2 * n, inner), (rank, inner), (n, inner), (8, inner)]
    block_out, input_grad, in_sum, out_sum, x_proj_sum, step_proj_sum, decay_sum, rows = pl.pallas_call(
        functools.partial(unpack_kernel, rank, n),
        in_specs=[VMEM] * 5,
        out_specs=[ANY] * 4 + [VMEM] * 4,
        out_shape=[jax.ShapeDtypeStruct(v, f32) for v in wanted],
        scratch_shapes=[pltpu.SemaphoreType.DMA((14,))],
        compiler_params=pltpu.CompilerParams(vmem_limit_bytes=VLIMIT2 << 19),
        name="unpack",
    )(*sums)
    return (block_out[None], input_grad[None], rows[7, :width], in_sum, rows[:taps], rows[taps], x_proj_sum.T, step_proj_sum,
            rows[taps + 1], decay_sum.T, rows[taps + 2], out_sum)


VLIMIT, VLIMIT2 = 97, 16


def solution(mesh):
    rows = P("batch", "seq", None)
    return jax.shard_map(
        functools.partial(shards, dict(mesh.shape)),
        mesh=mesh,
        in_specs=(rows,) + (P(),) * 11 + (rows,),
        out_specs=(rows, rows) + (P(),) * 10,
        check_vma=False,
    )
```

```python
import functools

import jax
import jax.numpy as jnp
from jax import lax
from jax.experimental import pallas as pl
from jax.experimental.pallas import tpu as pltpu
from jax.sharding import PartitionSpec as P

f32 = jnp.float32
bf16 = jnp.bfloat16
MESH = pl.DeviceIdType.MESH
EPSILON = 1e-05
LOG2E = 1.4426950408889634
LN2 = 0.6931471805599453
LANES = 128
SCAN = 512
WBLOCK = 256
SLOTS = 4
SMALL = (256, 1024)
PARTS = {"o0": 2, "o1": 2, "i1": 2, "x0": 2, "x1": 2}
SPREAD = {"i1b": "T2", "o0a": "T3", "o1a": "T3", "x1b": "T3"}
SENDS = 120
ORDER = [
    "gated", "i0", "i1", "o1", "a0", "b0", "o0", "a1", "b1", "o1", "a2", "o1", "i1", "o1b", "o0", "b2",
    "i0", "o1a", "i1", "i1b", "o0", "i1a", "o0a", "pre", "o1b", "mixg", "o0b", "i1b", "i0", "o1a", "i0a", "o0a",
    "xg", "x0", "taps", "o1b", "i1b", "i1a", "ng0", "o1a", "x1", "o0a", "o0b", "x0", "o1b", "i0a", "i1b", "i1a",
    "x0", "x0a", "o1a", "x1", "o1b", "x0b", "o0a", "i1a", "x1", "x0a", "o0b", "x1a", "x0b", "i0a", "x1b", "ng1",
    "x1a", "x0a", "i1b", "o1a", "o0a", "mid", "o0b", "x1b", "x0b", "i1b", "o1b", "i0a", "inp", "s", "i1a", "o1a",
    "o0a", "s", "x1b", "o0b", "x1a", "i0a", "i1a", "x1b", "s", "o0a", "o0a", "o0b", "i1b", "x1a", "i1a", "x0b",
    "x1b", "i0a", "o1b", "s", "x0a", "x1a", "o1a", "o0b", "s", "x0a", "x0b", "o0b", "x1a", "x1b", "x1b", "i1b",
    "o0b", "i0a", "s", "x1a", "x1b", "i1a", "x1a", "i0a", "s", "x0b", "i0a", "x0a", "s", "x0b", "i1b", "o1b",
    "o1b", "x0b", "i0a", "o1a", "x0a", "o0a", "s", "x1b", "o0b", "x1a", "o1b", "o0a", "x0b", "i1a", "x1a", "x0a",
    "bo", "x0a", "x0b", "i1a", "s", "o1a", "x1b", "i1b", "s", "x0a", "o1a",
]


def mult(value, by):
    return value if isinstance(value, int) else pl.multiple_of(value, by)


def split(value):
    high = value.astype(bf16)
    return high, (value - high.astype(f32)).astype(bf16)


def dot(a, b, dims):
    return lax.dot_general(a, b, (dims, ((), ())), preferred_element_type=f32)


def matmul(a, b, dims=((1,), (0,))):
    (ah, al), (bh, bl) = split(a), split(b)
    return dot(ah, bh, dims) + dot(al, bh, dims) + dot(ah, bl, dims)


def stacked(value):
    return jnp.concatenate(split(value), axis=0)


def rows_matmul(both, b, dims):
    rows = both.shape[0] // 2
    bh, bl = split(b)
    wide = dot(both, bh, dims)
    return wide[:rows] + wide[rows:] + dot(both[:rows], bl, dims)


def sigmoid(v):
    return 1.0 / (1.0 + jnp.exp(-v))


def loop(count, body):
    def step(i, _):
        body(i)
        return 0

    lax.fori_loop(0, count, step, 0)


class Place:
    def __init__(self, sizes):
        self.sizes = sizes
        self.s, self.b = lax.axis_index("seq"), lax.axis_index("batch")
        self.at = {"seq": self.s, "batch": self.b}
        self.x, self.c, self.y = self.s % 2, self.b % 2, self.b // 2
        self.odd = self.c

    def near(self, dx, dy, dc):
        dx, dy = dx * (1 - 2 * self.x), dy * (1 - 2 * self.y)
        return (self.s + dx, self.b + dc * (1 - 2 * self.c) + 2 * dy), (self.x + dx, self.y + dy)

    def bit(self, d):
        return self.at[d[0]] // (1 << d[1]) % 2

    def stage(self, pair):
        to = dict(self.at)
        first, second = pair
        if first == second:
            v = self.bit(first)
            to[first[0]] = to[first[0]] + (1 - 2 * v) * (1 << first[1])
        else:
            va, vb = self.bit(first), self.bit(second)
            to[first[0]] = to[first[0]] + (1 - self.odd) * (1 - 2 * va) * (1 << first[1])
            to[second[0]] = to[second[0]] + self.odd * (1 - 2 * vb) * (1 << second[1])
            v = (1 - self.odd) * va + self.odd * vb
        return (to["seq"], to["batch"]), v


class Links:
    def __init__(self, send, recv):
        self.send, self.recv, self.used, self.made, self.free, self.open = send, recv, 0, 0, [], []

    def copy(self, src, dst, to, start=True):
        i = self.used
        self.used += 1
        if self.free:
            k = self.free.pop()
        else:
            k = self.made
            self.made += 1
        assert self.used <= self.recv.shape[0] and self.made <= self.send.shape[0]
        c = pltpu.make_async_remote_copy(
            src_ref=src, dst_ref=dst, send_sem=self.send.at[k], recv_sem=self.recv.at[i], device_id=to, device_id_type=MESH
        )
        if start:
            c.start()
            self.open.append((c, k))
        return c

    def sent(self, *copies):
        for copy in copies:
            copy.wait_send()
            self.free += [k for c, k in self.open if c is copy]
            self.open = [(c, k) for c, k in self.open if c is not copy]

    def drain(self):
        self.sent(*(c for c, _ in self.open))


GROUP = [(1, 0, 0), (1, 0, 1), (0, 1, 0), (0, 1, 1), (0, 0, 1)]


def log2(size):
    return size.bit_length() - 1


def all_bits(sizes):
    s = [("seq", k) for k in range(log2(sizes["seq"]))]
    b = [("batch", k) for k in range(log2(sizes["batch"]))]
    return s, b


def small_plan(sizes):
    s, b = all_bits(sizes)
    return [(b[0], b[0]), (s[0], b[1]), (b[1], s[0])] + [(q, q) for q in s[1:] + b[2:]]


def halvings(rows, stages):
    out = []
    for _ in range(stages):
        ok = rows % 16 == 0
        out.append(ok)
        rows = rows // 2 if ok else rows
    return out


def landing_rows(rows, stages):
    total = 0
    for ok in halvings(rows, stages):
        rows = rows // 2 if ok else rows
        total += rows
    return total


def reduce_rows(place, links, plan, acc, land, kept):
    rows = acc.shape[0]
    off, base, before = 0, 0, []
    for pair, ok in zip(plan, halvings(rows, len(plan))):
        to, v = place.stage(pair)
        parent = off
        if ok:
            rows //= 2
            off, give = off + v * rows, off + (1 - v) * rows
        else:
            give = off
        copy = links.copy(acc.at[pl.ds(mult(give, 8), rows)], land.at[pl.ds(base, rows)], to)
        yield
        copy.wait_recv()
        links.sent(*before)
        before = [copy]
        if not ok:
            links.sent(copy)
            before = []

        def add(i, off=off, base=base):
            at = pl.ds(mult(off + i * 8, 8), 8)
            acc[at] = acc[at] + land[pl.ds(mult(base + i * 8, 8), 8)]

        loop(rows // 8, add)
        base += rows
        if ok:
            kept.append((to, parent, off, rows))
    links.sent(*before)
    return off, rows


def place_rows(acc, off, rows, whole):
    def one(i):
        whole(off + i * 8, 8)[...] = acc[pl.ds(mult(off + i * 8, 8), 8)]

    loop(rows // 8, one)


def small_chain(place, links, plan, acc, land, out):
    whole = lambda row, rows: out.at[pl.ds(mult(row, 8), rows)]
    kept = []
    off, rows = yield from reduce_rows(place, links, plan, acc, land, kept)
    place_rows(acc, off, rows, whole)
    for to, _, off, rows in reversed(kept):
        copy = links.copy(whole(off, rows), whole(off, rows), to)
        yield
        copy.wait_recv()


def tiled(count):
    return count in (2, 4, 6, 8, 12, 24)


def carry_peers(count, s):
    if tiled(count):
        return [lax.rem(s + i, count) for i in range(1, count)]
    return [s + (1 - 2 * (s // (1 << k) % 2)) * (1 << k) for k in range(log2(count))]


def carry_scratch(count, n, inner):
    v = lambda *shape: pltpu.VMEM(shape, f32)
    if tiled(count):
        w = inner // (count // 2)
        return dict(got=v(count, 2, 8, w), back=v(count, 2, 8, w), got_sum=v(count, 1, w), tile_dec=v(count, 8, w))
    return dict(got=v(2 * log2(count), 2, n, inner), back=v(2, n, inner), tot=v(2, n, inner))


def carry(place, links, m, way):
    return (carry_tiles if tiled(place.sizes["seq"]) else carry_doubling)(place, links, m, way)


def carry_doubling(place, links, m, way):
    bits = log2(place.sizes["seq"])
    m.edges[way] = jnp.zeros_like(m.edges[way])
    m.back[way] = jnp.ones_like(m.back[way])
    m.tot[0] = m.ends[way]
    m.tot[1] = jnp.exp2(m.a2[...] * m.sums[...])
    for k, p in enumerate(carry_peers(place.sizes["seq"], place.s)):
        got = m.got.at[way * bits + k]
        copy = links.copy(m.tot, got, (p, place.b))
        copy.wait_recv()
        links.sent(copy)
        later = place.bit(("seq", k))

        @pl.when(later == 1 - way)
        def _():
            m.edges[way] += m.back[way] * got[0]
            m.back[way] *= got[1]
            m.tot[0] += m.tot[1] * got[0]

        @pl.when(later == way)
        def _():
            m.tot[0] = got[0] + got[1] * m.tot[0]

        m.tot[1] *= got[1]
    yield
    yield


def carry_tiles(place, links, m, way):
    count, s, b = place.sizes["seq"], place.s, place.b
    across = count // 2
    width = m.ends.shape[2] // across
    peers = carry_peers(count, s)

    def cut(ref, p):
        return ref.at[pl.ds(mult(p // across * 8, 8), 8), pl.ds(mult(p % across * width, LANES), width)]

    def cut_sum(p):
        return m.sums.at[:, pl.ds(mult(p % across * width, LANES), width)]

    first = [links.copy(cut(m.ends.at[way], p), m.got.at[s, way], (p, b)) for p in peers]
    m.got[s, way] = cut(m.ends.at[way], s)[...]
    if way == 0:
        first += [links.copy(cut_sum(p), m.got_sum.at[s], (p, b)) for p in peers]
        m.got_sum[s] = cut_sum(s)[...]
    yield
    for c in first:
        c.wait_recv()
    if way == 0:
        a2 = cut(m.a2, s)[...]
        for p in range(count):
            m.tile_dec[p] = jnp.exp2(a2 * m.got_sum[p])
    value = jnp.zeros((8, width), f32)
    for p in reversed(range(count)) if way else range(count):
        m.back[p, way] = value
        value = m.got[p, way] + m.tile_dec[p] * value
    second = [links.copy(m.back.at[p, way], cut(m.edges.at[way], s), (p, b)) for p in peers]
    cut(m.edges.at[way], s)[...] = m.back[s, way]
    links.sent(*first)
    yield
    for c in second:
        c.wait_recv()
    links.sent(*second)


def wide(tile):
    return jnp.concatenate([tile] * (SCAN // LANES), axis=1)


def spread(row, n):
    return jnp.broadcast_to(row, (n, row.shape[1]))


def fold(value):
    return sum(value[:, k : k + LANES] for k in range(0, value.shape[1], LANES))


def scan_ends(m, lanes):
    a2 = m.a2[:, lanes]
    n = a2.shape[0]

    def chunk(i, h):
        at = pl.ds(pl.multiple_of(i * 8, 8), 8)
        s8, u8 = m.step[at, lanes], m.u[at, lanes]
        for j in range(8):
            b = wide(m.bb[pl.ds(pl.multiple_of((i * 8 + j) * n, 8), n)])
            h = jnp.exp2(spread(s8[j : j + 1], n) * a2) * h + spread(u8[j : j + 1], n) * b
        return h

    m.ends[0, :, lanes] = lax.fori_loop(0, m.step.shape[0] // 8, chunk, jnp.zeros_like(a2))


def scan_lams(m, lanes):
    a2 = m.a2[:, lanes]
    n = a2.shape[0]

    def chunk(i, held):
        dec, acc = held
        at = pl.ds(pl.multiple_of(i * 8, 8), 8)
        s8, d8 = m.step[at, lanes], m.d_res[at, lanes]
        for j in range(8):
            c = wide(m.cc[pl.ds(pl.multiple_of((i * 8 + j) * n, 8), n)])
            dec = dec * jnp.exp2(spread(s8[j : j + 1], n) * a2)
            acc = acc + dec * (spread(d8[j : j + 1], n) * c)
        return dec, acc

    zero = jnp.zeros_like(a2)
    m.ends[1, :, lanes] = lax.fori_loop(0, m.step.shape[0] // 8, chunk, (zero + 1.0, zero))[1]


def scan_out(m, lanes):
    a2 = m.a2[:, lanes]
    n = a2.shape[0]

    def chunk(i, h):
        at = pl.ds(pl.multiple_of(i * 8, 8), 8)
        s8, u8 = m.step[at, lanes], m.u[at, lanes]
        ys = []
        for j in range(8):
            t = pl.ds(pl.multiple_of((i * 8 + j) * n, 8), n)
            b, c = wide(m.bb[t]), wide(m.cc[t])
            h = jnp.exp2(spread(s8[j : j + 1], n) * a2) * h + spread(u8[j : j + 1], n) * b
            ys.append(jnp.sum(c * h, axis=0, keepdims=True))
        m.y[at, lanes] = jnp.concatenate(ys, axis=0)
        return h

    lax.fori_loop(0, m.step.shape[0] // 8, chunk, m.edges[0, :, lanes])


def scan_again(m, lanes, first):
    a2 = m.a2[:, lanes]
    n = a2.shape[0]
    tokens = m.step.shape[0]

    def ahead(i, h):
        at = pl.ds(pl.multiple_of(i * 8, 8), 8)
        s8, u8, d8 = m.step[at, lanes], m.u[at, lanes], m.d_res[at, lanes]
        for j in range(8):
            t = pl.ds(pl.multiple_of((i * 8 + j) * n, 8), n)
            m.h[i * 8 + j] = h
            h = jnp.exp2(spread(s8[j : j + 1], n) * a2) * h + spread(u8[j : j + 1], n) * wide(m.bb[t])
            part = fold(spread(d8[j : j + 1], n) * h)
            m.cg[t] = part if first else m.cg[t] + part
        return h

    lax.fori_loop(0, tokens // 8, ahead, m.edges[0, :, lanes])


def scan_back(m, lanes, first):
    a2 = m.a2[:, lanes]
    n = a2.shape[0]
    tokens = m.step.shape[0]

    def behind(i, held):
        q, rate = held
        r = tokens // 8 - 1 - i
        at = pl.ds(pl.multiple_of(r * 8, 8), 8)
        s8, u8, d8 = m.step[at, lanes], m.u[at, lanes], m.d_res[at, lanes]
        sg, lb = [None] * 8, [None] * 8
        for j in reversed(range(8)):
            t = pl.ds(pl.multiple_of((r * 8 + j) * n, 8), n)
            st = spread(s8[j : j + 1], n)
            lam = spread(d8[j : j + 1], n) * wide(m.cc[t]) + q
            q = jnp.exp2(st * a2) * lam
            dec = q * m.h[r * 8 + j]
            lb[j] = jnp.sum(lam * wide(m.bb[t]), axis=0, keepdims=True)
            sg[j] = jnp.sum(dec * a2, axis=0, keepdims=True)
            rate = rate + dec * st
            part = fold(lam * spread(u8[j : j + 1], n))
            m.bg[t] = part if first else m.bg[t] + part
        lb8, sg8 = jnp.concatenate(lb, axis=0), jnp.concatenate(sg, axis=0)
        m.sg[at, lanes] = LN2 * sg8 + m.mixed[at, lanes] * lb8
        m.gate[at, lanes] = s8 * lb8
        return q, rate

    _, rate = lax.fori_loop(0, tokens // 8, behind, (m.edges[1, :, lanes], jnp.zeros_like(a2)))
    m.rate[:, lanes] = rate


class Refs:
    pass


FETCH = ["x", "gain", "g", "w_out", "conv_w", "conv_b", "x_proj", "step_proj", "step_b", "code", "a2", "skip"]
ARGS = [v + "_h" for v in FETCH] + ["w_in"]
OUTS = ["block_out", "input_grad", "in_sum", "out_sum", "small_sum"]


UNITS = ["o0", "o1", "i0", "i1", "x0", "x1"]


def parts(unit):
    return [unit + "ab"[k] for k in range(PARTS.get(unit, 1))]


def recvs(sizes):
    bits, count = log2(sizes["seq"]), sizes["seq"]
    total = 6 + 2 + 3 * len(UNITS) + (5 * (count - 1) if tiled(count) else 2 * bits)
    total += len(small_plan(sizes)) + sum(halvings(SMALL[0], len(small_plan(sizes))))
    for unit in UNITS:
        for p in parts(unit):
            kept = sum(halvings(LANES * 3 // len(parts(unit)), bits)) - 1
            total += bits + 7 + kept + 3 * {"T1": 0, "T2": kept, "T3": kept - 1}[SPREAD.get(p, "T1")]
    return total


def scratch(sizes, tokens, width, inner, n, rank, taps):
    full = (tokens, inner)
    half, part = inner // 2, width // 2
    stages = log2(sizes["seq"])
    v = lambda *shape: pltpu.VMEM(shape, f32)
    sh = {name: v(*full) for name in ("gate", "d_res", "conv", "mixed", "pre", "step", "u", "y", "d_gate", "sg")}
    sh.update(
        x=v(tokens, width), g=v(tokens, width), vec=v(4, inner), gain=v(width // LANES, LANES),
        conv_b=v(inner // LANES, LANES), step_b=v(inner // LANES, LANES), skip=v(inner // LANES, LANES),
        code=pltpu.VMEM((inner // LANES, LANES), jnp.int32), conv_w=v(taps, inner), x_proj=v(rank + 2 * n, inner),
        step_proj=v(rank, inner), a2=v(n, inner), w_out=v(inner, width),
        normed=v(tokens, width), hid=v(8 + tokens, inner), cgr=v(tokens + 8, inner), proj=v(tokens, LANES),
        wbuf=v(SLOTS, width, WBLOCK), acc=v(tokens, width),
        bb=v(tokens * n, LANES), cc=v(tokens * n, LANES), bg=v(tokens * n, LANES), cg=v(tokens * n, LANES),
        h=v(tokens, n, SCAN), rate=v(n, inner), ends=v(2, n, inner), edges=v(2, n, inner), sums=v(1, inner),
        ng=v(4, tokens, part), gg=v(4, tokens, part),
        small=v(*SMALL), small_land=v(landing_rows(SMALL[0], len(small_plan(sizes))), SMALL[1]),
    )
    for unit in UNITS:
        sh["late_" + unit] = v(4, tokens, part)
        for p in parts(unit):
            rows = part // len(parts(unit))
            sh["tile_" + p] = v(rows, part)
            sh["land_" + p] = v(landing_rows(rows, stages), part)
    sh.update(carry_scratch(sizes["seq"], n, inner))
    sh["send"] = pltpu.SemaphoreType.DMA((SENDS,))
    sh["recv"] = pltpu.SemaphoreType.DMA((recvs(sizes),))
    sh["wsem"] = pltpu.SemaphoreType.DMA((SLOTS,))
    sh["isem"] = pltpu.SemaphoreType.DMA((len(FETCH),))
    return sh


def stream(m, first, last):
    def fetch(i, slot):
        cols = pl.ds(mult((first + i) * WBLOCK, WBLOCK), WBLOCK)
        return pltpu.make_async_copy(m.w_in.at[:, cols], m.wbuf.at[slot], m.wsem.at[slot])

    ahead = SLOTS - 1
    for k in range(ahead):
        fetch(k, k).start()

    def run(use):
        def body(i):
            slot = lax.rem(i, SLOTS)
            fetch(i, slot).wait()

            @pl.when(i + ahead < last - first)
            def _():
                fetch(i + ahead, lax.rem(i + ahead, SLOTS)).start()

            use(i, m.wbuf[slot])

        loop(last - first, body)

    return run


def late_chain(place, links, m, unit, value, left, right):
    late = getattr(m, "late_" + unit)
    width = late.shape[2]
    shift = int(unit[1]) * width
    mine = place.y if unit[0] == "o" else place.x
    to, _ = place.near(0, 1, 0) if unit[0] == "o" else place.near(1, 0, 0)
    core, _ = place.near(0, 0, 1)

    def cut(which):
        return value.at[:, pl.ds(mult(which * 2 * width + shift, LANES), width)]

    def pass_on(which):
        slot = late.at[which * 2 + place.c]
        return links.copy(slot, slot, core)

    sent = links.copy(cut(1 - mine), late.at[mine * 2 + place.c], to)
    late[mine * 2 + place.c] = cut(mine)[...]
    passed = [pass_on(mine)]
    yield
    sent.wait_recv()
    passed.append(pass_on(1 - mine))
    yield
    for copy in passed:
        copy.wait_recv()
    links.sent(sent, *passed)
    for i in range(2):
        cell = matmul(left(i), right(i), ((0,), (0,)))
        rows = cell.shape[0] // len(parts(unit))
        for k, p in enumerate(parts(unit)):
            tile = getattr(m, "tile_" + p)
            value = cell[k * rows : (k + 1) * rows]
            tile[...] = value if i == 0 else tile[...] + value


def piece_chain(place, links, m, p, zplan, out, base):
    acc, land = getattr(m, "tile_" + p), getattr(m, "land_" + p)
    rows, cols = acc.shape
    key, shift, r0 = p[0], int(p[1]) * m.x.shape[1] // 2, "ab".index(p[2]) * rows
    part = cols
    half = 2 * part
    bit = ("seq", 0) if key == "o" else ("batch", 1)
    x, y, c = place.x, place.y, place.c
    core, _ = place.near(0, 0, 1)

    def region(at, row, count):
        xx, yy = at
        if key == "o":
            top, side = yy * half + shift + r0 + xx * (rows // 2) + row, c * part
        else:
            top, side = c * part + r0 + yy * (rows // 2) + row, base + xx * half + shift
        return out.at[pl.ds(mult(top, 8), count), pl.ds(mult(side, LANES), cols)]

    kept = []
    off, count = yield from reduce_rows(place, links, [(bit, bit)] + zplan, acc, land, kept)
    edge = kept[0][2]
    place_rows(acc, off, count, lambda row, n: region((x, y), row - edge, n))
    row = off - edge
    held, across = [(x, y)], []

    def give(at, to):
        ref = region(at, row, count)
        return links.copy(ref, ref, to)

    steps = list(reversed(kept[1:]))
    kind = SPREAD.get(p, "T1")
    steps.insert({"T1": len(steps), "T2": 0, "T3": 1}[kind], None)
    for i, step in enumerate(steps):
        last = i == len(steps) - 1
        if step is not None:
            to, parent, _, size = step
            copies = [give(at, to) for at in held]
            yield
            for copy in copies:
                copy.wait_recv()
            links.sent(*copies)
            row, count = parent - edge, 2 * size
            continue
        first, at_a = place.near(1 - c, c, 0)
        second, at_b = place.near(c, 1 - c, 0)
        _, at_d = place.near(1, 1, 0)
        a, b = give((x, y), first), give((x, y), second)
        held = [(x, y), at_a, at_b, at_d]

        def onward(at):
            if last:
                across.append(give(at, core))

        onward((x, y))
        yield
        a.wait_recv()
        d = give(at_a, second)
        onward(at_a)
        yield
        b.wait_recv()
        onward(at_b)
        yield
        d.wait_recv()
        links.sent(a, b)
        onward(at_d)
    if not across:
        across = [give(at, core) for at in held]
    yield
    for copy in across:
        copy.wait_recv()


def block_kernel(sizes, names, *refs):
    m = Refs()
    for name, ref in zip(ARGS + OUTS + names, refs):
        setattr(m, name, ref)
    place = Place(sizes)
    links = Links(m.send, m.recv)
    s, b, c = place.s, place.b, place.c
    count = sizes["seq"]
    tokens, width = m.x.shape
    inner, n = m.a2.shape[1], m.a2.shape[0]
    rank = m.step_proj.shape[0]
    taps = m.conv_w.shape[0]
    half, part = inner // 2, width // 2
    blocks_of_half = inner // WBLOCK
    last = s == count - 1

    fetched = {}
    for i, name in enumerate(FETCH):
        fetched[name] = pltpu.make_async_copy(getattr(m, name + "_h"), getattr(m, name), m.isem.at[i])
    for name in FETCH[:3]:
        fetched[name].start()
    to_hidden = stream(m, 0, blocks_of_half)
    for name in FETCH[3:]:
        fetched[name].start()
    bar = pltpu.get_barrier_semaphore()
    greet = [place.near(*d)[0] for d in GROUP[1:]] + [(p, b) for p in carry_peers(count, s)]
    if not tiled(count):
        greet += [(lax.rem(s + 1, count), b), (lax.rem(s + count - 1, count), b)]
    for to in greet:
        pl.semaphore_signal(bar, inc=1, device_id=to, device_id_type=MESH)

    fetched["x"].wait()
    fetched["gain"].wait()

    def to_row(name, k):
        ref = getattr(m, name)
        for j in range(ref.shape[0]):
            m.vec[k : k + 1, j * LANES : (j + 1) * LANES] = ref[j : j + 1]

    to_row("gain", 3)
    x = m.x[...]
    rms = lax.rsqrt(jnp.mean(x * x, axis=1, keepdims=True) + EPSILON)
    m.normed[...] = x * rms * m.vec[3:4, :width]
    left = stacked(m.normed[...])

    def hidden_block(i, w):
        m.hid[pl.ds(8, tokens), pl.ds(mult(i * WBLOCK, WBLOCK), WBLOCK)] = rows_matmul(left, w, ((1,), (0,)))

    to_hidden(hidden_block)
    to_gate = stream(m, blocks_of_half, 2 * blocks_of_half)
    pl.semaphore_wait(bar, len(greet))
    halo = links.copy(m.hid.at[pl.ds(tokens, 8)], m.hid.at[pl.ds(0, 8)], (lax.rem(s + 1, count), b), start=False)

    @pl.when(jnp.logical_not(last))
    def _():
        halo.start()

    fetched["g"].wait()
    early = []
    for d in GROUP:
        to, _ = place.near(*d)
        cols = pl.ds(mult((c + d[2] * (1 - 2 * c)) * part, LANES), part)
        if not d[1]:
            early.append(links.copy(m.normed.at[:, cols], m.ng.at[place.x * 2 + c], to))
        if not d[0]:
            early.append(links.copy(m.g.at[:, cols], m.gg.at[place.y * 2 + c], to))
    own = pl.ds(mult(c * part, LANES), part)
    m.ng[place.x * 2 + c] = m.normed[:, own]
    m.gg[place.y * 2 + c] = m.g[:, own]


    for name in FETCH[3:]:
        fetched[name].wait()
    m.step_b[...] = m.step_b[...] - 0.5 * m.code[...].astype(f32)
    for k, name in enumerate(("conv_b", "step_b", "skip")):
        to_row(name, k)
    m.a2[...] = -LOG2E * jnp.exp(m.a2[...])
    g_left = stacked(m.g[...])

    def d_gated_block(i):
        cols = pl.ds(mult(i * WBLOCK, WBLOCK), WBLOCK)
        m.d_res[:, cols] = rows_matmul(g_left, m.w_out[cols], ((1,), (1,)))

    loop(blocks_of_half, d_gated_block)

    @pl.when(s > 0)
    def _():
        halo.wait_recv()

    @pl.when(s == 0)
    def _():
        m.hid[pl.ds(0, 8)] = jnp.zeros((8, inner), f32)

    def convolve(i):
        window = m.hid[pl.ds(mult(i * 8, 8), 16)]
        v = m.vec[0:1]
        for k in range(taps):
            o = 8 - taps + 1 + k
            v = v + m.conv_w[k : k + 1] * window[o : o + 8]
        at = pl.ds(mult(i * 8, 8), 8)
        m.conv[at] = v
        m.mixed[at] = v * sigmoid(v)

    loop(tokens // 8, convolve)

    proj = matmul(m.mixed[...], m.x_proj[...], ((1,), (1,)))
    m.proj[:, : proj.shape[1]] = proj
    for j in range(n):
        at = pl.ds(j, tokens, stride=n)
        m.bb[at] = jnp.broadcast_to(proj[:, rank + j : rank + j + 1], (tokens, LANES))
    low_left = stacked(proj[:, :rank])

    def step_block(i):
        cols = pl.ds(mult(i * WBLOCK, WBLOCK), WBLOCK)
        pre = rows_matmul(low_left, m.step_proj[:, cols], ((1,), (0,))) + m.vec[1:2, cols]
        step = jnp.maximum(pre, 0.0) + jnp.log1p(jnp.exp(-jnp.abs(pre)))
        m.pre[:, cols] = pre
        m.step[:, cols] = step
        m.u[:, cols] = step * m.mixed[:, cols]
        m.sums[:, cols] = jnp.sum(step, axis=0, keepdims=True)

    loop(blocks_of_half, step_block)

    blocks = [slice(k, k + SCAN) for k in range(0, inner, SCAN)]
    for lanes in blocks:
        scan_ends(m, lanes)
    ahead = carry(place, links, m, 0)
    next(ahead)
    for j in range(n):
        at = pl.ds(j, tokens, stride=n)
        m.cc[at] = jnp.broadcast_to(m.proj[:, rank + n + j : rank + n + j + 1], (tokens, LANES))

    def gate_block(i, w):
        cols = pl.ds(mult(i * WBLOCK, WBLOCK), WBLOCK)
        z = rows_matmul(left, w, ((1,), (0,)))
        sg = sigmoid(z)
        act = z * sg
        d = m.d_res[:, cols]
        m.gate[:, cols] = act
        m.d_res[:, cols] = d * act
        m.d_gate[:, cols] = d * (sg * (1.0 + z * (1.0 - sg)))

    to_gate(gate_block)
    next(ahead)
    for lanes in blocks:
        scan_lams(m, lanes)
    behind = carry(place, links, m, 1)
    next(behind)
    for _ in ahead:
        pass
    for lanes in blocks:
        scan_out(m, lanes)
    next(behind)

    def gated_rows(i):
        at = pl.ds(mult(i * 8, 8), 8)
        result = m.y[at] + m.vec[2:3] * m.mixed[at]
        m.y[at] = result * m.gate[at]
        m.d_gate[at] = m.d_gate[at] * result

    loop(tokens // 8, gated_rows)

    s_bits, b_bits = all_bits(sizes)
    zplan = [(k, k) for k in s_bits[1:] + b_bits[2:]]
    chains, v = {}, Refs()

    def pair(ref):
        return lambda i: ref[pl.ds(2 * i, 2)].reshape(2 * tokens, ref.shape[2])

    def go(name):
        try:
            next(chains[name])
        except StopIteration:
            del chains[name]
            if name in UNITS:
                where = {"o": (m.out_sum, 0), "i": (m.in_sum, inner), "x": (m.in_sum, 0)}[name[0]]
                for p in parts(name):
                    chains[p] = piece_chain(place, links, m, p, zplan, *where)

    def late(key, value, left, right):
        for unit in (key + "0", key + "1"):
            ref = getattr(m, "late_" + unit)
            chains[unit] = late_chain(place, links, m, unit, value, pair(ref if left is None else left), pair(ref if right is None else right))

    column = lax.broadcasted_iota(jnp.int32, (tokens, LANES), 1)
    zero = jnp.zeros((8, inner), f32)

    def collect(ref, base, total):
        for j in range(n):
            rows = jnp.sum(ref[pl.ds(j, tokens, stride=n)], axis=1, keepdims=True)
            total = total + jnp.where(column == base + j, rows, 0.0)
        return total

    def put_small(row, value):
        rows = value.shape[0]
        cut, top = SMALL[1], 80
        m.small[row : row + rows] = value[:, :cut]
        over = inner - cut
        if row < top:
            m.small[2 * top + row : 2 * top + row + rows, :over] = value[:, cut:]
        else:
            m.small[top + row : top + row + rows, over:] = value[:, cut:]

    def gated():
        late("o", m.y, None, m.gg)
        late("i", m.d_gate, m.ng, None)

    def again(k):
        scan_again(m, blocks[k], k == 0)

    def back(k):
        if k == 0:
            for _ in behind:
                pass
            for e in early:
                e.wait_recv()
            links.sent(*early)
        scan_back(m, blocks[k], k == 0)

    def pre():
        bc_grad = collect(m.cg, rank + n, collect(m.bg, rank, jnp.zeros((tokens, LANES), f32)))

        def rows(i, total):
            at = pl.ds(pl.multiple_of(i * 8, 8), 8)
            p = m.sg[at] * sigmoid(m.pre[at])
            m.sg[at] = p
            return total[0] + p, total[1] + m.d_res[at] * m.mixed[at]

        total = lax.fori_loop(0, tokens // 8, rows, (zero, zero))
        v.bias_grad, v.skip_grad = (jnp.sum(t, axis=0, keepdims=True) for t in total)
        low_grad = matmul(m.sg[...], m.step_proj[...], ((1,), (1,)))
        v.proj_grad = jnp.concatenate([low_grad, bc_grad[:, rank : rank + 2 * n]], axis=1)

    def mixg():
        pg_left = stacked(v.proj_grad)

        def block(i):
            cols = pl.ds(mult(i * WBLOCK, WBLOCK), WBLOCK)
            d = rows_matmul(pg_left, m.x_proj[:, cols], ((1,), (0,)))
            z = m.conv[:, cols]
            sg = sigmoid(z)
            d = d + m.gate[:, cols] + m.d_res[:, cols] * m.vec[2:3, cols]
            m.cgr[pl.ds(0, tokens), cols] = d * (sg * (1.0 + z * (1.0 - sg)))

        loop(blocks_of_half, block)
        v.halo_back = links.copy(
            m.cgr.at[pl.ds(0, 8)], m.cgr.at[pl.ds(tokens, 8)], (lax.rem(s + count - 1, count), b), start=False)

        @pl.when(s > 0)
        def _():
            v.halo_back.start()

    def xg():
        @pl.when(jnp.logical_not(last))
        def _():
            v.halo_back.wait_recv()

        @pl.when(last)
        def _():
            m.cgr[pl.ds(tokens, 8)] = jnp.zeros((8, inner), f32)

        def rows(i):
            window = m.cgr[pl.ds(mult(i * 8, 8), 16)]
            z = m.conv_w[0:1] * window[taps - 1 : taps + 7]
            for k in range(1, taps):
                o = taps - 1 - k
                z = z + m.conv_w[k : k + 1] * window[o : o + 8]
            m.gate[pl.ds(mult(i * 8, 8), 8)] = z

        loop(tokens // 8, rows)
        late("x", m.gate, m.ng, None)

    def taps_():
        def rows(i, total):
            at = pl.ds(pl.multiple_of(i * 8, 8), 8)
            window = m.hid[pl.ds(pl.multiple_of(i * 8, 8), 16)]
            z = m.cgr[at]
            o = 8 - taps + 1
            return tuple(t + z * window[o + k : o + k + 8] for k, t in enumerate(total[:-1])) + (total[-1] + z,)

        total = lax.fori_loop(0, tokens // 8, rows, (zero,) * (taps + 1))
        v.tap_rows = [jnp.sum(t, axis=0, keepdims=True) for t in total]

    def mid():
        put_small(0, matmul(v.proj_grad, m.mixed[...], ((0,), (0,))))
        put_small(rank + 2 * n, matmul(m.proj[:, :rank], m.sg[...], ((0,), (0,))))
        put_small(2 * rank + 2 * n, m.rate[...] * m.a2[...] * LN2)

    def normed_block(ref):
        def use(i, w):
            d = stacked(ref[:, pl.ds(mult(i * WBLOCK, WBLOCK), WBLOCK)])
            m.acc[...] = m.acc[...] + rows_matmul(d, w, ((1,), (1,)))

        return use

    def ng0():
        m.acc[...] = jnp.zeros_like(m.acc)
        stream(m, blocks_of_half, 2 * blocks_of_half)(normed_block(m.d_gate))

    def ng1():
        stream(m, 0, blocks_of_half)(normed_block(m.gate))

    def inp():
        x = m.x[...]
        rms = lax.rsqrt(jnp.mean(x * x, axis=1, keepdims=True) + EPSILON)
        normed_grad = m.acc[...]
        gain_grad = jnp.sum(normed_grad * x * rms, axis=0, keepdims=True)
        weighted = normed_grad * m.vec[3:4, :width]
        m.input_grad[...] = rms * weighted - rms * rms * rms * x * jnp.mean(weighted * x, axis=1, keepdims=True) + m.g[...]
        rows = v.tap_rows + [v.bias_grad, v.skip_grad, jnp.concatenate([gain_grad, jnp.zeros((1, inner - width), f32)], axis=1)]
        put_small(2 * rank + 3 * n, jnp.concatenate(rows, axis=0))
        end = 2 * rank + 3 * n + 8
        m.small[end:160] = jnp.zeros((160 - end, SMALL[1]), f32)
        m.small[240:256] = jnp.zeros((16, SMALL[1]), f32)
        m.small[80 + end : 240, SMALL[1] // 2 :] = jnp.zeros((160 - end, SMALL[1] // 2), f32)
        chains["s"] = small_chain(place, links, small_plan(sizes), m.small, m.small_land, m.small_sum)

    def bo():
        gl = stacked(m.y[...])

        def block(i):
            cols = pl.ds(mult(i * WBLOCK, WBLOCK), WBLOCK)
            m.block_out[:, cols] = m.x[:, cols] + rows_matmul(gl, m.w_out[:, cols], ((1,), (0,)))

        loop(width // WBLOCK, block)

    work = {
        "gated": gated, "a0": lambda: again(0), "b0": lambda: back(0), "a1": lambda: again(1), "b1": lambda: back(1),
        "a2": lambda: again(2), "b2": lambda: back(2), "pre": pre, "mixg": mixg,
        "xg": xg, "taps": taps_, "mid": mid, "ng0": ng0, "ng1": ng1, "inp": inp, "bo": bo,
    }
    for name in ORDER:
        if name in work:
            work.pop(name)()
        elif name in chains:
            go(name)
    assert not work
    while chains:
        for name in list(chains):
            go(name)

    @pl.when(jnp.logical_not(last))
    def _():
        halo.wait_send()

    @pl.when(s > 0)
    def _():
        v.halo_back.wait_send()

    links.drain()


def unpack_kernel(rank, n, a_v, b_v, c_v, d_v, small, a_o, b_o, c_o, d_o, x_proj_o, step_proj_o, decay_o, taps_o, *rest):
    row_os, sems = rest[:-1], rest[-1]
    copies = []
    for v, o, cuts in ((c_v, c_o, 8), (d_v, d_o, 4), (a_v, a_o, 1), (b_v, b_o, 1)):
        rows = v.shape[0] // cuts
        for k in range(cuts):
            at = pl.ds(k * rows, rows)
            copies.append(pltpu.make_async_copy(v.at[at], o.at[at], sems.at[len(copies)]))
    for c in copies:
        c.start()

    def take(row, rows):
        over = SMALL[1] // 2
        if row < 80:
            tail = small[160 + row : 160 + row + rows, :over]
        else:
            tail = small[80 + row : 80 + row + rows, over:]
        return jnp.concatenate([small[row : row + rows], tail], axis=1)

    x_proj_o[...] = take(0, rank + 2 * n)
    step_proj_o[...] = take(rank + 2 * n, rank)
    decay_o[...] = take(2 * rank + 2 * n, n)
    rows = take(2 * rank + 3 * n, 8)
    taps = taps_o.shape[0]
    taps_o[...] = rows[:taps]
    for k, ref in enumerate(row_os):
        for j in range(ref.shape[0]):
            ref[j : j + 1] = rows[taps + k : taps + k + 1, j * LANES : (j + 1) * LANES]
    for c in copies:
        c.wait()


VMEM = pl.BlockSpec(memory_space=pltpu.VMEM)
ANY = pl.BlockSpec(memory_space=pl.ANY)


def shards(sizes, inputs, norm_gain, w_in, conv_weight, conv_bias, x_proj, step_proj, step_bias, decay_code, decay_log,
           skip_gain, w_out, cotangent):
    seqs, tokens, width = inputs.shape
    assert seqs == 1 and sizes["batch"] == 4 and sizes["seq"] % 2 == 0
    inner = w_in.shape[1] // 2
    rank, n, taps = step_proj.shape[0], decay_log.shape[1], conv_weight.shape[0]
    sh = scratch(sizes, tokens, width, inner, n, rank, taps)
    tall = lambda u: u.reshape(-1, LANES)
    args = dict(
        x=inputs[0], g=cotangent[0], gain=tall(norm_gain), conv_w=conv_weight, conv_b=tall(conv_bias), x_proj=x_proj.T,
        step_proj=step_proj, step_b=tall(step_bias), code=tall(decay_code), a2=decay_log.T, skip=tall(skip_gain), w_out=w_out)
    held = [pltpu.VMEM(v, f32) for v in ((tokens, width), (tokens, width), (width, 2 * inner), (inner, width), SMALL)]
    sums = pl.pallas_call(
        functools.partial(block_kernel, sizes, list(sh)),
        in_specs=[ANY] * len(ARGS),
        out_specs=[VMEM] * 5,
        out_shape=held,
        scratch_shapes=list(sh.values()),
        compiler_params=pltpu.CompilerParams(collective_id=1, has_side_effects=True, vmem_limit_bytes=VLIMIT << 19),
        name="block",
    )(*(args[a] for a in FETCH), w_in)
    wanted = [v.shape for v in sums[:4]] + [(rank + 2 * n, inner), (rank, inner), (n, inner), (taps, inner)]
    wanted += [(inner // LANES, LANES)] * 3 + [(width // LANES, LANES)]
    block_out, input_grad, in_sum, out_sum, x_proj_sum, step_proj_sum, decay_sum, taps_sum, *rows = pl.pallas_call(
        functools.partial(unpack_kernel, rank, n),
        in_specs=[VMEM] * 5,
        out_specs=[ANY] * 4 + [VMEM] * 8,
        out_shape=[jax.ShapeDtypeStruct(v, f32) for v in wanted],
        scratch_shapes=[pltpu.SemaphoreType.DMA((14,))],
        compiler_params=pltpu.CompilerParams(vmem_limit_bytes=VLIMIT2 << 19),
        name="unpack",
    )(*sums)
    conv_b_sum, step_b_sum, skip_sum, gain_sum = (v.reshape(-1) for v in rows)
    return (block_out[None], input_grad[None], gain_sum, in_sum, taps_sum, conv_b_sum, x_proj_sum.T, step_proj_sum, step_b_sum,
            decay_sum.T, skip_sum, out_sum)


VLIMIT, VLIMIT2 = 97, 16


def solution(mesh):
    rows = P("batch", "seq", None)
    return jax.shard_map(
        functools.partial(shards, dict(mesh.shape)),
        mesh=mesh,
        in_specs=(rows,) + (P(),) * 11 + (rows,),
        out_specs=(rows, rows) + (P(),) * 10,
        check_vma=False,
    )
```

```python
import functools

import jax
import jax.numpy as jnp
from jax import lax
from jax.experimental import pallas as pl
from jax.experimental.pallas import tpu as pltpu
from jax.sharding import PartitionSpec as P

f32 = jnp.float32
bf16 = jnp.bfloat16
MESH = pl.DeviceIdType.MESH
EPSILON = 1e-05
LOG2E = 1.4426950408889634
LN2 = 0.6931471805599453
LANES = 128
SCAN = 512
WBLOCK = 256
SLOTS = 4
SMALL = (256, 1024)
PARTS = {"o1": 2, "x0": 2, "x1": 2}
SPREAD = {"o0a": "T3", "o1a": "T3", "x0b": "T3"}
SENDS = 64
ORDER = [
    "g0", "i0", "o0", "g1", "a0", "o1", "i1", "b0", "i0", "a1", "o0", "i0", "i0a", "o0", "o0a", "b1",
    "a2", "o1", "b2", "o1", "o1b", "i0a", "pre", "i1", "mixg", "o1a", "o1b", "i0a", "i1", "i1a", "xg", "o0a",
    "x0", "taps", "o1b", "i0a", "mid", "s", "o1a", "x1", "ng0", "x0", "i1a", "s", "o1b", "x0", "x0b", "o1a",
    "i0a", "x0a", "o0a", "x1", "ng1", "o1a", "s", "o1b", "i1a", "x1", "x1b", "bo", "s", "o1a", "x1a", "x0a",
    "o0a", "i0a", "s", "x1b", "inp", "i1a", "o0a", "x0b", "s", "x1b", "x0a", "i1a", "o1b", "o1a", "s", "x1b",
    "x0a", "o1a", "x1a", "o0a", "n", "i0a", "o1a", "x0b", "x0a", "o0a", "i0a", "s", "i1a", "n", "x1a", "x0b",
    "x0b", "o0a", "x1a", "n", "o1b", "s", "x1a", "x1b", "i1a", "x0b", "o1a", "x0a", "x1a", "o1b", "s", "x1b",
    "i1a", "o1b", "o1b", "i0a", "x0b", "x0b", "o0a", "i0a", "x0a", "x1a", "x1b", "i1a", "x0a", "n", "x0a", "x1a",
    "x1b", "x0b", "n", "i1a", "x1a", "x0a", "o1a", "x1b", "s", "o0a", "n", "x1a", "x0b", "x1b",
]


def mult(value, by):
    return value if isinstance(value, int) else pl.multiple_of(value, by)


def split(value):
    high = value.astype(bf16)
    return high, (value - high.astype(f32)).astype(bf16)


def dot(a, b, dims):
    return lax.dot_general(a, b, (dims, ((), ())), preferred_element_type=f32)


def matmul(a, b, dims=((1,), (0,))):
    (ah, al), (bh, bl) = split(a), split(b)
    return dot(ah, bh, dims) + dot(al, bh, dims) + dot(ah, bl, dims)


def stacked(value):
    return jnp.concatenate(split(value), axis=0)


def rows_matmul(both, b, dims):
    rows = both.shape[0] // 2
    bh, bl = split(b)
    wide = dot(both, bh, dims)
    return wide[:rows] + wide[rows:] + dot(both[:rows], bl, dims)


def sigmoid(v):
    return 1.0 / (1.0 + jnp.exp(-v))


def loop(count, body):
    def step(i, _):
        body(i)
        return 0

    lax.fori_loop(0, count, step, 0)


class Place:
    def __init__(self, sizes):
        self.sizes = sizes
        self.s, self.b = lax.axis_index("seq"), lax.axis_index("batch")
        self.at = {"seq": self.s, "batch": self.b}
        self.x, self.c, self.y = self.s % 2, self.b % 2, self.b // 2
        self.odd = self.c

    def near(self, dx, dy, dc):
        dx, dy = dx * (1 - 2 * self.x), dy * (1 - 2 * self.y)
        return (self.s + dx, self.b + dc * (1 - 2 * self.c) + 2 * dy), (self.x + dx, self.y + dy)

    def bit(self, d):
        return self.at[d[0]] // (1 << d[1]) % 2

    def stage(self, pair):
        to = dict(self.at)
        first, second = pair
        if first == second:
            v = self.bit(first)
            to[first[0]] = to[first[0]] + (1 - 2 * v) * (1 << first[1])
        else:
            va, vb = self.bit(first), self.bit(second)
            to[first[0]] = to[first[0]] + (1 - self.odd) * (1 - 2 * va) * (1 << first[1])
            to[second[0]] = to[second[0]] + self.odd * (1 - 2 * vb) * (1 << second[1])
            v = (1 - self.odd) * va + self.odd * vb
        return (to["seq"], to["batch"]), v


class Links:
    def __init__(self, send, recv):
        self.send, self.recv, self.used, self.made, self.free, self.open = send, recv, 0, 0, [], []

    def copy(self, src, dst, to, start=True):
        i = self.used
        self.used += 1
        if self.free:
            k = self.free.pop()
        else:
            k = self.made
            self.made += 1
        assert self.used <= self.recv.shape[0] and self.made <= self.send.shape[0]
        c = pltpu.make_async_remote_copy(
            src_ref=src, dst_ref=dst, send_sem=self.send.at[k], recv_sem=self.recv.at[i], device_id=to, device_id_type=MESH
        )
        if start:
            c.start()
            self.open.append((c, k))
        return c

    def sent(self, *copies):
        for copy in copies:
            copy.wait_send()
            self.free += [k for c, k in self.open if c is copy]
            self.open = [(c, k) for c, k in self.open if c is not copy]

    def drain(self):
        self.sent(*(c for c, _ in self.open))


GROUP = [(1, 0, 0), (1, 0, 1), (0, 1, 0), (0, 1, 1), (0, 0, 1)]


def log2(size):
    return size.bit_length() - 1


def all_bits(sizes):
    s = [("seq", k) for k in range(log2(sizes["seq"]))]
    b = [("batch", k) for k in range(log2(sizes["batch"]))]
    return s, b


def small_plan(sizes):
    s, b = all_bits(sizes)
    return [(b[0], b[0]), (s[0], b[1]), (b[1], s[0])] + [(q, q) for q in s[1:] + b[2:]]


def halvings(rows, stages):
    out = []
    for _ in range(stages):
        ok = rows % 16 == 0
        out.append(ok)
        rows = rows // 2 if ok else rows
    return out


def landing_rows(rows, stages):
    total = 0
    for ok in halvings(rows, stages):
        rows = rows // 2 if ok else rows
        total += rows
    return total


def reduce_rows(place, links, plan, acc, land, kept):
    rows = acc.shape[0]
    off, base, before = 0, 0, []
    for pair, ok in zip(plan, halvings(rows, len(plan))):
        to, v = place.stage(pair)
        parent = off
        if ok:
            rows //= 2
            off, give = off + v * rows, off + (1 - v) * rows
        else:
            give = off
        copy = links.copy(acc.at[pl.ds(mult(give, 8), rows)], land.at[pl.ds(base, rows)], to)
        yield
        copy.wait_recv()
        links.sent(*before)
        before = [copy]
        if not ok:
            links.sent(copy)
            before = []

        def add(i, off=off, base=base):
            at = pl.ds(mult(off + i * 8, 8), 8)
            acc[at] = acc[at] + land[pl.ds(mult(base + i * 8, 8), 8)]

        loop(rows // 8, add)
        base += rows
        if ok:
            kept.append((to, parent, off, rows))
    links.sent(*before)
    return off, rows


def place_rows(acc, off, rows, whole):
    def one(i):
        whole(off + i * 8, 8)[...] = acc[pl.ds(mult(off + i * 8, 8), 8)]

    loop(rows // 8, one)


def small_chain(place, links, plan, acc, land, out):
    whole = lambda row, rows: out.at[pl.ds(mult(row, 8), rows)]
    kept = []
    off, rows = yield from reduce_rows(place, links, plan, acc, land, kept)
    place_rows(acc, off, rows, whole)
    for to, _, off, rows in reversed(kept):
        copy = links.copy(whole(off, rows), whole(off, rows), to)
        yield
        copy.wait_recv()


def tiled(count):
    return count in (2, 4, 6, 8, 12, 24)


def carry_peers(count, s):
    if tiled(count):
        return [lax.rem(s + i, count) for i in range(1, count)]
    return [s + (1 - 2 * (s // (1 << k) % 2)) * (1 << k) for k in range(log2(count))]


def carry_scratch(count, n, inner):
    v = lambda *shape: pltpu.VMEM(shape, f32)
    if tiled(count):
        w = inner // (count // 2)
        return dict(got=v(count, 2, 8, w), back=v(count, 2, 8, w), got_sum=v(count, 1, w), tile_dec=v(count, 8, w))
    return dict(got=v(2 * log2(count), 2, n, inner), back=v(2, n, inner), tot=v(2, n, inner))


def carry(place, links, m, way):
    return (carry_tiles if tiled(place.sizes["seq"]) else carry_doubling)(place, links, m, way)


def carry_doubling(place, links, m, way):
    bits = log2(place.sizes["seq"])
    m.edges[way] = jnp.zeros_like(m.edges[way])
    m.back[way] = jnp.ones_like(m.back[way])
    m.tot[0] = m.ends[way]
    m.tot[1] = jnp.exp2(m.a2[...] * m.sums[...])
    for k, p in enumerate(carry_peers(place.sizes["seq"], place.s)):
        got = m.got.at[way * bits + k]
        copy = links.copy(m.tot, got, (p, place.b))
        copy.wait_recv()
        links.sent(copy)
        later = place.bit(("seq", k))

        @pl.when(later == 1 - way)
        def _():
            m.edges[way] += m.back[way] * got[0]
            m.back[way] *= got[1]
            m.tot[0] += m.tot[1] * got[0]

        @pl.when(later == way)
        def _():
            m.tot[0] = got[0] + got[1] * m.tot[0]

        m.tot[1] *= got[1]
    yield
    yield


def carry_tiles(place, links, m, way):
    count, s, b = place.sizes["seq"], place.s, place.b
    across = count // 2
    width = m.ends.shape[2] // across
    peers = carry_peers(count, s)

    def cut(ref, p):
        return ref.at[pl.ds(mult(p // across * 8, 8), 8), pl.ds(mult(p % across * width, LANES), width)]

    def cut_sum(p):
        return m.sums.at[:, pl.ds(mult(p % across * width, LANES), width)]

    first = [links.copy(cut(m.ends.at[way], p), m.got.at[s, way], (p, b)) for p in peers]
    m.got[s, way] = cut(m.ends.at[way], s)[...]
    if way == 0:
        first += [links.copy(cut_sum(p), m.got_sum.at[s], (p, b)) for p in peers]
        m.got_sum[s] = cut_sum(s)[...]
    yield
    for c in first:
        c.wait_recv()
    if way == 0:
        a2 = cut(m.a2, s)[...]
        for p in range(count):
            m.tile_dec[p] = jnp.exp2(a2 * m.got_sum[p])
    value = jnp.zeros((8, width), f32)
    for p in reversed(range(count)) if way else range(count):
        m.back[p, way] = value
        value = m.got[p, way] + m.tile_dec[p] * value
    second = [links.copy(m.back.at[p, way], cut(m.edges.at[way], s), (p, b)) for p in peers]
    cut(m.edges.at[way], s)[...] = m.back[s, way]
    links.sent(*first)
    yield
    for c in second:
        c.wait_recv()
    links.sent(*second)


def wide(tile, width=SCAN):
    return jnp.concatenate([tile] * (width // LANES), axis=1)


def spread(row, n):
    return jnp.broadcast_to(row, (n, row.shape[1]))


def fold(value):
    return sum(value[:, k : k + LANES] for k in range(0, value.shape[1], LANES))


def scan_ends(m, lanes):
    a2 = m.a2[:, lanes]
    n = a2.shape[0]

    def chunk(i, h):
        at = pl.ds(pl.multiple_of(i * 8, 8), 8)
        s8, u8 = m.step[at, lanes], m.u[at, lanes]
        for j in range(8):
            b = wide(m.bb[pl.ds(pl.multiple_of((i * 8 + j) * n, 8), n)])
            h = jnp.exp2(spread(s8[j : j + 1], n) * a2) * h + spread(u8[j : j + 1], n) * b
        return h

    m.ends[0, :, lanes] = lax.fori_loop(0, m.step.shape[0] // 8, chunk, jnp.zeros_like(a2))


def scan_lams(m, lanes):
    a2 = m.a2[:, lanes]
    n = a2.shape[0]

    def chunk(i, held):
        dec, acc = held
        at = pl.ds(pl.multiple_of(i * 8, 8), 8)
        s8, d8 = m.step[at, lanes], m.d_res[at, lanes]
        for j in range(8):
            c = wide(m.cc[pl.ds(pl.multiple_of((i * 8 + j) * n, 8), n)])
            dec = dec * jnp.exp2(spread(s8[j : j + 1], n) * a2)
            acc = acc + dec * (spread(d8[j : j + 1], n) * c)
        return dec, acc

    zero = jnp.zeros_like(a2)
    m.ends[1, :, lanes] = lax.fori_loop(0, m.step.shape[0] // 8, chunk, (zero + 1.0, zero))[1]


def scan_out(m, lanes):
    a2 = m.a2[:, lanes]
    n = a2.shape[0]

    def chunk(i, h):
        at = pl.ds(pl.multiple_of(i * 8, 8), 8)
        s8, u8 = m.step[at, lanes], m.u[at, lanes]
        ys = []
        for j in range(8):
            t = pl.ds(pl.multiple_of((i * 8 + j) * n, 8), n)
            b, c = wide(m.bb[t], a2.shape[1]), wide(m.cc[t], a2.shape[1])
            h = jnp.exp2(spread(s8[j : j + 1], n) * a2) * h + spread(u8[j : j + 1], n) * b
            ys.append(jnp.sum(c * h, axis=0, keepdims=True))
        m.y[at, lanes] = jnp.concatenate(ys, axis=0)
        return h

    lax.fori_loop(0, m.step.shape[0] // 8, chunk, m.edges[0, :, lanes])


def scan_again(m, lanes, first):
    a2 = m.a2[:, lanes]
    n = a2.shape[0]
    tokens = m.step.shape[0]

    def ahead(i, h):
        at = pl.ds(pl.multiple_of(i * 8, 8), 8)
        s8, u8, d8 = m.step[at, lanes], m.u[at, lanes], m.d_res[at, lanes]
        for j in range(8):
            t = pl.ds(pl.multiple_of((i * 8 + j) * n, 8), n)
            m.h[i * 8 + j] = h
            h = jnp.exp2(spread(s8[j : j + 1], n) * a2) * h + spread(u8[j : j + 1], n) * wide(m.bb[t])
            part = fold(spread(d8[j : j + 1], n) * h)
            m.cg[t] = part if first else m.cg[t] + part
        return h

    lax.fori_loop(0, tokens // 8, ahead, m.edges[0, :, lanes])


def scan_back(m, lanes, first):
    a2 = m.a2[:, lanes]
    n = a2.shape[0]
    tokens = m.step.shape[0]

    def behind(i, held):
        q, rate = held
        r = tokens // 8 - 1 - i
        at = pl.ds(pl.multiple_of(r * 8, 8), 8)
        s8, u8, d8 = m.step[at, lanes], m.u[at, lanes], m.d_res[at, lanes]
        sg, lb = [None] * 8, [None] * 8
        for j in reversed(range(8)):
            t = pl.ds(pl.multiple_of((r * 8 + j) * n, 8), n)
            st = spread(s8[j : j + 1], n)
            lam = spread(d8[j : j + 1], n) * wide(m.cc[t]) + q
            q = jnp.exp2(st * a2) * lam
            dec = q * m.h[r * 8 + j]
            lb[j] = jnp.sum(lam * wide(m.bb[t]), axis=0, keepdims=True)
            sg[j] = jnp.sum(dec * a2, axis=0, keepdims=True)
            rate = rate + dec * st
            part = fold(lam * spread(u8[j : j + 1], n))
            m.bg[t] = part if first else m.bg[t] + part
        lb8, sg8 = jnp.concatenate(lb, axis=0), jnp.concatenate(sg, axis=0)
        m.sg[at, lanes] = LN2 * sg8 + m.mixed[at, lanes] * lb8
        m.gate[at, lanes] = s8 * lb8
        return q, rate

    _, rate = lax.fori_loop(0, tokens // 8, behind, (m.edges[1, :, lanes], jnp.zeros_like(a2)))
    m.rate[:, lanes] = rate


class Refs:
    pass


FETCH = ["x", "gain", "g", "w_out", "conv_w", "conv_b", "x_proj", "step_proj", "step_b", "code", "a2", "skip"]
ARGS = [v + "_h" for v in FETCH] + ["w_in"]
OUTS = ["block_out", "input_grad", "in_sum", "out_sum", "small_sum", "gain_sum"]


UNITS = ["o0", "o1", "i0", "i1", "x0", "x1"]


def parts(unit):
    return [unit + "ab"[k] for k in range(PARTS.get(unit, 1))]


def recvs(sizes):
    bits, count = log2(sizes["seq"]), sizes["seq"]
    total = 6 + 2 + 3 * len(UNITS) + (5 * (count - 1) if tiled(count) else 2 * bits)
    total += 2 * len(small_plan(sizes)) + sum(halvings(SMALL[0], len(small_plan(sizes))))
    for unit in UNITS:
        for p in parts(unit):
            kept = sum(halvings(LANES * 3 // len(parts(unit)), bits)) - 1
            total += bits + 7 + kept + 3 * {"T1": 0, "T2": kept, "T3": kept - 1}[SPREAD.get(p, "T1")]
    return total


def scratch(sizes, tokens, width, inner, n, rank, taps):
    full = (tokens, inner)
    half, part = inner // 2, width // 2
    stages = log2(sizes["seq"])
    v = lambda *shape: pltpu.VMEM(shape, f32)
    sh = {name: v(*full) for name in ("gate", "d_res", "conv", "mixed", "pre", "step", "u", "y", "d_gate", "sg")}
    sh.update(
        x=v(tokens, width), g=v(tokens, width), vec=v(4, inner), gain=v(width // LANES, LANES),
        conv_b=v(inner // LANES, LANES), step_b=v(inner // LANES, LANES), skip=v(inner // LANES, LANES),
        code=pltpu.VMEM((inner // LANES, LANES), jnp.int32), conv_w=v(taps, inner), x_proj=v(rank + 2 * n, inner),
        step_proj=v(rank, inner), a2=v(n, inner), w_out=v(inner, width),
        normed=v(tokens, width), hid=v(8 + tokens, inner), cgr=v(tokens + 8, inner), proj=v(tokens, LANES),
        wbuf=v(SLOTS, width, WBLOCK), acc=v(tokens, width),
        bb=v(tokens * n, LANES), cc=v(tokens * n, LANES), bg=v(tokens * n, LANES), cg=v(tokens * n, LANES),
        h=v(tokens, n, SCAN), rate=v(n, inner), ends=v(2, n, inner), edges=v(2, n, inner), sums=v(1, inner),
        ng=v(4, tokens, part), gg=v(4, tokens, part),
        gains=v(8, LANES), gains_land=v(landing_rows(8, len(small_plan(sizes))), LANES),
        small=v(*SMALL), small_land=v(landing_rows(SMALL[0], len(small_plan(sizes))), SMALL[1]),
    )
    for unit in UNITS:
        sh["late_" + unit] = v(4, tokens, part)
        for p in parts(unit):
            rows = part // len(parts(unit))
            sh["tile_" + p] = v(rows, part)
            sh["land_" + p] = v(landing_rows(rows, stages), part)
    sh.update(carry_scratch(sizes["seq"], n, inner))
    sh["send"] = pltpu.SemaphoreType.DMA((SENDS,))
    sh["recv"] = pltpu.SemaphoreType.DMA((recvs(sizes),))
    sh["wsem"] = pltpu.SemaphoreType.DMA((SLOTS,))
    sh["isem"] = pltpu.SemaphoreType.DMA((len(FETCH),))
    return sh


def stream(m, first, last):
    def fetch(i, slot):
        cols = pl.ds(mult((first + i) * WBLOCK, WBLOCK), WBLOCK)
        return pltpu.make_async_copy(m.w_in.at[:, cols], m.wbuf.at[slot], m.wsem.at[slot])

    ahead = SLOTS - 1
    for k in range(ahead):
        fetch(k, k).start()

    def run(use):
        def body(i):
            slot = lax.rem(i, SLOTS)
            fetch(i, slot).wait()

            @pl.when(i + ahead < last - first)
            def _():
                fetch(i + ahead, lax.rem(i + ahead, SLOTS)).start()

            use(i, m.wbuf[slot])

        loop(last - first, body)

    return run


def late_chain(place, links, m, unit, value, left, right):
    late = getattr(m, "late_" + unit)
    width = late.shape[2]
    shift = int(unit[1]) * width
    mine = place.y if unit[0] == "o" else place.x
    to, _ = place.near(0, 1, 0) if unit[0] == "o" else place.near(1, 0, 0)
    core, _ = place.near(0, 0, 1)

    def cut(which):
        return value.at[:, pl.ds(mult(which * 2 * width + shift, LANES), width)]

    def pass_on(which):
        slot = late.at[which * 2 + place.c]
        return links.copy(slot, slot, core)

    sent = links.copy(cut(1 - mine), late.at[mine * 2 + place.c], to)
    late[mine * 2 + place.c] = cut(mine)[...]
    passed = [pass_on(mine)]
    yield
    sent.wait_recv()
    passed.append(pass_on(1 - mine))
    yield
    for copy in passed:
        copy.wait_recv()
    links.sent(sent, *passed)
    for i in range(2):
        cell = matmul(left(i), right(i), ((0,), (0,)))
        rows = cell.shape[0] // len(parts(unit))
        for k, p in enumerate(parts(unit)):
            tile = getattr(m, "tile_" + p)
            value = cell[k * rows : (k + 1) * rows]
            tile[...] = value if i == 0 else tile[...] + value


def piece_chain(place, links, m, p, zplan, out, base):
    acc, land = getattr(m, "tile_" + p), getattr(m, "land_" + p)
    rows, cols = acc.shape
    key, shift, r0 = p[0], int(p[1]) * m.x.shape[1] // 2, "ab".index(p[2]) * rows
    part = cols
    half = 2 * part
    bit = ("seq", 0) if key == "o" else ("batch", 1)
    x, y, c = place.x, place.y, place.c
    core, _ = place.near(0, 0, 1)

    def region(at, row, count):
        xx, yy = at
        if key == "o":
            top, side = yy * half + shift + r0 + xx * (rows // 2) + row, c * part
        else:
            top, side = c * part + r0 + yy * (rows // 2) + row, base + xx * half + shift
        return out.at[pl.ds(mult(top, 8), count), pl.ds(mult(side, LANES), cols)]

    kept = []
    off, count = yield from reduce_rows(place, links, [(bit, bit)] + zplan, acc, land, kept)
    edge = kept[0][2]
    place_rows(acc, off, count, lambda row, n: region((x, y), row - edge, n))
    row = off - edge
    held, across = [(x, y)], []

    def give(at, to):
        ref = region(at, row, count)
        return links.copy(ref, ref, to)

    steps = list(reversed(kept[1:]))
    kind = SPREAD.get(p, "T1")
    steps.insert({"T1": len(steps), "T2": 0, "T3": 1}[kind], None)
    for i, step in enumerate(steps):
        last = i == len(steps) - 1
        if step is not None:
            to, parent, _, size = step
            copies = [give(at, to) for at in held]
            yield
            for copy in copies:
                copy.wait_recv()
            links.sent(*copies)
            row, count = parent - edge, 2 * size
            continue
        first, at_a = place.near(1 - c, c, 0)
        second, at_b = place.near(c, 1 - c, 0)
        _, at_d = place.near(1, 1, 0)
        a, b = give((x, y), first), give((x, y), second)
        held = [(x, y), at_a, at_b, at_d]

        def onward(at):
            if last:
                across.append(give(at, core))

        onward((x, y))
        yield
        a.wait_recv()
        d = give(at_a, second)
        onward(at_a)
        yield
        b.wait_recv()
        onward(at_b)
        yield
        d.wait_recv()
        links.sent(a, b)
        onward(at_d)
    if not across:
        across = [give(at, core) for at in held]
    yield
    for copy in across:
        copy.wait_recv()


def block_kernel(sizes, names, *refs):
    m = Refs()
    for name, ref in zip(ARGS + OUTS + names, refs):
        setattr(m, name, ref)
    place = Place(sizes)
    links = Links(m.send, m.recv)
    s, b, c = place.s, place.b, place.c
    count = sizes["seq"]
    tokens, width = m.x.shape
    inner, n = m.a2.shape[1], m.a2.shape[0]
    rank = m.step_proj.shape[0]
    taps = m.conv_w.shape[0]
    half, part = inner // 2, width // 2
    blocks_of_half = inner // WBLOCK
    last = s == count - 1

    fetched = {}
    for i, name in enumerate(FETCH):
        fetched[name] = pltpu.make_async_copy(getattr(m, name + "_h"), getattr(m, name), m.isem.at[i])
    for name in FETCH[:3]:
        fetched[name].start()
    to_hidden = stream(m, 0, blocks_of_half)
    for name in FETCH[3:]:
        fetched[name].start()
    bar = pltpu.get_barrier_semaphore()
    greet = [place.near(*d)[0] for d in GROUP[1:]] + [(p, b) for p in carry_peers(count, s)]
    if not tiled(count):
        greet += [(lax.rem(s + 1, count), b), (lax.rem(s + count - 1, count), b)]
    for to in greet:
        pl.semaphore_signal(bar, inc=1, device_id=to, device_id_type=MESH)

    fetched["x"].wait()
    fetched["gain"].wait()

    def to_row(name, k):
        ref = getattr(m, name)
        for j in range(ref.shape[0]):
            m.vec[k : k + 1, j * LANES : (j + 1) * LANES] = ref[j : j + 1]

    to_row("gain", 3)
    x = m.x[...]
    rms = lax.rsqrt(jnp.mean(x * x, axis=1, keepdims=True) + EPSILON)
    m.normed[...] = x * rms * m.vec[3:4, :width]
    left = stacked(m.normed[...])

    def hidden_block(i, w):
        m.hid[pl.ds(8, tokens), pl.ds(mult(i * WBLOCK, WBLOCK), WBLOCK)] = rows_matmul(left, w, ((1,), (0,)))

    to_hidden(hidden_block)
    to_gate = stream(m, blocks_of_half, 2 * blocks_of_half)
    pl.semaphore_wait(bar, len(greet))
    halo = links.copy(m.hid.at[pl.ds(tokens, 8)], m.hid.at[pl.ds(0, 8)], (lax.rem(s + 1, count), b), start=False)

    @pl.when(jnp.logical_not(last))
    def _():
        halo.start()

    fetched["g"].wait()
    early = []
    for d in GROUP:
        to, _ = place.near(*d)
        cols = pl.ds(mult((c + d[2] * (1 - 2 * c)) * part, LANES), part)
        if not d[1]:
            early.append(links.copy(m.normed.at[:, cols], m.ng.at[place.x * 2 + c], to))
        if not d[0]:
            early.append(links.copy(m.g.at[:, cols], m.gg.at[place.y * 2 + c], to))
    own = pl.ds(mult(c * part, LANES), part)
    m.ng[place.x * 2 + c] = m.normed[:, own]
    m.gg[place.y * 2 + c] = m.g[:, own]


    for name in FETCH[3:]:
        fetched[name].wait()
    m.step_b[...] = m.step_b[...] - 0.5 * m.code[...].astype(f32)
    for k, name in enumerate(("conv_b", "step_b", "skip")):
        to_row(name, k)
    m.a2[...] = -LOG2E * jnp.exp(m.a2[...])
    def convolve(i):
        window = m.hid[pl.ds(mult(i * 8, 8), 16)]
        v = m.vec[0:1]
        for k in range(taps):
            o = 8 - taps + 1 + k
            v = v + m.conv_w[k : k + 1] * window[o : o + 8]
        at = pl.ds(mult(i * 8, 8), 8)
        m.conv[at] = v
        m.mixed[at] = v * sigmoid(v)

    loop(tokens // 8 - 1, lambda i: convolve(i + 1))

    @pl.when(s > 0)
    def _():
        halo.wait_recv()

    @pl.when(s == 0)
    def _():
        m.hid[pl.ds(0, 8)] = jnp.zeros((8, inner), f32)

    convolve(0)

    proj = matmul(m.mixed[...], m.x_proj[...], ((1,), (1,)))
    m.proj[:, : proj.shape[1]] = proj
    for j in range(n):
        at = pl.ds(j, tokens, stride=n)
        m.bb[at] = jnp.broadcast_to(proj[:, rank + j : rank + j + 1], (tokens, LANES))
    low_left = stacked(proj[:, :rank])

    def step_block(i):
        cols = pl.ds(mult(i * WBLOCK, WBLOCK), WBLOCK)
        pre = rows_matmul(low_left, m.step_proj[:, cols], ((1,), (0,))) + m.vec[1:2, cols]
        step = jnp.maximum(pre, 0.0) + jnp.log1p(jnp.exp(-jnp.abs(pre)))
        m.pre[:, cols] = pre
        m.step[:, cols] = step
        m.u[:, cols] = step * m.mixed[:, cols]
        m.sums[:, cols] = jnp.sum(step, axis=0, keepdims=True)

    loop(blocks_of_half, step_block)

    blocks = [slice(k, k + SCAN) for k in range(0, inner, SCAN)]
    for lanes in blocks:
        scan_ends(m, lanes)
    ahead = carry(place, links, m, 0)
    next(ahead)
    g_left = stacked(m.g[...])

    def d_gated_block(i):
        cols = pl.ds(mult(i * WBLOCK, WBLOCK), WBLOCK)
        m.d_res[:, cols] = rows_matmul(g_left, m.w_out[cols], ((1,), (1,)))

    loop(blocks_of_half, d_gated_block)
    for j in range(n):
        at = pl.ds(j, tokens, stride=n)
        m.cc[at] = jnp.broadcast_to(m.proj[:, rank + n + j : rank + n + j + 1], (tokens, LANES))

    def gate_block(i, w):
        cols = pl.ds(mult(i * WBLOCK, WBLOCK), WBLOCK)
        z = rows_matmul(left, w, ((1,), (0,)))
        sg = sigmoid(z)
        act = z * sg
        d = m.d_res[:, cols]
        m.gate[:, cols] = act
        m.d_res[:, cols] = d * act
        m.d_gate[:, cols] = d * (sg * (1.0 + z * (1.0 - sg)))

    to_gate(gate_block)
    next(ahead)
    for lanes in blocks:
        scan_lams(m, lanes)
    behind = carry(place, links, m, 1)
    next(behind)
    for _ in ahead:
        pass
    def finish_quarters(k):
        for first in (k * part, half + k * part):
            cols = slice(first, first + part)
            scan_out(m, cols)

            def rows(i):
                at = pl.ds(mult(i * 8, 8), 8)
                result = m.y[at, cols] + m.vec[2:3, cols] * m.mixed[at, cols]
                m.y[at, cols] = result * m.gate[at, cols]
                m.d_gate[at, cols] = m.d_gate[at, cols] * result

            loop(tokens // 8, rows)

    s_bits, b_bits = all_bits(sizes)
    zplan = [(k, k) for k in s_bits[1:] + b_bits[2:]]
    chains, v = {}, Refs()

    def pair(ref):
        return lambda i: ref[pl.ds(2 * i, 2)].reshape(2 * tokens, ref.shape[2])

    def go(name):
        try:
            next(chains[name])
        except StopIteration:
            del chains[name]
            if name in UNITS:
                where = {"o": (m.out_sum, 0), "i": (m.in_sum, inner), "x": (m.in_sum, 0)}[name[0]]
                for p in parts(name):
                    chains[p] = piece_chain(place, links, m, p, zplan, *where)

    def late(key, value, left, right, which=(0, 1)):
        for unit in (key + str(k) for k in which):
            ref = getattr(m, "late_" + unit)
            chains[unit] = late_chain(place, links, m, unit, value, pair(ref if left is None else left), pair(ref if right is None else right))

    column = lax.broadcasted_iota(jnp.int32, (tokens, LANES), 1)
    zero = jnp.zeros((8, inner), f32)

    def collect(ref, base, total):
        for j in range(n):
            rows = jnp.sum(ref[pl.ds(j, tokens, stride=n)], axis=1, keepdims=True)
            total = total + jnp.where(column == base + j, rows, 0.0)
        return total

    def put_small(row, value):
        rows = value.shape[0]
        cut, top = SMALL[1], 80
        m.small[row : row + rows] = value[:, :cut]
        over = inner - cut
        if row < top:
            m.small[2 * top + row : 2 * top + row + rows, :over] = value[:, cut:]
        else:
            m.small[top + row : top + row + rows, over:] = value[:, cut:]

    def quarters(k):
        finish_quarters(k)
        late("o", m.y, None, m.gg, (k,))
        late("i", m.d_gate, m.ng, None, (k,))
        if k == 0:
            next(behind)

    def again(k):
        scan_again(m, blocks[k], k == 0)

    def back(k):
        if k == 0:
            for _ in behind:
                pass
            for e in early:
                e.wait_recv()
            links.sent(*early)
        scan_back(m, blocks[k], k == 0)

    def pre():
        bc_grad = collect(m.cg, rank + n, collect(m.bg, rank, jnp.zeros((tokens, LANES), f32)))

        def rows(i, total):
            at = pl.ds(pl.multiple_of(i * 8, 8), 8)
            p = m.sg[at] * sigmoid(m.pre[at])
            m.sg[at] = p
            return total[0] + p, total[1] + m.d_res[at] * m.mixed[at]

        total = lax.fori_loop(0, tokens // 8, rows, (zero, zero))
        v.bias_grad, v.skip_grad = (jnp.sum(t, axis=0, keepdims=True) for t in total)
        low_grad = matmul(m.sg[...], m.step_proj[...], ((1,), (1,)))
        v.proj_grad = jnp.concatenate([low_grad, bc_grad[:, rank : rank + 2 * n]], axis=1)

    def mixg():
        pg_left = stacked(v.proj_grad)

        def block(i):
            cols = pl.ds(mult(i * WBLOCK, WBLOCK), WBLOCK)
            d = rows_matmul(pg_left, m.x_proj[:, cols], ((1,), (0,)))
            z = m.conv[:, cols]
            sg = sigmoid(z)
            d = d + m.gate[:, cols] + m.d_res[:, cols] * m.vec[2:3, cols]
            m.cgr[pl.ds(0, tokens), cols] = d * (sg * (1.0 + z * (1.0 - sg)))

        loop(blocks_of_half, block)
        v.halo_back = links.copy(
            m.cgr.at[pl.ds(0, 8)], m.cgr.at[pl.ds(tokens, 8)], (lax.rem(s + count - 1, count), b), start=False)

        @pl.when(s > 0)
        def _():
            v.halo_back.start()

    def xg():
        @pl.when(jnp.logical_not(last))
        def _():
            v.halo_back.wait_recv()

        @pl.when(last)
        def _():
            m.cgr[pl.ds(tokens, 8)] = jnp.zeros((8, inner), f32)

        def rows(i):
            window = m.cgr[pl.ds(mult(i * 8, 8), 16)]
            z = m.conv_w[0:1] * window[taps - 1 : taps + 7]
            for k in range(1, taps):
                o = taps - 1 - k
                z = z + m.conv_w[k : k + 1] * window[o : o + 8]
            m.gate[pl.ds(mult(i * 8, 8), 8)] = z

        loop(tokens // 8, rows)
        late("x", m.gate, m.ng, None)

    def taps_():
        def rows(i, total):
            at = pl.ds(pl.multiple_of(i * 8, 8), 8)
            window = m.hid[pl.ds(pl.multiple_of(i * 8, 8), 16)]
            z = m.cgr[at]
            o = 8 - taps + 1
            return tuple(t + z * window[o + k : o + k + 8] for k, t in enumerate(total[:-1])) + (total[-1] + z,)

        total = lax.fori_loop(0, tokens // 8, rows, (zero,) * (taps + 1))
        v.tap_rows = [jnp.sum(t, axis=0, keepdims=True) for t in total]

    def mid():
        put_small(0, matmul(v.proj_grad, m.mixed[...], ((0,), (0,))))
        put_small(rank + 2 * n, matmul(m.proj[:, :rank], m.sg[...], ((0,), (0,))))
        put_small(2 * rank + 2 * n, m.rate[...] * m.a2[...] * LN2)
        rows = v.tap_rows + [v.bias_grad, v.skip_grad, zero[:1]]
        put_small(2 * rank + 3 * n, jnp.concatenate(rows, axis=0))
        end = 2 * rank + 3 * n + 8
        m.small[end:160] = jnp.zeros((160 - end, SMALL[1]), f32)
        m.small[240:256] = jnp.zeros((16, SMALL[1]), f32)
        m.small[80 + end : 240, SMALL[1] // 2 :] = jnp.zeros((160 - end, SMALL[1] // 2), f32)
        chains["s"] = small_chain(place, links, small_plan(sizes), m.small, m.small_land, m.small_sum)

    def normed_block(ref):
        def use(i, w):
            d = stacked(ref[:, pl.ds(mult(i * WBLOCK, WBLOCK), WBLOCK)])
            m.acc[...] = m.acc[...] + rows_matmul(d, w, ((1,), (1,)))

        return use

    def ng0():
        m.acc[...] = jnp.zeros_like(m.acc)
        stream(m, blocks_of_half, 2 * blocks_of_half)(normed_block(m.d_gate))

    def ng1():
        stream(m, 0, blocks_of_half)(normed_block(m.gate))

    def inp():
        x = m.x[...]
        rms = lax.rsqrt(jnp.mean(x * x, axis=1, keepdims=True) + EPSILON)
        normed_grad = m.acc[...]
        gain_grad = jnp.sum(normed_grad * x * rms, axis=0, keepdims=True)
        weighted = normed_grad * m.vec[3:4, :width]
        m.input_grad[...] = rms * weighted - rms * rms * rms * x * jnp.mean(weighted * x, axis=1, keepdims=True) + m.g[...]
        for k in range(width // LANES):
            m.gains[k : k + 1] = gain_grad[:, k * LANES : (k + 1) * LANES]
        m.gains[width // LANES :] = jnp.zeros((8 - width // LANES, LANES), f32)
        chains["n"] = small_chain(place, links, small_plan(sizes), m.gains, m.gains_land, m.gain_sum)

    def bo():
        gl = stacked(m.y[...])

        def block(i):
            cols = pl.ds(mult(i * WBLOCK, WBLOCK), WBLOCK)
            m.block_out[:, cols] = m.x[:, cols] + rows_matmul(gl, m.w_out[:, cols], ((1,), (0,)))

        loop(width // WBLOCK, block)

    work = {
        "g0": lambda: quarters(0), "g1": lambda: quarters(1), "a0": lambda: again(0), "b0": lambda: back(0), "a1": lambda: again(1), "b1": lambda: back(1),
        "a2": lambda: again(2), "b2": lambda: back(2), "pre": pre, "mixg": mixg,
        "xg": xg, "taps": taps_, "mid": mid, "ng0": ng0, "ng1": ng1, "inp": inp, "bo": bo,
    }
    for name in ORDER:
        if name in work:
            work.pop(name)()
        elif name in chains:
            go(name)
    assert not work
    while chains:
        for name in list(chains):
            go(name)

    @pl.when(jnp.logical_not(last))
    def _():
        halo.wait_send()

    @pl.when(s > 0)
    def _():
        v.halo_back.wait_send()

    links.drain()


def unpack_kernel(rank, n, a_v, b_v, c_v, d_v, small, gains, a_o, b_o, c_o, d_o, x_proj_o, step_proj_o, decay_o, taps_o, *rest):
    row_os, sems = rest[:-1], rest[-1]
    copies = []
    for v, o, cuts in ((c_v, c_o, 8), (d_v, d_o, 4), (a_v, a_o, 1), (b_v, b_o, 1)):
        rows = v.shape[0] // cuts
        for k in range(cuts):
            at = pl.ds(k * rows, rows)
            copies.append(pltpu.make_async_copy(v.at[at], o.at[at], sems.at[len(copies)]))
    for c in copies:
        c.start()

    def take(row, rows):
        over = SMALL[1] // 2
        if row < 80:
            tail = small[160 + row : 160 + row + rows, :over]
        else:
            tail = small[80 + row : 80 + row + rows, over:]
        return jnp.concatenate([small[row : row + rows], tail], axis=1)

    x_proj_o[...] = take(0, rank + 2 * n)
    step_proj_o[...] = take(rank + 2 * n, rank)
    decay_o[...] = take(2 * rank + 2 * n, n)
    rows = take(2 * rank + 3 * n, 8)
    taps = taps_o.shape[0]
    taps_o[...] = rows[:taps]
    row_os[3][...] = gains[: row_os[3].shape[0]]
    for k, ref in enumerate(row_os[:3]):
        for j in range(ref.shape[0]):
            ref[j : j + 1] = rows[taps + k : taps + k + 1, j * LANES : (j + 1) * LANES]
    for c in copies:
        c.wait()


VMEM = pl.BlockSpec(memory_space=pltpu.VMEM)
ANY = pl.BlockSpec(memory_space=pl.ANY)


def shards(sizes, inputs, norm_gain, w_in, conv_weight, conv_bias, x_proj, step_proj, step_bias, decay_code, decay_log,
           skip_gain, w_out, cotangent):
    seqs, tokens, width = inputs.shape
    assert seqs == 1 and sizes["batch"] == 4 and sizes["seq"] % 2 == 0
    inner = w_in.shape[1] // 2
    rank, n, taps = step_proj.shape[0], decay_log.shape[1], conv_weight.shape[0]
    sh = scratch(sizes, tokens, width, inner, n, rank, taps)
    tall = lambda u: u.reshape(-1, LANES)
    args = dict(
        x=inputs[0], g=cotangent[0], gain=tall(norm_gain), conv_w=conv_weight, conv_b=tall(conv_bias), x_proj=x_proj.T,
        step_proj=step_proj, step_b=tall(step_bias), code=tall(decay_code), a2=decay_log.T, skip=tall(skip_gain), w_out=w_out)
    held = [pltpu.VMEM(v, f32) for v in ((tokens, width), (tokens, width), (width, 2 * inner), (inner, width), SMALL, (8, LANES))]
    sums = pl.pallas_call(
        functools.partial(block_kernel, sizes, list(sh)),
        in_specs=[ANY] * len(ARGS),
        out_specs=[VMEM] * 6,
        out_shape=held,
        scratch_shapes=list(sh.values()),
        compiler_params=pltpu.CompilerParams(collective_id=1, has_side_effects=True, vmem_limit_bytes=VLIMIT << 19),
        name="block",
    )(*(args[a] for a in FETCH), w_in)
    wanted = [v.shape for v in sums[:4]] + [(rank + 2 * n, inner), (rank, inner), (n, inner), (taps, inner)]
    wanted += [(inner // LANES, LANES)] * 3 + [(width // LANES, LANES)]
    block_out, input_grad, in_sum, out_sum, x_proj_sum, step_proj_sum, decay_sum, taps_sum, *rows = pl.pallas_call(
        functools.partial(unpack_kernel, rank, n),
        in_specs=[VMEM] * 6,
        out_specs=[ANY] * 4 + [VMEM] * 8,
        out_shape=[jax.ShapeDtypeStruct(v, f32) for v in wanted],
        scratch_shapes=[pltpu.SemaphoreType.DMA((14,))],
        compiler_params=pltpu.CompilerParams(vmem_limit_bytes=VLIMIT2 << 19),
        name="unpack",
    )(*sums)
    conv_b_sum, step_b_sum, skip_sum, gain_sum = (v.reshape(-1) for v in rows)
    return (block_out[None], input_grad[None], gain_sum, in_sum, taps_sum, conv_b_sum, x_proj_sum.T, step_proj_sum, step_b_sum,
            decay_sum.T, skip_sum, out_sum)


VLIMIT, VLIMIT2 = 97, 16


def solution(mesh):
    rows = P("batch", "seq", None)
    return jax.shard_map(
        functools.partial(shards, dict(mesh.shape)),
        mesh=mesh,
        in_specs=(rows,) + (P(),) * 11 + (rows,),
        out_specs=(rows, rows) + (P(),) * 10,
        check_vma=False,
    )
```

```python
import functools

import jax
import jax.numpy as jnp
from jax import lax
from jax.experimental import pallas as pl
from jax.experimental.pallas import tpu as pltpu
from jax.sharding import PartitionSpec as P

f32 = jnp.float32
bf16 = jnp.bfloat16
MESH = pl.DeviceIdType.MESH
EPSILON = 1e-05
LOG2E = 1.4426950408889634
LN2 = 0.6931471805599453
LANES = 128
SCAN = 512
WBLOCK = 256
SLOTS = 4
SMALL = (256, 1024)
PARTS = {"o1": 2, "x0": 2, "x1": 2}
SPREAD = {"i1a": "T3", "o1b": "T3", "x1a": "T3"}
SENDS = 64
ORDER = [
    "g0", "o0", "i0", "g1", "o1", "a0", "i1", "b0", "i0", "a1", "i0", "o0", "i0a", "o1", "b1", "o1",
    "o1a", "i1", "a2", "o1b", "o0", "o0a", "b2", "i0a", "pre", "o1a", "mixg", "i0a", "i1", "i1a", "o1b", "xg",
    "x0", "o1a", "taps", "o0a", "i0a", "mid", "s", "o1b", "x1", "s", "x0", "i1a", "o1a", "x0", "x0a", "o0a",
    "o1a", "x0b", "o1b", "i0a", "x1", "x1", "x1b", "i1a", "ng0", "o0a", "o1b", "o1a", "x0b", "s", "x0a", "ng1",
    "x1b", "x1a", "i1a", "o0a", "x0b", "x0a", "o1b", "i0a", "x1b", "i1a", "o1b", "s", "x0a", "x1a", "x0b", "inp",
    "o0a", "o1a", "s", "o1b", "x0a", "x1b", "o1a", "s", "x0b", "n", "i1a", "o1a", "i0a", "x1a", "i1a", "i1a",
    "o0a", "x1a", "x0b", "x1a", "s", "o0a", "x1b", "x0a", "n", "x1a", "i0a", "x0b", "o0a", "s", "x0b", "x0a",
    "i0a", "x1a", "x0a", "x1a", "o1b", "x1b", "i1a", "n", "x0b", "bo", "s", "x0a", "i1a", "n", "x1b", "x0a",
    "x1b", "x1a", "n", "o1b", "s", "i0a", "x1b", "o1a", "x1a", "o0a", "n", "s", "x0b", "x1b",
]


def mult(value, by):
    return value if isinstance(value, int) else pl.multiple_of(value, by)


def split(value):
    high = value.astype(bf16)
    return high, (value - high.astype(f32)).astype(bf16)


def dot(a, b, dims):
    return lax.dot_general(a, b, (dims, ((), ())), preferred_element_type=f32)


def matmul(a, b, dims=((1,), (0,))):
    (ah, al), (bh, bl) = split(a), split(b)
    return dot(ah, bh, dims) + dot(al, bh, dims) + dot(ah, bl, dims)


def stacked(value):
    return jnp.concatenate(split(value), axis=0)


def rows_matmul(both, b, dims):
    rows = both.shape[0] // 2
    bh, bl = split(b)
    wide = dot(both, bh, dims)
    return wide[:rows] + wide[rows:] + dot(both[:rows], bl, dims)


def sigmoid(v):
    return 1.0 / (1.0 + jnp.exp(-v))


def loop(count, body):
    def step(i, _):
        body(i)
        return 0

    lax.fori_loop(0, count, step, 0)


class Place:
    def __init__(self, sizes):
        self.sizes = sizes
        self.s, self.b = lax.axis_index("seq"), lax.axis_index("batch")
        self.at = {"seq": self.s, "batch": self.b}
        self.x, self.c, self.y = self.s % 2, self.b % 2, self.b // 2
        self.odd = self.c

    def near(self, dx, dy, dc):
        dx, dy = dx * (1 - 2 * self.x), dy * (1 - 2 * self.y)
        return (self.s + dx, self.b + dc * (1 - 2 * self.c) + 2 * dy), (self.x + dx, self.y + dy)

    def bit(self, d):
        return self.at[d[0]] // (1 << d[1]) % 2

    def stage(self, pair):
        to = dict(self.at)
        first, second = pair
        if first == second:
            v = self.bit(first)
            to[first[0]] = to[first[0]] + (1 - 2 * v) * (1 << first[1])
        else:
            va, vb = self.bit(first), self.bit(second)
            to[first[0]] = to[first[0]] + (1 - self.odd) * (1 - 2 * va) * (1 << first[1])
            to[second[0]] = to[second[0]] + self.odd * (1 - 2 * vb) * (1 << second[1])
            v = (1 - self.odd) * va + self.odd * vb
        return (to["seq"], to["batch"]), v


class Links:
    def __init__(self, send, recv):
        self.send, self.recv, self.used, self.made, self.free, self.open = send, recv, 0, 0, [], []

    def copy(self, src, dst, to, start=True):
        i = self.used
        self.used += 1
        if self.free:
            k = self.free.pop()
        else:
            k = self.made
            self.made += 1
        assert self.used <= self.recv.shape[0] and self.made <= self.send.shape[0]
        c = pltpu.make_async_remote_copy(
            src_ref=src, dst_ref=dst, send_sem=self.send.at[k], recv_sem=self.recv.at[i], device_id=to, device_id_type=MESH
        )
        if start:
            c.start()
            self.open.append((c, k))
        return c

    def sent(self, *copies):
        for copy in copies:
            copy.wait_send()
            self.free += [k for c, k in self.open if c is copy]
            self.open = [(c, k) for c, k in self.open if c is not copy]

    def drain(self):
        self.sent(*(c for c, _ in self.open))


GROUP = [(1, 0, 0), (1, 0, 1), (0, 1, 0), (0, 1, 1), (0, 0, 1)]


def log2(size):
    return size.bit_length() - 1


def all_bits(sizes):
    s = [("seq", k) for k in range(log2(sizes["seq"]))]
    b = [("batch", k) for k in range(log2(sizes["batch"]))]
    return s, b


def small_plan(sizes):
    s, b = all_bits(sizes)
    return [(b[0], b[0]), (s[0], b[1]), (b[1], s[0])] + [(q, q) for q in s[1:] + b[2:]]


def halvings(rows, stages):
    out = []
    for _ in range(stages):
        ok = rows % 16 == 0
        out.append(ok)
        rows = rows // 2 if ok else rows
    return out


def landing_rows(rows, stages):
    total = 0
    for ok in halvings(rows, stages):
        rows = rows // 2 if ok else rows
        total += rows
    return total


def reduce_rows(place, links, plan, acc, land, kept):
    rows = acc.shape[0]
    off, base, before = 0, 0, []
    for pair, ok in zip(plan, halvings(rows, len(plan))):
        to, v = place.stage(pair)
        parent = off
        if ok:
            rows //= 2
            off, give = off + v * rows, off + (1 - v) * rows
        else:
            give = off
        copy = links.copy(acc.at[pl.ds(mult(give, 8), rows)], land.at[pl.ds(base, rows)], to)
        yield
        copy.wait_recv()
        links.sent(*before)
        before = [copy]
        if not ok:
            links.sent(copy)
            before = []

        def add(i, off=off, base=base):
            at = pl.ds(mult(off + i * 8, 8), 8)
            acc[at] = acc[at] + land[pl.ds(mult(base + i * 8, 8), 8)]

        loop(rows // 8, add)
        base += rows
        if ok:
            kept.append((to, parent, off, rows))
    links.sent(*before)
    return off, rows


def place_rows(acc, off, rows, whole):
    def one(i):
        whole(off + i * 8, 8)[...] = acc[pl.ds(mult(off + i * 8, 8), 8)]

    loop(rows // 8, one)


def small_chain(place, links, plan, acc, land, out):
    whole = lambda row, rows: out.at[pl.ds(mult(row, 8), rows)]
    kept = []
    off, rows = yield from reduce_rows(place, links, plan, acc, land, kept)
    place_rows(acc, off, rows, whole)
    for to, _, off, rows in reversed(kept):
        copy = links.copy(whole(off, rows), whole(off, rows), to)
        yield
        copy.wait_recv()


def tiled(count):
    return count in (2, 4, 6, 8, 12, 24)


def carry_peers(count, s):
    if tiled(count):
        return [lax.rem(s + i, count) for i in range(1, count)]
    return [s + (1 - 2 * (s // (1 << k) % 2)) * (1 << k) for k in range(log2(count))]


def carry_scratch(count, n, inner):
    v = lambda *shape: pltpu.VMEM(shape, f32)
    if tiled(count):
        w = inner // (count // 2)
        return dict(got=v(count, 2, 8, w), back=v(count, 2, 8, w), got_sum=v(count, 1, w), tile_dec=v(count, 8, w))
    return dict(got=v(2 * log2(count), 2, n, inner), back=v(2, n, inner), tot=v(2, n, inner))


def carry(place, links, m, way):
    return (carry_tiles if tiled(place.sizes["seq"]) else carry_doubling)(place, links, m, way)


def carry_doubling(place, links, m, way):
    bits = log2(place.sizes["seq"])
    inner = m.a2.shape[1]
    for k in range(0, inner, SCAN):
        (scan_lams if way else scan_ends)(m, slice(k, k + SCAN))
    m.edges[way] = jnp.zeros_like(m.edges[way])
    m.back[way] = jnp.ones_like(m.back[way])
    m.tot[0] = m.ends[way]
    m.tot[1] = jnp.exp2(m.a2[...] * m.sums[...])
    for k, p in enumerate(carry_peers(place.sizes["seq"], place.s)):
        got = m.got.at[way * bits + k]
        copy = links.copy(m.tot, got, (p, place.b))
        copy.wait_recv()
        links.sent(copy)
        later = place.bit(("seq", k))

        @pl.when(later == 1 - way)
        def _():
            m.edges[way] += m.back[way] * got[0]
            m.back[way] *= got[1]
            m.tot[0] += m.tot[1] * got[0]

        @pl.when(later == way)
        def _():
            m.tot[0] = got[0] + got[1] * m.tot[0]

        m.tot[1] *= got[1]
    yield
    yield


def carry_tiles(place, links, m, way):
    count, s, b = place.sizes["seq"], place.s, place.b
    across = count // 2
    width = m.ends.shape[2] // across
    peers = carry_peers(count, s)

    def cut(ref, p):
        return ref.at[pl.ds(mult(p // across * 8, 8), 8), pl.ds(mult(p % across * width, LANES), width)]

    def cut_sum(p):
        return m.sums.at[:, pl.ds(mult(p % across * width, LANES), width)]

    first = []
    for k in range(across):
        (scan_lams if way else scan_ends)(m, pl.ds(mult(lax.rem(s + k, across) * width, LANES), width))
        for i in (k, k + across):
            if i:
                p = peers[i - 1]
                first.append(links.copy(cut(m.ends.at[way], p), m.got.at[s, way], (p, b)))
                if way == 0:
                    first.append(links.copy(cut_sum(p), m.got_sum.at[s], (p, b)))
    m.got[s, way] = cut(m.ends.at[way], s)[...]
    if way == 0:
        m.got_sum[s] = cut_sum(s)[...]
    yield
    for c in first:
        c.wait_recv()
    if way == 0:
        a2 = cut(m.a2, s)[...]
        for p in range(count):
            m.tile_dec[p] = jnp.exp2(a2 * m.got_sum[p])
    value = jnp.zeros((8, width), f32)
    for p in reversed(range(count)) if way else range(count):
        m.back[p, way] = value
        value = m.got[p, way] + m.tile_dec[p] * value
    second = [links.copy(m.back.at[p, way], cut(m.edges.at[way], s), (p, b)) for p in peers]
    cut(m.edges.at[way], s)[...] = m.back[s, way]
    links.sent(*first)
    yield
    for c in second:
        c.wait_recv()
    links.sent(*second)


def wide(tile, width=SCAN):
    return jnp.concatenate([tile] * (width // LANES), axis=1)


def spread(row, n):
    return jnp.broadcast_to(row, (n, row.shape[1]))


def fold(value):
    return sum(value[:, k : k + LANES] for k in range(0, value.shape[1], LANES))


def scan_ends(m, lanes):
    a2 = m.a2[:, lanes]
    n = a2.shape[0]

    def chunk(i, h):
        at = pl.ds(pl.multiple_of(i * 8, 8), 8)
        s8, u8 = m.step[at, lanes], m.u[at, lanes]
        for j in range(8):
            b = wide(m.bb[pl.ds(pl.multiple_of((i * 8 + j) * n, 8), n)], a2.shape[1])
            h = jnp.exp2(spread(s8[j : j + 1], n) * a2) * h + spread(u8[j : j + 1], n) * b
        return h

    m.ends[0, :, lanes] = lax.fori_loop(0, m.step.shape[0] // 8, chunk, jnp.zeros_like(a2))


def scan_lams(m, lanes):
    a2 = m.a2[:, lanes]
    n = a2.shape[0]

    def chunk(i, held):
        dec, acc = held
        at = pl.ds(pl.multiple_of(i * 8, 8), 8)
        s8, d8 = m.step[at, lanes], m.d_res[at, lanes]
        for j in range(8):
            c = wide(m.cc[pl.ds(pl.multiple_of((i * 8 + j) * n, 8), n)], a2.shape[1])
            dec = dec * jnp.exp2(spread(s8[j : j + 1], n) * a2)
            acc = acc + dec * (spread(d8[j : j + 1], n) * c)
        return dec, acc

    zero = jnp.zeros_like(a2)
    m.ends[1, :, lanes] = lax.fori_loop(0, m.step.shape[0] // 8, chunk, (zero + 1.0, zero))[1]


def scan_out(m, lanes):
    a2 = m.a2[:, lanes]
    n = a2.shape[0]

    def chunk(i, h):
        at = pl.ds(pl.multiple_of(i * 8, 8), 8)
        s8, u8 = m.step[at, lanes], m.u[at, lanes]
        ys = []
        for j in range(8):
            t = pl.ds(pl.multiple_of((i * 8 + j) * n, 8), n)
            b, c = wide(m.bb[t], a2.shape[1]), wide(m.cc[t], a2.shape[1])
            h = jnp.exp2(spread(s8[j : j + 1], n) * a2) * h + spread(u8[j : j + 1], n) * b
            ys.append(jnp.sum(c * h, axis=0, keepdims=True))
        m.y[at, lanes] = jnp.concatenate(ys, axis=0)
        return h

    lax.fori_loop(0, m.step.shape[0] // 8, chunk, m.edges[0, :, lanes])


def scan_again(m, lanes, first):
    a2 = m.a2[:, lanes]
    n = a2.shape[0]
    tokens = m.step.shape[0]

    def ahead(i, h):
        at = pl.ds(pl.multiple_of(i * 8, 8), 8)
        s8, u8, d8 = m.step[at, lanes], m.u[at, lanes], m.d_res[at, lanes]
        for j in range(8):
            t = pl.ds(pl.multiple_of((i * 8 + j) * n, 8), n)
            m.h[i * 8 + j] = h
            h = jnp.exp2(spread(s8[j : j + 1], n) * a2) * h + spread(u8[j : j + 1], n) * wide(m.bb[t])
            part = fold(spread(d8[j : j + 1], n) * h)
            m.cg[t] = part if first else m.cg[t] + part
        return h

    lax.fori_loop(0, tokens // 8, ahead, m.edges[0, :, lanes])


def scan_back(m, lanes, first):
    a2 = m.a2[:, lanes]
    n = a2.shape[0]
    tokens = m.step.shape[0]

    def behind(i, held):
        q, rate = held
        r = tokens // 8 - 1 - i
        at = pl.ds(pl.multiple_of(r * 8, 8), 8)
        s8, u8, d8 = m.step[at, lanes], m.u[at, lanes], m.d_res[at, lanes]
        sg, lb = [None] * 8, [None] * 8
        for j in reversed(range(8)):
            t = pl.ds(pl.multiple_of((r * 8 + j) * n, 8), n)
            st = spread(s8[j : j + 1], n)
            lam = spread(d8[j : j + 1], n) * wide(m.cc[t]) + q
            q = jnp.exp2(st * a2) * lam
            dec = q * m.h[r * 8 + j]
            lb[j] = jnp.sum(lam * wide(m.bb[t]), axis=0, keepdims=True)
            sg[j] = jnp.sum(dec * a2, axis=0, keepdims=True)
            rate = rate + dec * st
            part = fold(lam * spread(u8[j : j + 1], n))
            m.bg[t] = part if first else m.bg[t] + part
        lb8, sg8 = jnp.concatenate(lb, axis=0), jnp.concatenate(sg, axis=0)
        m.sg[at, lanes] = LN2 * sg8 + m.mixed[at, lanes] * lb8
        m.gate[at, lanes] = s8 * lb8
        return q, rate

    _, rate = lax.fori_loop(0, tokens // 8, behind, (m.edges[1, :, lanes], jnp.zeros_like(a2)))
    m.rate[:, lanes] = rate


class Refs:
    pass


FETCH = ["x", "gain", "g", "w_out", "conv_w", "conv_b", "x_proj", "step_proj", "step_b", "code", "a2", "skip"]
ARGS = [v + "_h" for v in FETCH] + ["w_in"]
OUTS = ["block_out", "input_grad", "in_sum", "out_sum", "small_sum", "gain_sum"]


UNITS = ["o0", "o1", "i0", "i1", "x0", "x1"]


def parts(unit):
    return [unit + "ab"[k] for k in range(PARTS.get(unit, 1))]


def recvs(sizes):
    bits, count = log2(sizes["seq"]), sizes["seq"]
    total = 6 + 2 + 3 * len(UNITS) + (5 * (count - 1) if tiled(count) else 2 * bits)
    total += 2 * len(small_plan(sizes)) + sum(halvings(SMALL[0], len(small_plan(sizes))))
    for unit in UNITS:
        for p in parts(unit):
            kept = sum(halvings(LANES * 3 // len(parts(unit)), bits)) - 1
            total += bits + 7 + kept + 3 * {"T1": 0, "T2": kept, "T3": kept - 1}[SPREAD.get(p, "T1")]
    return total


def scratch(sizes, tokens, width, inner, n, rank, taps):
    full = (tokens, inner)
    half, part = inner // 2, width // 2
    stages = log2(sizes["seq"])
    v = lambda *shape: pltpu.VMEM(shape, f32)
    sh = {name: v(*full) for name in ("gate", "d_res", "conv", "mixed", "pre", "step", "u", "y", "d_gate", "sg")}
    sh.update(
        x=v(tokens, width), g=v(tokens, width), vec=v(4, inner), gain=v(width // LANES, LANES),
        conv_b=v(inner // LANES, LANES), step_b=v(inner // LANES, LANES), skip=v(inner // LANES, LANES),
        code=pltpu.VMEM((inner // LANES, LANES), jnp.int32), conv_w=v(taps, inner), x_proj=v(rank + 2 * n, inner),
        step_proj=v(rank, inner), a2=v(n, inner), w_out=v(inner, width),
        normed=v(tokens, width), hid=v(8 + tokens, inner), cgr=v(tokens + 8, inner), proj=v(tokens, LANES),
        wbuf=v(SLOTS, width, WBLOCK), acc=v(tokens, width),
        bb=v(tokens * n, LANES), cc=v(tokens * n, LANES), bg=v(tokens * n, LANES), cg=v(tokens * n, LANES),
        h=v(tokens, n, SCAN), rate=v(n, inner), ends=v(2, n, inner), edges=v(2, n, inner), sums=v(1, inner),
        ng=v(4, tokens, part), gg=v(4, tokens, part),
        gains=v(8, LANES), gains_land=v(landing_rows(8, len(small_plan(sizes))), LANES),
        small=v(*SMALL), small_land=v(landing_rows(SMALL[0], len(small_plan(sizes))), SMALL[1]),
    )
    for unit in UNITS:
        sh["late_" + unit] = v(4, tokens, part)
        for p in parts(unit):
            rows = part // len(parts(unit))
            sh["tile_" + p] = v(rows, part)
            sh["land_" + p] = v(landing_rows(rows, stages), part)
    sh.update(carry_scratch(sizes["seq"], n, inner))
    sh["send"] = pltpu.SemaphoreType.DMA((SENDS,))
    sh["recv"] = pltpu.SemaphoreType.DMA((recvs(sizes),))
    sh["wsem"] = pltpu.SemaphoreType.DMA((SLOTS,))
    sh["isem"] = pltpu.SemaphoreType.DMA((len(FETCH),))
    return sh


def stream(m, first, last):
    def fetch(i, slot):
        cols = pl.ds(mult((first + i) * WBLOCK, WBLOCK), WBLOCK)
        return pltpu.make_async_copy(m.w_in.at[:, cols], m.wbuf.at[slot], m.wsem.at[slot])

    ahead = SLOTS - 1
    for k in range(ahead):
        fetch(k, k).start()

    def run(use):
        def body(i):
            slot = lax.rem(i, SLOTS)
            fetch(i, slot).wait()

            @pl.when(i + ahead < last - first)
            def _():
                fetch(i + ahead, lax.rem(i + ahead, SLOTS)).start()

            use(i, m.wbuf[slot])

        loop(last - first, body)

    return run


def late_chain(place, links, m, unit, value, left, right):
    late = getattr(m, "late_" + unit)
    width = late.shape[2]
    shift = int(unit[1]) * width
    mine = place.y if unit[0] == "o" else place.x
    to, _ = place.near(0, 1, 0) if unit[0] == "o" else place.near(1, 0, 0)
    core, _ = place.near(0, 0, 1)

    def cut(which):
        return value.at[:, pl.ds(mult(which * 2 * width + shift, LANES), width)]

    def pass_on(which):
        slot = late.at[which * 2 + place.c]
        return links.copy(slot, slot, core)

    sent = links.copy(cut(1 - mine), late.at[mine * 2 + place.c], to)
    late[mine * 2 + place.c] = cut(mine)[...]
    passed = [pass_on(mine)]
    yield
    sent.wait_recv()
    passed.append(pass_on(1 - mine))
    yield
    for copy in passed:
        copy.wait_recv()
    links.sent(sent, *passed)
    for i in range(2):
        cell = matmul(left(i), right(i), ((0,), (0,)))
        rows = cell.shape[0] // len(parts(unit))
        for k, p in enumerate(parts(unit)):
            tile = getattr(m, "tile_" + p)
            value = cell[k * rows : (k + 1) * rows]
            tile[...] = value if i == 0 else tile[...] + value


def piece_chain(place, links, m, p, zplan, out, base):
    acc, land = getattr(m, "tile_" + p), getattr(m, "land_" + p)
    rows, cols = acc.shape
    key, shift, r0 = p[0], int(p[1]) * m.x.shape[1] // 2, "ab".index(p[2]) * rows
    part = cols
    half = 2 * part
    bit = ("seq", 0) if key == "o" else ("batch", 1)
    x, y, c = place.x, place.y, place.c
    core, _ = place.near(0, 0, 1)

    def region(at, row, count):
        xx, yy = at
        if key == "o":
            top, side = yy * half + shift + r0 + xx * (rows // 2) + row, c * part
        else:
            top, side = c * part + r0 + yy * (rows // 2) + row, base + xx * half + shift
        return out.at[pl.ds(mult(top, 8), count), pl.ds(mult(side, LANES), cols)]

    kept = []
    off, count = yield from reduce_rows(place, links, [(bit, bit)] + zplan, acc, land, kept)
    edge = kept[0][2]
    place_rows(acc, off, count, lambda row, n: region((x, y), row - edge, n))
    row = off - edge
    held, across = [(x, y)], []

    def give(at, to):
        ref = region(at, row, count)
        return links.copy(ref, ref, to)

    steps = list(reversed(kept[1:]))
    kind = SPREAD.get(p, "T1")
    steps.insert({"T1": len(steps), "T2": 0, "T3": 1}[kind], None)
    for i, step in enumerate(steps):
        last = i == len(steps) - 1
        if step is not None:
            to, parent, _, size = step
            copies = [give(at, to) for at in held]
            yield
            for copy in copies:
                copy.wait_recv()
            links.sent(*copies)
            row, count = parent - edge, 2 * size
            continue
        first, at_a = place.near(1 - c, c, 0)
        second, at_b = place.near(c, 1 - c, 0)
        _, at_d = place.near(1, 1, 0)
        a, b = give((x, y), first), give((x, y), second)
        held = [(x, y), at_a, at_b, at_d]

        def onward(at):
            if last:
                across.append(give(at, core))

        onward((x, y))
        yield
        a.wait_recv()
        d = give(at_a, second)
        onward(at_a)
        yield
        b.wait_recv()
        onward(at_b)
        yield
        d.wait_recv()
        links.sent(a, b)
        onward(at_d)
    if not across:
        across = [give(at, core) for at in held]
    yield
    for copy in across:
        copy.wait_recv()


def block_kernel(sizes, names, *refs):
    m = Refs()
    for name, ref in zip(ARGS + OUTS + names, refs):
        setattr(m, name, ref)
    place = Place(sizes)
    links = Links(m.send, m.recv)
    s, b, c = place.s, place.b, place.c
    count = sizes["seq"]
    tokens, width = m.x.shape
    inner, n = m.a2.shape[1], m.a2.shape[0]
    rank = m.step_proj.shape[0]
    taps = m.conv_w.shape[0]
    half, part = inner // 2, width // 2
    blocks_of_half = inner // WBLOCK
    last = s == count - 1

    fetched = {}
    for i, name in enumerate(FETCH):
        fetched[name] = pltpu.make_async_copy(getattr(m, name + "_h"), getattr(m, name), m.isem.at[i])
    for name in FETCH[:3]:
        fetched[name].start()
    to_hidden = stream(m, 0, blocks_of_half)
    for name in FETCH[3:]:
        fetched[name].start()
    bar = pltpu.get_barrier_semaphore()
    greet = [place.near(*d)[0] for d in GROUP[1:]] + [(p, b) for p in carry_peers(count, s)]
    if not tiled(count):
        greet += [(lax.rem(s + 1, count), b), (lax.rem(s + count - 1, count), b)]
    for to in greet:
        pl.semaphore_signal(bar, inc=1, device_id=to, device_id_type=MESH)

    fetched["x"].wait()
    fetched["gain"].wait()

    def to_row(name, k):
        ref = getattr(m, name)
        for j in range(ref.shape[0]):
            m.vec[k : k + 1, j * LANES : (j + 1) * LANES] = ref[j : j + 1]

    to_row("gain", 3)
    x = m.x[...]
    rms = lax.rsqrt(jnp.mean(x * x, axis=1, keepdims=True) + EPSILON)
    scaled = x * m.vec[3:4, :width]
    m.normed[...] = scaled * rms
    left = stacked(scaled)

    def hidden_block(i, w):
        m.hid[pl.ds(8, tokens), pl.ds(mult(i * WBLOCK, WBLOCK), WBLOCK)] = rms * rows_matmul(left, w, ((1,), (0,)))

    to_hidden(hidden_block)
    to_gate = stream(m, blocks_of_half, 2 * blocks_of_half)
    pl.semaphore_wait(bar, len(greet))
    halo = links.copy(m.hid.at[pl.ds(tokens, 8)], m.hid.at[pl.ds(0, 8)], (lax.rem(s + 1, count), b), start=False)

    @pl.when(jnp.logical_not(last))
    def _():
        halo.start()

    fetched["g"].wait()
    early = []
    for d in GROUP:
        to, _ = place.near(*d)
        cols = pl.ds(mult((c + d[2] * (1 - 2 * c)) * part, LANES), part)
        if not d[1]:
            early.append(links.copy(m.normed.at[:, cols], m.ng.at[place.x * 2 + c], to))
        if not d[0]:
            early.append(links.copy(m.g.at[:, cols], m.gg.at[place.y * 2 + c], to))
    own = pl.ds(mult(c * part, LANES), part)
    m.ng[place.x * 2 + c] = m.normed[:, own]
    m.gg[place.y * 2 + c] = m.g[:, own]


    for name in FETCH[3:]:
        fetched[name].wait()
    m.step_b[...] = m.step_b[...] - 0.5 * m.code[...].astype(f32)
    for k, name in enumerate(("conv_b", "step_b", "skip")):
        to_row(name, k)
    m.a2[...] = -LOG2E * jnp.exp(m.a2[...])
    def convolve(i):
        window = m.hid[pl.ds(mult(i * 8, 8), 16)]
        v = m.vec[0:1]
        for k in range(taps):
            o = 8 - taps + 1 + k
            v = v + m.conv_w[k : k + 1] * window[o : o + 8]
        at = pl.ds(mult(i * 8, 8), 8)
        m.conv[at] = v
        m.mixed[at] = v * sigmoid(v)

    loop(tokens // 8 - 1, lambda i: convolve(i + 1))

    @pl.when(s > 0)
    def _():
        halo.wait_recv()

    @pl.when(s == 0)
    def _():
        m.hid[pl.ds(0, 8)] = jnp.zeros((8, inner), f32)

    convolve(0)

    proj = matmul(m.mixed[...], m.x_proj[...], ((1,), (1,)))
    m.proj[:, : proj.shape[1]] = proj
    for j in range(n):
        at = pl.ds(j, tokens, stride=n)
        m.bb[at] = jnp.broadcast_to(proj[:, rank + j : rank + j + 1], (tokens, LANES))
    low_left = stacked(proj[:, :rank])

    def step_block(i):
        cols = pl.ds(mult(i * WBLOCK, WBLOCK), WBLOCK)
        pre = rows_matmul(low_left, m.step_proj[:, cols], ((1,), (0,))) + m.vec[1:2, cols]
        step = jnp.maximum(pre, 0.0) + jnp.log1p(jnp.exp(-jnp.abs(pre)))
        m.pre[:, cols] = pre
        m.step[:, cols] = step
        m.u[:, cols] = step * m.mixed[:, cols]
        m.sums[:, cols] = jnp.sum(step, axis=0, keepdims=True)

    loop(blocks_of_half, step_block)

    blocks = [slice(k, k + SCAN) for k in range(0, inner, SCAN)]
    ahead = carry(place, links, m, 0)
    next(ahead)
    g_left = stacked(m.g[...])

    def d_gated_block(i):
        cols = pl.ds(mult(i * WBLOCK, WBLOCK), WBLOCK)
        m.d_res[:, cols] = rows_matmul(g_left, m.w_out[cols], ((1,), (1,)))

    loop(blocks_of_half, d_gated_block)
    for j in range(n):
        at = pl.ds(j, tokens, stride=n)
        m.cc[at] = jnp.broadcast_to(m.proj[:, rank + n + j : rank + n + j + 1], (tokens, LANES))

    def gate_block(i, w):
        cols = pl.ds(mult(i * WBLOCK, WBLOCK), WBLOCK)
        z = rms * rows_matmul(left, w, ((1,), (0,)))
        sg = sigmoid(z)
        act = z * sg
        d = m.d_res[:, cols]
        m.gate[:, cols] = act
        m.d_res[:, cols] = d * act
        m.d_gate[:, cols] = d * (sg * (1.0 + z * (1.0 - sg)))

    to_gate(gate_block)
    next(ahead)
    behind = carry(place, links, m, 1)
    next(behind)
    for _ in ahead:
        pass
    def finish_quarters(k):
        for first in (k * part, half + k * part):
            cols = slice(first, first + part)
            scan_out(m, cols)

            def rows(i):
                at = pl.ds(mult(i * 8, 8), 8)
                result = m.y[at, cols] + m.vec[2:3, cols] * m.mixed[at, cols]
                m.y[at, cols] = result * m.gate[at, cols]
                m.d_gate[at, cols] = m.d_gate[at, cols] * result

            loop(tokens // 8, rows)

    s_bits, b_bits = all_bits(sizes)
    zplan = [(k, k) for k in s_bits[1:] + b_bits[2:]]
    chains, v = {}, Refs()

    def pair(ref):
        return lambda i: ref[pl.ds(2 * i, 2)].reshape(2 * tokens, ref.shape[2])

    def go(name):
        try:
            next(chains[name])
        except StopIteration:
            del chains[name]
            if name in UNITS:
                where = {"o": (m.out_sum, 0), "i": (m.in_sum, inner), "x": (m.in_sum, 0)}[name[0]]
                for p in parts(name):
                    chains[p] = piece_chain(place, links, m, p, zplan, *where)

    def late(key, value, left, right, which=(0, 1)):
        for unit in (key + str(k) for k in which):
            ref = getattr(m, "late_" + unit)
            chains[unit] = late_chain(place, links, m, unit, value, pair(ref if left is None else left), pair(ref if right is None else right))

    column = lax.broadcasted_iota(jnp.int32, (tokens, LANES), 1)
    zero = jnp.zeros((8, inner), f32)

    def collect(ref, base, total):
        for j in range(n):
            rows = jnp.sum(ref[pl.ds(j, tokens, stride=n)], axis=1, keepdims=True)
            total = total + jnp.where(column == base + j, rows, 0.0)
        return total

    def put_small(row, value):
        rows = value.shape[0]
        cut, top = SMALL[1], 80
        m.small[row : row + rows] = value[:, :cut]
        over = inner - cut
        if row < top:
            m.small[2 * top + row : 2 * top + row + rows, :over] = value[:, cut:]
        else:
            m.small[top + row : top + row + rows, over:] = value[:, cut:]

    def quarters(k):
        finish_quarters(k)
        late("o", m.y, None, m.gg, (k,))
        late("i", m.d_gate, m.ng, None, (k,))
        if k == 0:
            next(behind)

    def again(k):
        scan_again(m, blocks[k], k == 0)

    def back(k):
        if k == 0:
            for _ in behind:
                pass
            for e in early:
                e.wait_recv()
            links.sent(*early)
        scan_back(m, blocks[k], k == 0)

    def pre():
        bc_grad = collect(m.cg, rank + n, collect(m.bg, rank, jnp.zeros((tokens, LANES), f32)))

        def rows(i, total):
            at = pl.ds(pl.multiple_of(i * 8, 8), 8)
            p = m.sg[at] * sigmoid(m.pre[at])
            m.sg[at] = p
            return total[0] + p, total[1] + m.d_res[at] * m.mixed[at]

        total = lax.fori_loop(0, tokens // 8, rows, (zero, zero))
        v.bias_grad, v.skip_grad = (jnp.sum(t, axis=0, keepdims=True) for t in total)
        low_grad = matmul(m.sg[...], m.step_proj[...], ((1,), (1,)))
        v.proj_grad = jnp.concatenate([low_grad, bc_grad[:, rank : rank + 2 * n]], axis=1)

    def mixg():
        pg_left = stacked(v.proj_grad)

        def block(i):
            cols = pl.ds(mult(i * WBLOCK, WBLOCK), WBLOCK)
            d = rows_matmul(pg_left, m.x_proj[:, cols], ((1,), (0,)))
            z = m.conv[:, cols]
            sg = sigmoid(z)
            d = d + m.gate[:, cols] + m.d_res[:, cols] * m.vec[2:3, cols]
            m.cgr[pl.ds(0, tokens), cols] = d * (sg * (1.0 + z * (1.0 - sg)))

        loop(blocks_of_half, block)
        v.halo_back = links.copy(
            m.cgr.at[pl.ds(0, 8)], m.cgr.at[pl.ds(tokens, 8)], (lax.rem(s + count - 1, count), b), start=False)

        @pl.when(s > 0)
        def _():
            v.halo_back.start()

    def xg():
        @pl.when(jnp.logical_not(last))
        def _():
            v.halo_back.wait_recv()

        @pl.when(last)
        def _():
            m.cgr[pl.ds(tokens, 8)] = jnp.zeros((8, inner), f32)

        def rows(i):
            window = m.cgr[pl.ds(mult(i * 8, 8), 16)]
            z = m.conv_w[0:1] * window[taps - 1 : taps + 7]
            for k in range(1, taps):
                o = taps - 1 - k
                z = z + m.conv_w[k : k + 1] * window[o : o + 8]
            m.gate[pl.ds(mult(i * 8, 8), 8)] = z

        loop(tokens // 8, rows)
        late("x", m.gate, m.ng, None)

    def taps_():
        def rows(i, total):
            at = pl.ds(pl.multiple_of(i * 8, 8), 8)
            window = m.hid[pl.ds(pl.multiple_of(i * 8, 8), 16)]
            z = m.cgr[at]
            o = 8 - taps + 1
            return tuple(t + z * window[o + k : o + k + 8] for k, t in enumerate(total[:-1])) + (total[-1] + z,)

        total = lax.fori_loop(0, tokens // 8, rows, (zero,) * (taps + 1))
        v.tap_rows = [jnp.sum(t, axis=0, keepdims=True) for t in total]

    def mid():
        put_small(0, matmul(v.proj_grad, m.mixed[...], ((0,), (0,))))
        put_small(rank + 2 * n, matmul(m.proj[:, :rank], m.sg[...], ((0,), (0,))))
        put_small(2 * rank + 2 * n, m.rate[...] * m.a2[...] * LN2)
        rows = v.tap_rows + [v.bias_grad, v.skip_grad, zero[:1]]
        put_small(2 * rank + 3 * n, jnp.concatenate(rows, axis=0))
        end = 2 * rank + 3 * n + 8
        m.small[end:160] = jnp.zeros((160 - end, SMALL[1]), f32)
        m.small[240:256] = jnp.zeros((16, SMALL[1]), f32)
        m.small[80 + end : 240, SMALL[1] // 2 :] = jnp.zeros((160 - end, SMALL[1] // 2), f32)
        chains["s"] = small_chain(place, links, small_plan(sizes), m.small, m.small_land, m.small_sum)

    def normed_block(ref):
        def use(i, w):
            d = stacked(ref[:, pl.ds(mult(i * WBLOCK, WBLOCK), WBLOCK)])
            m.acc[...] = m.acc[...] + rows_matmul(d, w, ((1,), (1,)))

        return use

    def ng0():
        m.acc[...] = jnp.zeros_like(m.acc)
        stream(m, blocks_of_half, 2 * blocks_of_half)(normed_block(m.d_gate))

    def ng1():
        stream(m, 0, blocks_of_half)(normed_block(m.gate))

    def inp():
        x = m.x[...]
        rms = lax.rsqrt(jnp.mean(x * x, axis=1, keepdims=True) + EPSILON)
        normed_grad = m.acc[...]
        gain_grad = jnp.sum(normed_grad * x * rms, axis=0, keepdims=True)
        weighted = normed_grad * m.vec[3:4, :width]
        m.input_grad[...] = rms * weighted - rms * rms * rms * x * jnp.mean(weighted * x, axis=1, keepdims=True) + m.g[...]
        for k in range(width // LANES):
            m.gains[k : k + 1] = gain_grad[:, k * LANES : (k + 1) * LANES]
        m.gains[width // LANES :] = jnp.zeros((8 - width // LANES, LANES), f32)
        chains["n"] = small_chain(place, links, small_plan(sizes), m.gains, m.gains_land, m.gain_sum)

    def bo():
        gl = stacked(m.y[...])

        def block(i):
            cols = pl.ds(mult(i * WBLOCK, WBLOCK), WBLOCK)
            m.block_out[:, cols] = m.x[:, cols] + rows_matmul(gl, m.w_out[:, cols], ((1,), (0,)))

        loop(width // WBLOCK, block)

    work = {
        "g0": lambda: quarters(0), "g1": lambda: quarters(1), "a0": lambda: again(0), "b0": lambda: back(0), "a1": lambda: again(1), "b1": lambda: back(1),
        "a2": lambda: again(2), "b2": lambda: back(2), "pre": pre, "mixg": mixg,
        "xg": xg, "taps": taps_, "mid": mid, "ng0": ng0, "ng1": ng1, "inp": inp, "bo": bo,
    }
    for name in ORDER:
        if name in work:
            work.pop(name)()
        elif name in chains:
            go(name)
    assert not work
    while chains:
        for name in list(chains):
            go(name)

    @pl.when(jnp.logical_not(last))
    def _():
        halo.wait_send()

    @pl.when(s > 0)
    def _():
        v.halo_back.wait_send()

    links.drain()


def unpack_kernel(rank, n, a_v, b_v, c_v, d_v, small, gains, a_o, b_o, c_o, d_o, x_proj_o, step_proj_o, decay_o, taps_o, *rest):
    row_os, sems = rest[:-1], rest[-1]
    copies = []
    for v, o, cuts in ((c_v, c_o, 8), (d_v, d_o, 4), (a_v, a_o, 1), (b_v, b_o, 1)):
        rows = v.shape[0] // cuts
        for k in range(cuts):
            at = pl.ds(k * rows, rows)
            copies.append(pltpu.make_async_copy(v.at[at], o.at[at], sems.at[len(copies)]))
    for c in copies:
        c.start()

    def take(row, rows):
        over = SMALL[1] // 2
        if row < 80:
            tail = small[160 + row : 160 + row + rows, :over]
        else:
            tail = small[80 + row : 80 + row + rows, over:]
        return jnp.concatenate([small[row : row + rows], tail], axis=1)

    x_proj_o[...] = take(0, rank + 2 * n)
    step_proj_o[...] = take(rank + 2 * n, rank)
    decay_o[...] = take(2 * rank + 2 * n, n)
    rows = take(2 * rank + 3 * n, 8)
    taps = taps_o.shape[0]
    taps_o[...] = rows[:taps]
    row_os[3][...] = gains[: row_os[3].shape[0]]
    for k, ref in enumerate(row_os[:3]):
        for j in range(ref.shape[0]):
            ref[j : j + 1] = rows[taps + k : taps + k + 1, j * LANES : (j + 1) * LANES]
    for c in copies:
        c.wait()


VMEM = pl.BlockSpec(memory_space=pltpu.VMEM)
ANY = pl.BlockSpec(memory_space=pl.ANY)


def shards(sizes, inputs, norm_gain, w_in, conv_weight, conv_bias, x_proj, step_proj, step_bias, decay_code, decay_log,
           skip_gain, w_out, cotangent):
    seqs, tokens, width = inputs.shape
    assert seqs == 1 and sizes["batch"] == 4 and sizes["seq"] % 2 == 0
    inner = w_in.shape[1] // 2
    rank, n, taps = step_proj.shape[0], decay_log.shape[1], conv_weight.shape[0]
    sh = scratch(sizes, tokens, width, inner, n, rank, taps)
    tall = lambda u: u.reshape(-1, LANES)
    args = dict(
        x=inputs[0], g=cotangent[0], gain=tall(norm_gain), conv_w=conv_weight, conv_b=tall(conv_bias), x_proj=x_proj.T,
        step_proj=step_proj, step_b=tall(step_bias), code=tall(decay_code), a2=decay_log.T, skip=tall(skip_gain), w_out=w_out)
    held = [pltpu.VMEM(v, f32) for v in ((tokens, width), (tokens, width), (width, 2 * inner), (inner, width), SMALL, (8, LANES))]
    sums = pl.pallas_call(
        functools.partial(block_kernel, sizes, list(sh)),
        in_specs=[ANY] * len(ARGS),
        out_specs=[VMEM] * 6,
        out_shape=held,
        scratch_shapes=list(sh.values()),
        compiler_params=pltpu.CompilerParams(collective_id=1, has_side_effects=True, vmem_limit_bytes=VLIMIT << 19),
        name="block",
    )(*(args[a] for a in FETCH), w_in)
    wanted = [v.shape for v in sums[:4]] + [(rank + 2 * n, inner), (rank, inner), (n, inner), (taps, inner)]
    wanted += [(inner // LANES, LANES)] * 3 + [(width // LANES, LANES)]
    block_out, input_grad, in_sum, out_sum, x_proj_sum, step_proj_sum, decay_sum, taps_sum, *rows = pl.pallas_call(
        functools.partial(unpack_kernel, rank, n),
        in_specs=[VMEM] * 6,
        out_specs=[ANY] * 4 + [VMEM] * 8,
        out_shape=[jax.ShapeDtypeStruct(v, f32) for v in wanted],
        scratch_shapes=[pltpu.SemaphoreType.DMA((14,))],
        compiler_params=pltpu.CompilerParams(vmem_limit_bytes=VLIMIT2 << 19),
        name="unpack",
    )(*sums)
    conv_b_sum, step_b_sum, skip_sum, gain_sum = (v.reshape(-1) for v in rows)
    return (block_out[None], input_grad[None], gain_sum, in_sum, taps_sum, conv_b_sum, x_proj_sum.T, step_proj_sum, step_b_sum,
            decay_sum.T, skip_sum, out_sum)


VLIMIT, VLIMIT2 = 97, 16


def solution(mesh):
    rows = P("batch", "seq", None)
    return jax.shard_map(
        functools.partial(shards, dict(mesh.shape)),
        mesh=mesh,
        in_specs=(rows,) + (P(),) * 11 + (rows,),
        out_specs=(rows, rows) + (P(),) * 10,
        check_vma=False,
    )
```

```python
import functools

import jax
import jax.numpy as jnp
from jax import lax
from jax.experimental import pallas as pl
from jax.experimental.pallas import tpu as pltpu
from jax.sharding import PartitionSpec as P

f32 = jnp.float32
bf16 = jnp.bfloat16
MESH = pl.DeviceIdType.MESH
EPSILON = 1e-05
LOG2E = 1.4426950408889634
LN2 = 0.6931471805599453
LANES = 128
SCAN = 512
WBLOCK = 256
SLOTS = 4
SMALL = (256, 1024)
PARTS = {"o0": 2, "o1": 2, "i0": 2, "x0": 2, "x1": 2}
SPREAD = {"o1a": "T3", "x0b": "T3", "x1b": "T3"}
SENDS = 72
ORDER = [
    "g0", "o0", "i0", "g1", "a0", "i1", "o1", "b0", "a1", "o0", "i0", "b1", "o0", "i0", "i0a", "o0b",
    "a2", "o0a", "i0b", "o1", "b2", "pre", "mixg", "i1", "o1", "o1a", "o0b", "i1", "i1a", "o0a", "xg", "x1",
    "i0b", "taps", "o0b", "o1a", "mid", "o0a", "s", "i0a", "x0", "i0b", "x1", "s", "i1a", "o0b", "x1", "o0a",
    "x1a", "o1b", "i0b", "o0b", "x0", "i0a", "x1b", "o0a", "o1a", "x0", "x0b", "x1a", "i0b", "o0b", "x1b", "i0a",
    "x0a", "s", "o1a", "i1a", "ng0", "o1b", "i0a", "o0a", "x1a", "o1a", "i0b", "x1b", "x0b", "i1a", "ng1", "x0a",
    "i0a", "s", "x1b", "x0b", "o1a", "inp", "i1a", "x1a", "o0a", "o1b", "o0b", "n", "i0b", "bo", "x0a", "o1a",
    "x1b", "i0a", "n", "x0b", "x1a", "o1b", "o1a", "i1a", "x0a", "s", "o1b", "x0b", "x1b", "n", "s", "x1b",
    "i0a", "o0b", "i0b", "x0a", "x1a", "s", "x0b", "x1b", "o1b", "x0b", "i0a", "x0a", "o0b", "s", "i0b", "x1a",
    "o0b", "x0b", "i1a", "o1b", "o0a", "n", "o1a", "x1a", "o0a", "i1a", "n", "x1b", "o1b", "s", "o1b", "i0b",
    "x1a", "x0b", "o1a", "x0a", "i0a", "i1a", "n", "o1b", "o0a", "x0a", "s", "i1a", "x0b", "x0a", "s", "x1a",
    "x1b", "x0a",
]


def mult(value, by):
    return value if isinstance(value, int) else pl.multiple_of(value, by)


def split(value):
    high = value.astype(bf16)
    return high, (value - high.astype(f32)).astype(bf16)


def dot(a, b, dims):
    return lax.dot_general(a, b, (dims, ((), ())), preferred_element_type=f32)


def matmul(a, b, dims=((1,), (0,))):
    (ah, al), (bh, bl) = split(a), split(b)
    return dot(ah, bh, dims) + dot(al, bh, dims) + dot(ah, bl, dims)


def stacked(value):
    return jnp.concatenate(split(value), axis=0)


def rows_matmul(both, b, dims):
    rows = both.shape[0] // 2
    bh, bl = split(b)
    wide = dot(both, bh, dims)
    return wide[:rows] + wide[rows:] + dot(both[:rows], bl, dims)


def sigmoid(v):
    return 1.0 / (1.0 + jnp.exp(-v))


def loop(count, body):
    def step(i, _):
        body(i)
        return 0

    lax.fori_loop(0, count, step, 0)


class Place:
    def __init__(self, sizes):
        self.sizes = sizes
        self.s, self.b = lax.axis_index("seq"), lax.axis_index("batch")
        self.at = {"seq": self.s, "batch": self.b}
        self.x, self.c, self.y = self.s % 2, self.b % 2, self.b // 2
        self.odd = self.c

    def near(self, dx, dy, dc):
        dx, dy = dx * (1 - 2 * self.x), dy * (1 - 2 * self.y)
        return (self.s + dx, self.b + dc * (1 - 2 * self.c) + 2 * dy), (self.x + dx, self.y + dy)

    def bit(self, d):
        return self.at[d[0]] // (1 << d[1]) % 2

    def stage(self, pair):
        to = dict(self.at)
        first, second = pair
        if first == second:
            v = self.bit(first)
            to[first[0]] = to[first[0]] + (1 - 2 * v) * (1 << first[1])
        else:
            va, vb = self.bit(first), self.bit(second)
            to[first[0]] = to[first[0]] + (1 - self.odd) * (1 - 2 * va) * (1 << first[1])
            to[second[0]] = to[second[0]] + self.odd * (1 - 2 * vb) * (1 << second[1])
            v = (1 - self.odd) * va + self.odd * vb
        return (to["seq"], to["batch"]), v


class Links:
    def __init__(self, send, recv):
        self.send, self.recv, self.used, self.made, self.free, self.open = send, recv, 0, 0, [], []

    def copy(self, src, dst, to, start=True):
        i = self.used
        self.used += 1
        if self.free:
            k = self.free.pop()
        else:
            k = self.made
            self.made += 1
        assert self.used <= self.recv.shape[0] and self.made <= self.send.shape[0]
        c = pltpu.make_async_remote_copy(
            src_ref=src, dst_ref=dst, send_sem=self.send.at[k], recv_sem=self.recv.at[i], device_id=to, device_id_type=MESH
        )
        if start:
            c.start()
            self.open.append((c, k))
        return c

    def sent(self, *copies):
        for copy in copies:
            copy.wait_send()
            self.free += [k for c, k in self.open if c is copy]
            self.open = [(c, k) for c, k in self.open if c is not copy]

    def drain(self):
        self.sent(*(c for c, _ in self.open))


GROUP = [(1, 0, 0), (1, 0, 1), (0, 1, 0), (0, 1, 1), (0, 0, 1)]


def log2(size):
    return size.bit_length() - 1


def all_bits(sizes):
    s = [("seq", k) for k in range(log2(sizes["seq"]))]
    b = [("batch", k) for k in range(log2(sizes["batch"]))]
    return s, b


def small_plan(sizes):
    s, b = all_bits(sizes)
    return [(b[0], b[0]), (s[0], b[1]), (b[1], s[0])] + [(q, q) for q in s[1:] + b[2:]]


def halvings(rows, stages):
    out = []
    for _ in range(stages):
        ok = rows % 16 == 0
        out.append(ok)
        rows = rows // 2 if ok else rows
    return out


def landing_rows(rows, stages):
    total = 0
    for ok in halvings(rows, stages):
        rows = rows // 2 if ok else rows
        total += rows
    return total


def reduce_rows(place, links, plan, acc, land, kept):
    rows = acc.shape[0]
    off, base, before = 0, 0, []
    for pair, ok in zip(plan, halvings(rows, len(plan))):
        to, v = place.stage(pair)
        parent = off
        if ok:
            rows //= 2
            off, give = off + v * rows, off + (1 - v) * rows
        else:
            give = off
        copy = links.copy(acc.at[pl.ds(mult(give, 8), rows)], land.at[pl.ds(base, rows)], to)
        yield
        copy.wait_recv()
        links.sent(*before)
        before = [copy]
        if not ok:
            links.sent(copy)
            before = []

        def add(i, off=off, base=base):
            at = pl.ds(mult(off + i * 8, 8), 8)
            acc[at] = acc[at] + land[pl.ds(mult(base + i * 8, 8), 8)]

        loop(rows // 8, add)
        base += rows
        if ok:
            kept.append((to, parent, off, rows))
    links.sent(*before)
    return off, rows


def place_rows(acc, off, rows, whole):
    def one(i):
        whole(off + i * 8, 8)[...] = acc[pl.ds(mult(off + i * 8, 8), 8)]

    loop(rows // 8, one)


def small_chain(place, links, plan, acc, land, out):
    whole = lambda row, rows: out.at[pl.ds(mult(row, 8), rows)]
    kept = []
    off, rows = yield from reduce_rows(place, links, plan, acc, land, kept)
    place_rows(acc, off, rows, whole)
    for to, _, off, rows in reversed(kept):
        copy = links.copy(whole(off, rows), whole(off, rows), to)
        yield
        copy.wait_recv()


def tiled(count):
    return count in (2, 4, 6, 8, 12, 24)


def carry_peers(count, s):
    if tiled(count):
        return [lax.rem(s + i, count) for i in range(1, count)]
    return [s + (1 - 2 * (s // (1 << k) % 2)) * (1 << k) for k in range(log2(count))]


def carry_scratch(count, n, inner):
    v = lambda *shape: pltpu.VMEM(shape, f32)
    if tiled(count):
        w = inner // (count // 2)
        return dict(got=v(count, 2, 8, w), back=v(count, 2, 8, w), got_sum=v(count, 1, w), tile_dec=v(count, 8, w))
    return dict(got=v(2 * log2(count), 2, n, inner), back=v(2, n, inner), tot=v(2, n, inner))


def carry(place, links, m, way):
    return (carry_tiles if tiled(place.sizes["seq"]) else carry_doubling)(place, links, m, way)


def carry_doubling(place, links, m, way):
    bits = log2(place.sizes["seq"])
    m.edges[way] = jnp.zeros_like(m.edges[way])
    m.back[way] = jnp.ones_like(m.back[way])
    m.tot[0] = m.ends[way]
    m.tot[1] = jnp.exp2(m.a2[...] * m.sums[...])
    for k, p in enumerate(carry_peers(place.sizes["seq"], place.s)):
        got = m.got.at[way * bits + k]
        copy = links.copy(m.tot, got, (p, place.b))
        copy.wait_recv()
        links.sent(copy)
        later = place.bit(("seq", k))

        @pl.when(later == 1 - way)
        def _():
            m.edges[way] += m.back[way] * got[0]
            m.back[way] *= got[1]
            m.tot[0] += m.tot[1] * got[0]

        @pl.when(later == way)
        def _():
            m.tot[0] = got[0] + got[1] * m.tot[0]

        m.tot[1] *= got[1]
    yield
    yield


def carry_tiles(place, links, m, way):
    count, s, b = place.sizes["seq"], place.s, place.b
    across = count // 2
    width = m.ends.shape[2] // across
    peers = carry_peers(count, s)

    def cut(ref, p):
        return ref.at[pl.ds(mult(p // across * 8, 8), 8), pl.ds(mult(p % across * width, LANES), width)]

    def cut_sum(p):
        return m.sums.at[:, pl.ds(mult(p % across * width, LANES), width)]

    first = [links.copy(cut(m.ends.at[way], p), m.got.at[s, way], (p, b)) for p in peers]
    m.got[s, way] = cut(m.ends.at[way], s)[...]
    if way == 0:
        first += [links.copy(cut_sum(p), m.got_sum.at[s], (p, b)) for p in peers]
        m.got_sum[s] = cut_sum(s)[...]
    yield
    for c in first:
        c.wait_recv()
    if way == 0:
        a2 = cut(m.a2, s)[...]
        for p in range(count):
            m.tile_dec[p] = jnp.exp2(a2 * m.got_sum[p])
    value = jnp.zeros((8, width), f32)
    for p in reversed(range(count)) if way else range(count):
        m.back[p, way] = value
        value = m.got[p, way] + m.tile_dec[p] * value
    second = [links.copy(m.back.at[p, way], cut(m.edges.at[way], s), (p, b)) for p in peers]
    cut(m.edges.at[way], s)[...] = m.back[s, way]
    links.sent(*first)
    yield
    for c in second:
        c.wait_recv()
    links.sent(*second)


def wide(tile, width=SCAN):
    return jnp.concatenate([tile] * (width // LANES), axis=1)


def spread(row, n):
    return jnp.broadcast_to(row, (n, row.shape[1]))


def fold(value):
    return sum(value[:, k : k + LANES] for k in range(0, value.shape[1], LANES))


def scan_ends(m, lanes):
    a2 = m.a2[:, lanes]
    n = a2.shape[0]

    def chunk(i, h):
        at = pl.ds(pl.multiple_of(i * 8, 8), 8)
        s8, u8 = m.step[at, lanes], m.u[at, lanes]
        for j in range(8):
            b = wide(m.bb[pl.ds(pl.multiple_of((i * 8 + j) * n, 8), n)])
            h = jnp.exp2(spread(s8[j : j + 1], n) * a2) * h + spread(u8[j : j + 1], n) * b
        return h

    m.ends[0, :, lanes] = lax.fori_loop(0, m.step.shape[0] // 8, chunk, jnp.zeros_like(a2))


def scan_lams(m, lanes):
    a2 = m.a2[:, lanes]
    n = a2.shape[0]

    def chunk(i, held):
        dec, acc = held
        at = pl.ds(pl.multiple_of(i * 8, 8), 8)
        s8, d8 = m.step[at, lanes], m.d_res[at, lanes]
        for j in range(8):
            c = wide(m.cc[pl.ds(pl.multiple_of((i * 8 + j) * n, 8), n)])
            dec = dec * jnp.exp2(spread(s8[j : j + 1], n) * a2)
            acc = acc + dec * (spread(d8[j : j + 1], n) * c)
        return dec, acc

    zero = jnp.zeros_like(a2)
    m.ends[1, :, lanes] = lax.fori_loop(0, m.step.shape[0] // 8, chunk, (zero + 1.0, zero))[1]


def scan_out(m, lanes):
    a2 = m.a2[:, lanes]
    n = a2.shape[0]

    def chunk(i, h):
        at = pl.ds(pl.multiple_of(i * 8, 8), 8)
        s8, u8 = m.step[at, lanes], m.u[at, lanes]
        ys = []
        for j in range(8):
            t = pl.ds(pl.multiple_of((i * 8 + j) * n, 8), n)
            b, c = wide(m.bb[t], a2.shape[1]), wide(m.cc[t], a2.shape[1])
            h = jnp.exp2(spread(s8[j : j + 1], n) * a2) * h + spread(u8[j : j + 1], n) * b
            ys.append(jnp.sum(c * h, axis=0, keepdims=True))
        m.y[at, lanes] = jnp.concatenate(ys, axis=0)
        return h

    lax.fori_loop(0, m.step.shape[0] // 8, chunk, m.edges[0, :, lanes])


def scan_again(m, lanes, first):
    a2 = m.a2[:, lanes]
    n = a2.shape[0]
    tokens = m.step.shape[0]

    def ahead(i, h):
        at = pl.ds(pl.multiple_of(i * 8, 8), 8)
        s8, u8, d8 = m.step[at, lanes], m.u[at, lanes], m.d_res[at, lanes]
        for j in range(8):
            t = pl.ds(pl.multiple_of((i * 8 + j) * n, 8), n)
            m.h[i * 8 + j] = h
            h = jnp.exp2(spread(s8[j : j + 1], n) * a2) * h + spread(u8[j : j + 1], n) * wide(m.bb[t])
            part = fold(spread(d8[j : j + 1], n) * h)
            m.cg[t] = part if first else m.cg[t] + part
        return h

    lax.fori_loop(0, tokens // 8, ahead, m.edges[0, :, lanes])


def scan_back(m, lanes, first):
    a2 = m.a2[:, lanes]
    n = a2.shape[0]
    tokens = m.step.shape[0]

    def behind(i, held):
        q, rate = held
        r = tokens // 8 - 1 - i
        at = pl.ds(pl.multiple_of(r * 8, 8), 8)
        s8, u8, d8 = m.step[at, lanes], m.u[at, lanes], m.d_res[at, lanes]
        sg, lb = [None] * 8, [None] * 8
        for j in reversed(range(8)):
            t = pl.ds(pl.multiple_of((r * 8 + j) * n, 8), n)
            st = spread(s8[j : j + 1], n)
            lam = spread(d8[j : j + 1], n) * wide(m.cc[t]) + q
            q = jnp.exp2(st * a2) * lam
            dec = q * m.h[r * 8 + j]
            lb[j] = jnp.sum(lam * wide(m.bb[t]), axis=0, keepdims=True)
            sg[j] = jnp.sum(dec * a2, axis=0, keepdims=True)
            rate = rate + dec * st
            part = fold(lam * spread(u8[j : j + 1], n))
            m.bg[t] = part if first else m.bg[t] + part
        lb8, sg8 = jnp.concatenate(lb, axis=0), jnp.concatenate(sg, axis=0)
        m.sg[at, lanes] = LN2 * sg8 + m.mixed[at, lanes] * lb8
        m.gate[at, lanes] = s8 * lb8
        return q, rate

    _, rate = lax.fori_loop(0, tokens // 8, behind, (m.edges[1, :, lanes], jnp.zeros_like(a2)))
    m.rate[:, lanes] = rate


class Refs:
    pass


FETCH = ["x", "gain", "g", "w_out", "conv_w", "conv_b", "x_proj", "step_proj", "step_b", "code", "a2", "skip"]
ARGS = [v + "_h" for v in FETCH] + ["w_in"]
OUTS = ["block_out", "input_grad", "in_sum", "out_sum", "small_sum", "gain_sum"]


UNITS = ["o0", "o1", "i0", "i1", "x0", "x1"]


def parts(unit):
    return [unit + "ab"[k] for k in range(PARTS.get(unit, 1))]


def recvs(sizes):
    bits, count = log2(sizes["seq"]), sizes["seq"]
    total = 6 + 2 + 3 * len(UNITS) + (5 * (count - 1) if tiled(count) else 2 * bits)
    total += 2 * len(small_plan(sizes)) + sum(halvings(SMALL[0], len(small_plan(sizes))))
    for unit in UNITS:
        for p in parts(unit):
            kept = sum(halvings(LANES * 3 // len(parts(unit)), bits)) - 1
            total += bits + 7 + kept + 3 * {"T1": 0, "T2": kept, "T3": kept - 1}[SPREAD.get(p, "T1")]
    return total


def scratch(sizes, tokens, width, inner, n, rank, taps):
    full = (tokens, inner)
    half, part = inner // 2, width // 2
    stages = log2(sizes["seq"])
    v = lambda *shape: pltpu.VMEM(shape, f32)
    sh = {name: v(*full) for name in ("gate", "d_res", "conv", "mixed", "pre", "step", "u", "y", "d_gate", "sg")}
    sh.update(
        x=v(tokens, width), g=v(tokens, width), vec=v(4, inner), gain=v(width // LANES, LANES),
        conv_b=v(inner // LANES, LANES), step_b=v(inner // LANES, LANES), skip=v(inner // LANES, LANES),
        code=pltpu.VMEM((inner // LANES, LANES), jnp.int32), conv_w=v(taps, inner), x_proj=v(rank + 2 * n, inner),
        step_proj=v(rank, inner), a2=v(n, inner), w_out=v(inner, width),
        normed=v(tokens, width), hid=v(8 + tokens, inner), cgr=v(tokens + 8, inner), proj=v(tokens, LANES),
        wbuf=v(SLOTS, width, WBLOCK), acc=v(tokens, width),
        bb=v(tokens * n, LANES), cc=v(tokens * n, LANES), bg=v(tokens * n, LANES), cg=v(tokens * n, LANES),
        h=v(tokens, n, SCAN), rate=v(n, inner), ends=v(2, n, inner), edges=v(2, n, inner), sums=v(1, inner),
        ng=v(4, tokens, part), gg=v(4, tokens, part),
        gains=v(8, LANES), gains_land=v(landing_rows(8, len(small_plan(sizes))), LANES),
        small=v(*SMALL), small_land=v(landing_rows(SMALL[0], len(small_plan(sizes))), SMALL[1]),
    )
    for unit in UNITS:
        sh["late_" + unit] = v(4, tokens, part)
        for p in parts(unit):
            rows = part // len(parts(unit))
            sh["tile_" + p] = v(rows, part)
            sh["land_" + p] = v(landing_rows(rows, stages), part)
    sh.update(carry_scratch(sizes["seq"], n, inner))
    sh["send"] = pltpu.SemaphoreType.DMA((SENDS,))
    sh["recv"] = pltpu.SemaphoreType.DMA((recvs(sizes),))
    sh["wsem"] = pltpu.SemaphoreType.DMA((SLOTS,))
    sh["isem"] = pltpu.SemaphoreType.DMA((len(FETCH),))
    return sh


def stream(m, first, last):
    def fetch(i, slot):
        cols = pl.ds(mult((first + i) * WBLOCK, WBLOCK), WBLOCK)
        return pltpu.make_async_copy(m.w_in.at[:, cols], m.wbuf.at[slot], m.wsem.at[slot])

    ahead = SLOTS - 1
    for k in range(ahead):
        fetch(k, k).start()

    def run(use):
        def body(i):
            slot = lax.rem(i, SLOTS)
            fetch(i, slot).wait()

            @pl.when(i + ahead < last - first)
            def _():
                fetch(i + ahead, lax.rem(i + ahead, SLOTS)).start()

            use(i, m.wbuf[slot])

        loop(last - first, body)

    return run


def late_chain(place, links, m, unit, value, left, right):
    late = getattr(m, "late_" + unit)
    width = late.shape[2]
    shift = int(unit[1]) * width
    mine = place.y if unit[0] == "o" else place.x
    to, _ = place.near(0, 1, 0) if unit[0] == "o" else place.near(1, 0, 0)
    core, _ = place.near(0, 0, 1)

    def cut(which):
        return value.at[:, pl.ds(mult(which * 2 * width + shift, LANES), width)]

    def pass_on(which):
        slot = late.at[which * 2 + place.c]
        return links.copy(slot, slot, core)

    sent = links.copy(cut(1 - mine), late.at[mine * 2 + place.c], to)
    late[mine * 2 + place.c] = cut(mine)[...]
    passed = [pass_on(mine)]
    yield
    sent.wait_recv()
    passed.append(pass_on(1 - mine))
    yield
    for copy in passed:
        copy.wait_recv()
    links.sent(sent, *passed)
    for i in range(2):
        cell = matmul(left(i), right(i), ((0,), (0,)))
        rows = cell.shape[0] // len(parts(unit))
        for k, p in enumerate(parts(unit)):
            tile = getattr(m, "tile_" + p)
            value = cell[k * rows : (k + 1) * rows]
            tile[...] = value if i == 0 else tile[...] + value


def piece_chain(place, links, m, p, zplan, out, base):
    acc, land = getattr(m, "tile_" + p), getattr(m, "land_" + p)
    rows, cols = acc.shape
    key, shift, r0 = p[0], int(p[1]) * m.x.shape[1] // 2, "ab".index(p[2]) * rows
    part = cols
    half = 2 * part
    bit = ("seq", 0) if key == "o" else ("batch", 1)
    x, y, c = place.x, place.y, place.c
    core, _ = place.near(0, 0, 1)

    def region(at, row, count):
        xx, yy = at
        if key == "o":
            top, side = yy * half + shift + r0 + xx * (rows // 2) + row, c * part
        else:
            top, side = c * part + r0 + yy * (rows // 2) + row, base + xx * half + shift
        return out.at[pl.ds(mult(top, 8), count), pl.ds(mult(side, LANES), cols)]

    kept = []
    off, count = yield from reduce_rows(place, links, [(bit, bit)] + zplan, acc, land, kept)
    edge = kept[0][2]
    place_rows(acc, off, count, lambda row, n: region((x, y), row - edge, n))
    row = off - edge
    held, across = [(x, y)], []

    def give(at, to):
        ref = region(at, row, count)
        return links.copy(ref, ref, to)

    steps = list(reversed(kept[1:]))
    kind = SPREAD.get(p, "T1")
    steps.insert({"T1": len(steps), "T2": 0, "T3": 1}[kind], None)
    for i, step in enumerate(steps):
        last = i == len(steps) - 1
        if step is not None:
            to, parent, _, size = step
            copies = [give(at, to) for at in held]
            yield
            for copy in copies:
                copy.wait_recv()
            links.sent(*copies)
            row, count = parent - edge, 2 * size
            continue
        first, at_a = place.near(1 - c, c, 0)
        second, at_b = place.near(c, 1 - c, 0)
        _, at_d = place.near(1, 1, 0)
        a, b = give((x, y), first), give((x, y), second)
        held = [(x, y), at_a, at_b, at_d]

        def onward(at):
            if last:
                across.append(give(at, core))

        onward((x, y))
        yield
        a.wait_recv()
        d = give(at_a, second)
        onward(at_a)
        yield
        b.wait_recv()
        onward(at_b)
        yield
        d.wait_recv()
        links.sent(a, b)
        onward(at_d)
    if not across:
        across = [give(at, core) for at in held]
    yield
    for copy in across:
        copy.wait_recv()


def block_kernel(sizes, names, *refs):
    m = Refs()
    for name, ref in zip(ARGS + OUTS + names, refs):
        setattr(m, name, ref)
    place = Place(sizes)
    links = Links(m.send, m.recv)
    s, b, c = place.s, place.b, place.c
    count = sizes["seq"]
    tokens, width = m.x.shape
    inner, n = m.a2.shape[1], m.a2.shape[0]
    rank = m.step_proj.shape[0]
    taps = m.conv_w.shape[0]
    half, part = inner // 2, width // 2
    blocks_of_half = inner // WBLOCK
    last = s == count - 1

    fetched = {}
    for i, name in enumerate(FETCH):
        fetched[name] = pltpu.make_async_copy(getattr(m, name + "_h"), getattr(m, name), m.isem.at[i])
    for name in FETCH[:3]:
        fetched[name].start()
    to_hidden = stream(m, 0, blocks_of_half)
    for name in FETCH[3:]:
        fetched[name].start()
    bar = pltpu.get_barrier_semaphore()
    greet = [place.near(*d)[0] for d in GROUP[1:]] + [(p, b) for p in carry_peers(count, s)]
    if not tiled(count):
        greet += [(lax.rem(s + 1, count), b), (lax.rem(s + count - 1, count), b)]
    for to in greet:
        pl.semaphore_signal(bar, inc=1, device_id=to, device_id_type=MESH)

    fetched["x"].wait()
    fetched["gain"].wait()

    def to_row(name, k):
        ref = getattr(m, name)
        for j in range(ref.shape[0]):
            m.vec[k : k + 1, j * LANES : (j + 1) * LANES] = ref[j : j + 1]

    to_row("gain", 3)
    x = m.x[...]
    rms = lax.rsqrt(jnp.mean(x * x, axis=1, keepdims=True) + EPSILON)
    scaled = x * m.vec[3:4, :width]
    m.normed[...] = scaled * rms
    left = stacked(scaled)

    def hidden_block(i, w):
        m.hid[pl.ds(8, tokens), pl.ds(mult(i * WBLOCK, WBLOCK), WBLOCK)] = rms * rows_matmul(left, w, ((1,), (0,)))

    to_hidden(hidden_block)
    to_gate = stream(m, blocks_of_half, 2 * blocks_of_half)
    pl.semaphore_wait(bar, len(greet))
    halo = links.copy(m.hid.at[pl.ds(tokens, 8)], m.hid.at[pl.ds(0, 8)], (lax.rem(s + 1, count), b), start=False)

    @pl.when(jnp.logical_not(last))
    def _():
        halo.start()

    fetched["g"].wait()
    early = []
    for d in GROUP:
        to, _ = place.near(*d)
        cols = pl.ds(mult((c + d[2] * (1 - 2 * c)) * part, LANES), part)
        if not d[1]:
            early.append(links.copy(m.normed.at[:, cols], m.ng.at[place.x * 2 + c], to))
        if not d[0]:
            early.append(links.copy(m.g.at[:, cols], m.gg.at[place.y * 2 + c], to))
    own = pl.ds(mult(c * part, LANES), part)
    m.ng[place.x * 2 + c] = m.normed[:, own]
    m.gg[place.y * 2 + c] = m.g[:, own]


    for name in FETCH[3:]:
        fetched[name].wait()
    m.step_b[...] = m.step_b[...] - 0.5 * m.code[...].astype(f32)
    for k, name in enumerate(("conv_b", "step_b", "skip")):
        to_row(name, k)
    m.a2[...] = -LOG2E * jnp.exp(m.a2[...])
    def convolve(i):
        window = m.hid[pl.ds(mult(i * 8, 8), 16)]
        v = m.vec[0:1]
        for k in range(taps):
            o = 8 - taps + 1 + k
            v = v + m.conv_w[k : k + 1] * window[o : o + 8]
        at = pl.ds(mult(i * 8, 8), 8)
        m.conv[at] = v
        m.mixed[at] = v * sigmoid(v)

    loop(tokens // 8 - 1, lambda i: convolve(i + 1))

    @pl.when(s > 0)
    def _():
        halo.wait_recv()

    @pl.when(s == 0)
    def _():
        m.hid[pl.ds(0, 8)] = jnp.zeros((8, inner), f32)

    convolve(0)

    proj = matmul(m.mixed[...], m.x_proj[...], ((1,), (1,)))
    m.proj[:, : proj.shape[1]] = proj
    for j in range(n):
        at = pl.ds(j, tokens, stride=n)
        m.bb[at] = jnp.broadcast_to(proj[:, rank + j : rank + j + 1], (tokens, LANES))
    low_left = stacked(proj[:, :rank])

    def step_block(i):
        cols = pl.ds(mult(i * WBLOCK, WBLOCK), WBLOCK)
        pre = rows_matmul(low_left, m.step_proj[:, cols], ((1,), (0,))) + m.vec[1:2, cols]
        step = jnp.maximum(pre, 0.0) + jnp.log1p(jnp.exp(-jnp.abs(pre)))
        m.pre[:, cols] = pre
        m.step[:, cols] = step
        m.u[:, cols] = step * m.mixed[:, cols]
        m.sums[:, cols] = jnp.sum(step, axis=0, keepdims=True)

    loop(blocks_of_half, step_block)

    blocks = [slice(k, k + SCAN) for k in range(0, inner, SCAN)]
    for lanes in blocks:
        scan_ends(m, lanes)
    ahead = carry(place, links, m, 0)
    next(ahead)
    g_left = stacked(m.g[...])

    def d_gated_block(i):
        cols = pl.ds(mult(i * WBLOCK, WBLOCK), WBLOCK)
        m.d_res[:, cols] = rows_matmul(g_left, m.w_out[cols], ((1,), (1,)))

    loop(blocks_of_half, d_gated_block)
    for j in range(n):
        at = pl.ds(j, tokens, stride=n)
        m.cc[at] = jnp.broadcast_to(m.proj[:, rank + n + j : rank + n + j + 1], (tokens, LANES))

    def gate_block(i, w):
        cols = pl.ds(mult(i * WBLOCK, WBLOCK), WBLOCK)
        z = rms * rows_matmul(left, w, ((1,), (0,)))
        sg = sigmoid(z)
        act = z * sg
        d = m.d_res[:, cols]
        m.gate[:, cols] = act
        m.d_res[:, cols] = d * act
        m.d_gate[:, cols] = d * (sg * (1.0 + z * (1.0 - sg)))

    to_gate(gate_block)
    next(ahead)
    for lanes in blocks:
        scan_lams(m, lanes)
    behind = carry(place, links, m, 1)
    next(behind)
    for _ in ahead:
        pass
    def finish_quarters(k):
        for first in (k * part, half + k * part):
            cols = slice(first, first + part)
            scan_out(m, cols)

            def rows(i):
                at = pl.ds(mult(i * 8, 8), 8)
                result = m.y[at, cols] + m.vec[2:3, cols] * m.mixed[at, cols]
                m.y[at, cols] = result * m.gate[at, cols]
                m.d_gate[at, cols] = m.d_gate[at, cols] * result

            loop(tokens // 8, rows)

    s_bits, b_bits = all_bits(sizes)
    zplan = [(k, k) for k in s_bits[1:] + b_bits[2:]]
    chains, v = {}, Refs()

    def pair(ref):
        return lambda i: ref[pl.ds(2 * i, 2)].reshape(2 * tokens, ref.shape[2])

    def go(name):
        try:
            next(chains[name])
        except StopIteration:
            del chains[name]
            if name in UNITS:
                where = {"o": (m.out_sum, 0), "i": (m.in_sum, inner), "x": (m.in_sum, 0)}[name[0]]
                for p in parts(name):
                    chains[p] = piece_chain(place, links, m, p, zplan, *where)

    def late(key, value, left, right, which=(0, 1)):
        for unit in (key + str(k) for k in which):
            ref = getattr(m, "late_" + unit)
            chains[unit] = late_chain(place, links, m, unit, value, pair(ref if left is None else left), pair(ref if right is None else right))

    column = lax.broadcasted_iota(jnp.int32, (tokens, LANES), 1)
    zero = jnp.zeros((8, inner), f32)

    def collect(ref, base, total):
        for j in range(n):
            rows = jnp.sum(ref[pl.ds(j, tokens, stride=n)], axis=1, keepdims=True)
            total = total + jnp.where(column == base + j, rows, 0.0)
        return total

    def put_small(row, value):
        rows = value.shape[0]
        cut, top = SMALL[1], 80
        m.small[row : row + rows] = value[:, :cut]
        over = inner - cut
        if row < top:
            m.small[2 * top + row : 2 * top + row + rows, :over] = value[:, cut:]
        else:
            m.small[top + row : top + row + rows, over:] = value[:, cut:]

    def quarters(k):
        finish_quarters(k)
        late("o", m.y, None, m.gg, (k,))
        late("i", m.d_gate, m.ng, None, (k,))
        if k == 0:
            next(behind)

    def again(k):
        scan_again(m, blocks[k], k == 0)

    def back(k):
        if k == 0:
            for _ in behind:
                pass
            for e in early:
                e.wait_recv()
            links.sent(*early)
        scan_back(m, blocks[k], k == 0)

    def pre():
        bc_grad = collect(m.cg, rank + n, collect(m.bg, rank, jnp.zeros((tokens, LANES), f32)))

        def rows(i, total):
            at = pl.ds(pl.multiple_of(i * 8, 8), 8)
            p = m.sg[at] * sigmoid(m.pre[at])
            m.sg[at] = p
            return total[0] + p, total[1] + m.d_res[at] * m.mixed[at]

        total = lax.fori_loop(0, tokens // 8, rows, (zero, zero))
        v.bias_grad, v.skip_grad = (jnp.sum(t, axis=0, keepdims=True) for t in total)
        low_grad = matmul(m.sg[...], m.step_proj[...], ((1,), (1,)))
        v.proj_grad = jnp.concatenate([low_grad, bc_grad[:, rank : rank + 2 * n]], axis=1)

    def mixg():
        pg_left = stacked(v.proj_grad)

        def block(i):
            cols = pl.ds(mult(i * WBLOCK, WBLOCK), WBLOCK)
            d = rows_matmul(pg_left, m.x_proj[:, cols], ((1,), (0,)))
            z = m.conv[:, cols]
            sg = sigmoid(z)
            d = d + m.gate[:, cols] + m.d_res[:, cols] * m.vec[2:3, cols]
            m.cgr[pl.ds(0, tokens), cols] = d * (sg * (1.0 + z * (1.0 - sg)))

        loop(blocks_of_half, block)
        v.halo_back = links.copy(
            m.cgr.at[pl.ds(0, 8)], m.cgr.at[pl.ds(tokens, 8)], (lax.rem(s + count - 1, count), b), start=False)

        @pl.when(s > 0)
        def _():
            v.halo_back.start()

    def xg():
        @pl.when(jnp.logical_not(last))
        def _():
            v.halo_back.wait_recv()

        @pl.when(last)
        def _():
            m.cgr[pl.ds(tokens, 8)] = jnp.zeros((8, inner), f32)

        def rows(i):
            window = m.cgr[pl.ds(mult(i * 8, 8), 16)]
            z = m.conv_w[0:1] * window[taps - 1 : taps + 7]
            for k in range(1, taps):
                o = taps - 1 - k
                z = z + m.conv_w[k : k + 1] * window[o : o + 8]
            m.gate[pl.ds(mult(i * 8, 8), 8)] = z

        loop(tokens // 8, rows)
        late("x", m.gate, m.ng, None)

    def taps_():
        def rows(i, total):
            at = pl.ds(pl.multiple_of(i * 8, 8), 8)
            window = m.hid[pl.ds(pl.multiple_of(i * 8, 8), 16)]
            z = m.cgr[at]
            o = 8 - taps + 1
            return tuple(t + z * window[o + k : o + k + 8] for k, t in enumerate(total[:-1])) + (total[-1] + z,)

        total = lax.fori_loop(0, tokens // 8, rows, (zero,) * (taps + 1))
        v.tap_rows = [jnp.sum(t, axis=0, keepdims=True) for t in total]

    def mid():
        put_small(0, matmul(v.proj_grad, m.mixed[...], ((0,), (0,))))
        put_small(rank + 2 * n, matmul(m.proj[:, :rank], m.sg[...], ((0,), (0,))))
        put_small(2 * rank + 2 * n, m.rate[...] * m.a2[...] * LN2)
        rows = v.tap_rows + [v.bias_grad, v.skip_grad, zero[:1]]
        put_small(2 * rank + 3 * n, jnp.concatenate(rows, axis=0))
        end = 2 * rank + 3 * n + 8
        m.small[end:160] = jnp.zeros((160 - end, SMALL[1]), f32)
        m.small[240:256] = jnp.zeros((16, SMALL[1]), f32)
        m.small[80 + end : 240, SMALL[1] // 2 :] = jnp.zeros((160 - end, SMALL[1] // 2), f32)
        chains["s"] = small_chain(place, links, small_plan(sizes), m.small, m.small_land, m.small_sum)

    def normed_block(ref):
        def use(i, w):
            d = stacked(ref[:, pl.ds(mult(i * WBLOCK, WBLOCK), WBLOCK)])
            m.acc[...] = m.acc[...] + rows_matmul(d, w, ((1,), (1,)))

        return use

    def ng0():
        m.acc[...] = jnp.zeros_like(m.acc)
        stream(m, blocks_of_half, 2 * blocks_of_half)(normed_block(m.d_gate))

    def ng1():
        stream(m, 0, blocks_of_half)(normed_block(m.gate))

    def inp():
        x = m.x[...]
        rms = lax.rsqrt(jnp.mean(x * x, axis=1, keepdims=True) + EPSILON)
        normed_grad = m.acc[...]
        gain_grad = jnp.sum(normed_grad * x * rms, axis=0, keepdims=True)
        weighted = normed_grad * m.vec[3:4, :width]
        m.input_grad[...] = rms * weighted - rms * rms * rms * x * jnp.mean(weighted * x, axis=1, keepdims=True) + m.g[...]
        for k in range(width // LANES):
            m.gains[k : k + 1] = gain_grad[:, k * LANES : (k + 1) * LANES]
        m.gains[width // LANES :] = jnp.zeros((8 - width // LANES, LANES), f32)
        chains["n"] = small_chain(place, links, small_plan(sizes), m.gains, m.gains_land, m.gain_sum)

    def bo():
        gl = stacked(m.y[...])

        def block(i):
            cols = pl.ds(mult(i * WBLOCK, WBLOCK), WBLOCK)
            m.block_out[:, cols] = m.x[:, cols] + rows_matmul(gl, m.w_out[:, cols], ((1,), (0,)))

        loop(width // WBLOCK, block)

    work = {
        "g0": lambda: quarters(0), "g1": lambda: quarters(1), "a0": lambda: again(0), "b0": lambda: back(0), "a1": lambda: again(1), "b1": lambda: back(1),
        "a2": lambda: again(2), "b2": lambda: back(2), "pre": pre, "mixg": mixg,
        "xg": xg, "taps": taps_, "mid": mid, "ng0": ng0, "ng1": ng1, "inp": inp, "bo": bo,
    }
    for name in ORDER:
        if name in work:
            work.pop(name)()
        elif name in chains:
            go(name)
    assert not work
    while chains:
        for name in list(chains):
            go(name)

    @pl.when(jnp.logical_not(last))
    def _():
        halo.wait_send()

    @pl.when(s > 0)
    def _():
        v.halo_back.wait_send()

    links.drain()


def unpack_kernel(rank, n, a_v, b_v, c_v, d_v, small, gains, a_o, b_o, c_o, d_o, x_proj_o, step_proj_o, decay_o, taps_o, *rest):
    row_os, sems = rest[:-1], rest[-1]
    copies = []
    for v, o, cuts in ((c_v, c_o, 8), (d_v, d_o, 4), (a_v, a_o, 1), (b_v, b_o, 1)):
        rows = v.shape[0] // cuts
        for k in range(cuts):
            at = pl.ds(k * rows, rows)
            copies.append(pltpu.make_async_copy(v.at[at], o.at[at], sems.at[len(copies)]))
    for c in copies:
        c.start()

    def take(row, rows):
        over = SMALL[1] // 2
        if row < 80:
            tail = small[160 + row : 160 + row + rows, :over]
        else:
            tail = small[80 + row : 80 + row + rows, over:]
        return jnp.concatenate([small[row : row + rows], tail], axis=1)

    x_proj_o[...] = take(0, rank + 2 * n)
    step_proj_o[...] = take(rank + 2 * n, rank)
    decay_o[...] = take(2 * rank + 2 * n, n)
    rows = take(2 * rank + 3 * n, 8)
    taps = taps_o.shape[0]
    taps_o[...] = rows[:taps]
    row_os[3][...] = gains[: row_os[3].shape[0]]
    for k, ref in enumerate(row_os[:3]):
        for j in range(ref.shape[0]):
            ref[j : j + 1] = rows[taps + k : taps + k + 1, j * LANES : (j + 1) * LANES]
    for c in copies:
        c.wait()


VMEM = pl.BlockSpec(memory_space=pltpu.VMEM)
ANY = pl.BlockSpec(memory_space=pl.ANY)


def shards(sizes, inputs, norm_gain, w_in, conv_weight, conv_bias, x_proj, step_proj, step_bias, decay_code, decay_log,
           skip_gain, w_out, cotangent):
    seqs, tokens, width = inputs.shape
    assert seqs == 1 and sizes["batch"] == 4 and sizes["seq"] % 2 == 0
    inner = w_in.shape[1] // 2
    rank, n, taps = step_proj.shape[0], decay_log.shape[1], conv_weight.shape[0]
    sh = scratch(sizes, tokens, width, inner, n, rank, taps)
    tall = lambda u: u.reshape(-1, LANES)
    args = dict(
        x=inputs[0], g=cotangent[0], gain=tall(norm_gain), conv_w=conv_weight, conv_b=tall(conv_bias), x_proj=x_proj.T,
        step_proj=step_proj, step_b=tall(step_bias), code=tall(decay_code), a2=decay_log.T, skip=tall(skip_gain), w_out=w_out)
    held = [pltpu.VMEM(v, f32) for v in ((tokens, width), (tokens, width), (width, 2 * inner), (inner, width), SMALL, (8, LANES))]
    sums = pl.pallas_call(
        functools.partial(block_kernel, sizes, list(sh)),
        in_specs=[ANY] * len(ARGS),
        out_specs=[VMEM] * 6,
        out_shape=held,
        scratch_shapes=list(sh.values()),
        compiler_params=pltpu.CompilerParams(collective_id=1, has_side_effects=True, vmem_limit_bytes=VLIMIT << 19),
        name="block",
    )(*(args[a] for a in FETCH), w_in)
    wanted = [v.shape for v in sums[:4]] + [(rank + 2 * n, inner), (rank, inner), (n, inner), (taps, inner)]
    wanted += [(inner // LANES, LANES)] * 3 + [(width // LANES, LANES)]
    block_out, input_grad, in_sum, out_sum, x_proj_sum, step_proj_sum, decay_sum, taps_sum, *rows = pl.pallas_call(
        functools.partial(unpack_kernel, rank, n),
        in_specs=[VMEM] * 6,
        out_specs=[ANY] * 4 + [VMEM] * 8,
        out_shape=[jax.ShapeDtypeStruct(v, f32) for v in wanted],
        scratch_shapes=[pltpu.SemaphoreType.DMA((14,))],
        compiler_params=pltpu.CompilerParams(vmem_limit_bytes=VLIMIT2 << 19),
        name="unpack",
    )(*sums)
    conv_b_sum, step_b_sum, skip_sum, gain_sum = (v.reshape(-1) for v in rows)
    return (block_out[None], input_grad[None], gain_sum, in_sum, taps_sum, conv_b_sum, x_proj_sum.T, step_proj_sum, step_b_sum,
            decay_sum.T, skip_sum, out_sum)


VLIMIT, VLIMIT2 = 97, 16


def solution(mesh):
    rows = P("batch", "seq", None)
    return jax.shard_map(
        functools.partial(shards, dict(mesh.shape)),
        mesh=mesh,
        in_specs=(rows,) + (P(),) * 11 + (rows,),
        out_specs=(rows, rows) + (P(),) * 10,
        check_vma=False,
    )
```

```python
import functools

import jax
import jax.numpy as jnp
from jax import lax
from jax.experimental import pallas as pl
from jax.experimental.pallas import tpu as pltpu
from jax.sharding import PartitionSpec as P

f32 = jnp.float32
bf16 = jnp.bfloat16
MESH = pl.DeviceIdType.MESH
EPSILON = 1e-05
LOG2E = 1.4426950408889634
LN2 = 0.6931471805599453
LANES = 128
SCAN = 512
WBLOCK = 256
SLOTS = 4
SMALL = (256, 1024)
PARTS = {"o0": 2, "o1": 2, "i0": 2, "x0": 2, "x1": 2}
SPREAD = {"o1a": "T3", "x0b": "T3", "x1b": "T3"}
SENDS = 72
ORDER = [
    "g0", "o0", "i0", "g1", "a0", "i1", "o1", "b0", "a1", "o0", "i0", "b1", "o0", "i0", "i0a", "o0b",
    "a2", "o0a", "i0b", "o1", "b2", "pre", "mixg", "i1", "o1", "o1a", "o0b", "i1", "i1a", "o0a", "xg", "x1",
    "i0b", "taps", "o0b", "o1a", "mid", "o0a", "s", "i0a", "x0", "i0b", "x1", "s", "i1a", "o0b", "x1", "o0a",
    "x1a", "o1b", "i0b", "o0b", "x0", "i0a", "x1b", "o0a", "o1a", "x0", "x0b", "x1a", "i0b", "o0b", "x1b", "i0a",
    "x0a", "s", "o1a", "i1a", "ng0", "o1b", "i0a", "o0a", "x1a", "o1a", "i0b", "x1b", "x0b", "i1a", "ng1", "x0a",
    "i0a", "s", "x1b", "x0b", "o1a", "inp", "i1a", "x1a", "o0a", "o1b", "o0b", "n", "i0b", "bo", "x0a", "o1a",
    "x1b", "i0a", "n", "x0b", "x1a", "o1b", "o1a", "i1a", "x0a", "s", "o1b", "x0b", "x1b", "n", "s", "x1b",
    "i0a", "o0b", "i0b", "x0a", "x1a", "s", "x0b", "x1b", "o1b", "x0b", "i0a", "x0a", "o0b", "s", "i0b", "x1a",
    "o0b", "x0b", "i1a", "o1b", "o0a", "n", "o1a", "x1a", "o0a", "i1a", "n", "x1b", "o1b", "s", "o1b", "i0b",
    "x1a", "x0b", "o1a", "x0a", "i0a", "i1a", "n", "o1b", "o0a", "x0a", "s", "i1a", "x0b", "x0a", "s", "x1a",
    "x1b", "x0a",
]


def mult(value, by):
    return value if isinstance(value, int) else pl.multiple_of(value, by)


def split(value):
    high = value.astype(bf16)
    return high, (value - high.astype(f32)).astype(bf16)


def dot(a, b, dims):
    return lax.dot_general(a, b, (dims, ((), ())), preferred_element_type=f32)


def matmul(a, b, dims=((1,), (0,))):
    (ah, al), (bh, bl) = split(a), split(b)
    return dot(ah, bh, dims) + dot(al, bh, dims) + dot(ah, bl, dims)


def stacked(value):
    return jnp.concatenate(split(value), axis=0)


def rows_matmul(both, b, dims):
    rows = both.shape[0] // 2
    bh, bl = split(b)
    wide = dot(both, bh, dims)
    return wide[:rows] + wide[rows:] + dot(both[:rows], bl, dims)


def sigmoid(v):
    return 1.0 / (1.0 + jnp.exp(-v))


def loop(count, body):
    def step(i, _):
        body(i)
        return 0

    lax.fori_loop(0, count, step, 0)


class Place:
    def __init__(self, sizes):
        self.sizes = sizes
        self.s, self.b = lax.axis_index("seq"), lax.axis_index("batch")
        self.at = {"seq": self.s, "batch": self.b}
        self.x, self.c, self.y = self.s % 2, self.b % 2, self.b // 2
        self.odd = self.c

    def near(self, dx, dy, dc):
        dx, dy = dx * (1 - 2 * self.x), dy * (1 - 2 * self.y)
        return (self.s + dx, self.b + dc * (1 - 2 * self.c) + 2 * dy), (self.x + dx, self.y + dy)

    def bit(self, d):
        return self.at[d[0]] // (1 << d[1]) % 2

    def stage(self, pair):
        to = dict(self.at)
        first, second = pair
        if first == second:
            v = self.bit(first)
            to[first[0]] = to[first[0]] + (1 - 2 * v) * (1 << first[1])
        else:
            va, vb = self.bit(first), self.bit(second)
            to[first[0]] = to[first[0]] + (1 - self.odd) * (1 - 2 * va) * (1 << first[1])
            to[second[0]] = to[second[0]] + self.odd * (1 - 2 * vb) * (1 << second[1])
            v = (1 - self.odd) * va + self.odd * vb
        return (to["seq"], to["batch"]), v


class Links:
    def __init__(self, send, recv):
        self.send, self.recv, self.used, self.made, self.free, self.open = send, recv, 0, 0, [], []

    def group(self):
        self.used += 1
        return self.used - 1

    def copy(self, src, dst, to, start=True, group=None):
        i = self.group() if group is None else group
        if self.free:
            k = self.free.pop()
        else:
            k = self.made
            self.made += 1
        assert self.used <= self.recv.shape[0] and self.made <= self.send.shape[0]
        c = pltpu.make_async_remote_copy(
            src_ref=src, dst_ref=dst, send_sem=self.send.at[k], recv_sem=self.recv.at[i], device_id=to, device_id_type=MESH
        )
        if start:
            c.start()
            self.open.append((c, k))
        return c

    def take(self, like, group):
        pltpu.make_async_copy(like, like, self.recv.at[group]).wait()

    def sent(self, *copies):
        for copy in copies:
            copy.wait_send()
            self.free += [k for c, k in self.open if c is copy]
            self.open = [(c, k) for c, k in self.open if c is not copy]

    def drain(self):
        self.sent(*(c for c, _ in self.open))


GROUP = [(1, 0, 0), (1, 0, 1), (0, 1, 0), (0, 1, 1), (0, 0, 1)]


def log2(size):
    return size.bit_length() - 1


def all_bits(sizes):
    s = [("seq", k) for k in range(log2(sizes["seq"]))]
    b = [("batch", k) for k in range(log2(sizes["batch"]))]
    return s, b


def small_plan(sizes):
    s, b = all_bits(sizes)
    return [(b[0], b[0]), (s[0], b[1]), (b[1], s[0])] + [(q, q) for q in s[1:] + b[2:]]


def halvings(rows, stages):
    out = []
    for _ in range(stages):
        ok = rows % 16 == 0
        out.append(ok)
        rows = rows // 2 if ok else rows
    return out


def landing_rows(rows, stages):
    total = 0
    for ok in halvings(rows, stages):
        rows = rows // 2 if ok else rows
        total += rows
    return total


def reduce_rows(place, links, plan, acc, land, kept):
    rows = acc.shape[0]
    off, base, before = 0, 0, []
    for pair, ok in zip(plan, halvings(rows, len(plan))):
        to, v = place.stage(pair)
        parent = off
        if ok:
            rows //= 2
            off, give = off + v * rows, off + (1 - v) * rows
        else:
            give = off
        copy = links.copy(acc.at[pl.ds(mult(give, 8), rows)], land.at[pl.ds(base, rows)], to)
        yield
        copy.wait_recv()
        links.sent(*before)
        before = [copy]
        if not ok:
            links.sent(copy)
            before = []

        def add(i, off=off, base=base):
            at = pl.ds(mult(off + i * 8, 8), 8)
            acc[at] = acc[at] + land[pl.ds(mult(base + i * 8, 8), 8)]

        loop(rows // 8, add)
        base += rows
        if ok:
            kept.append((to, parent, off, rows))
    links.sent(*before)
    return off, rows


def place_rows(acc, off, rows, whole):
    def one(i):
        whole(off + i * 8, 8)[...] = acc[pl.ds(mult(off + i * 8, 8), 8)]

    loop(rows // 8, one)


def small_chain(place, links, plan, acc, land, out):
    whole = lambda row, rows: out.at[pl.ds(mult(row, 8), rows)]
    kept = []
    off, rows = yield from reduce_rows(place, links, plan, acc, land, kept)
    place_rows(acc, off, rows, whole)
    for to, _, off, rows in reversed(kept):
        copy = links.copy(whole(off, rows), whole(off, rows), to)
        yield
        copy.wait_recv()


def tiled(count):
    return count in (2, 4, 6, 8, 12, 24)


def carry_peers(count, s):
    if tiled(count):
        return [lax.rem(s + i, count) for i in range(1, count)]
    return [s + (1 - 2 * (s // (1 << k) % 2)) * (1 << k) for k in range(log2(count))]


def carry_scratch(count, n, inner):
    v = lambda *shape: pltpu.VMEM(shape, f32)
    if tiled(count):
        w = inner // (count // 2)
        return dict(got=v(count, 2, 8, w), back=v(count, 2, 8, w), got_sum=v(count, 1, w), tile_dec=v(count, 8, w))
    return dict(got=v(2 * log2(count), 2, n, inner), back=v(2, n, inner), tot=v(2, n, inner))


def carry(place, links, m, way):
    return (carry_tiles if tiled(place.sizes["seq"]) else carry_doubling)(place, links, m, way)


def carry_doubling(place, links, m, way):
    bits = log2(place.sizes["seq"])
    m.edges[way] = jnp.zeros_like(m.edges[way])
    m.back[way] = jnp.ones_like(m.back[way])
    m.tot[0] = m.ends[way]
    m.tot[1] = jnp.exp2(m.a2[...] * m.sums[...])
    for k, p in enumerate(carry_peers(place.sizes["seq"], place.s)):
        got = m.got.at[way * bits + k]
        copy = links.copy(m.tot, got, (p, place.b))
        copy.wait_recv()
        links.sent(copy)
        later = place.bit(("seq", k))

        @pl.when(later == 1 - way)
        def _():
            m.edges[way] += m.back[way] * got[0]
            m.back[way] *= got[1]
            m.tot[0] += m.tot[1] * got[0]

        @pl.when(later == way)
        def _():
            m.tot[0] = got[0] + got[1] * m.tot[0]

        m.tot[1] *= got[1]
    yield
    yield


def carry_tiles(place, links, m, way):
    count, s, b = place.sizes["seq"], place.s, place.b
    across = count // 2
    width = m.ends.shape[2] // across
    peers = carry_peers(count, s)

    def cut(ref, p):
        return ref.at[pl.ds(mult(p // across * 8, 8), 8), pl.ds(mult(p % across * width, LANES), width)]

    def cut_sum(p):
        return m.sums.at[:, pl.ds(mult(p % across * width, LANES), width)]

    one, two, three = links.group(), links.group(), links.group()
    others = pl.ds(0, count - 1)
    first = [links.copy(cut(m.ends.at[way], p), m.got.at[s, way], (p, b), group=one) for p in peers]
    m.got[s, way] = cut(m.ends.at[way], s)[...]
    if way == 0:
        first += [links.copy(cut_sum(p), m.got_sum.at[s], (p, b), group=three) for p in peers]
        m.got_sum[s] = cut_sum(s)[...]
    yield
    links.take(m.got.at[others, way], one)
    if way == 0:
        links.take(m.got_sum.at[others], three)
        a2 = cut(m.a2, s)[...]
        for p in range(count):
            m.tile_dec[p] = jnp.exp2(a2 * m.got_sum[p])
    value = jnp.zeros((8, width), f32)
    for p in reversed(range(count)) if way else range(count):
        m.back[p, way] = value
        value = m.got[p, way] + m.tile_dec[p] * value
    second = [links.copy(m.back.at[p, way], cut(m.edges.at[way], s), (p, b), group=two) for p in peers]
    cut(m.edges.at[way], s)[...] = m.back[s, way]
    links.sent(*first)
    yield
    links.take(m.back.at[others, way], two)
    links.sent(*second)


def wide(tile, width=SCAN):
    return jnp.concatenate([tile] * (width // LANES), axis=1)


def spread(row, n):
    return jnp.broadcast_to(row, (n, row.shape[1]))


def fold(value):
    return sum(value[:, k : k + LANES] for k in range(0, value.shape[1], LANES))


def scan_ends(m, lanes):
    a2 = m.a2[:, lanes]
    n = a2.shape[0]

    def chunk(i, h):
        at = pl.ds(pl.multiple_of(i * 8, 8), 8)
        s8, u8 = m.step[at, lanes], m.u[at, lanes]
        for j in range(8):
            b = wide(m.bb[pl.ds(pl.multiple_of((i * 8 + j) * n, 8), n)])
            h = jnp.exp2(spread(s8[j : j + 1], n) * a2) * h + spread(u8[j : j + 1], n) * b
        return h

    m.ends[0, :, lanes] = lax.fori_loop(0, m.step.shape[0] // 8, chunk, jnp.zeros_like(a2))


def scan_lams(m, lanes):
    a2 = m.a2[:, lanes]
    n = a2.shape[0]

    def chunk(i, held):
        dec, acc = held
        at = pl.ds(pl.multiple_of(i * 8, 8), 8)
        s8, d8 = m.step[at, lanes], m.d_res[at, lanes]
        for j in range(8):
            c = wide(m.cc[pl.ds(pl.multiple_of((i * 8 + j) * n, 8), n)])
            dec = dec * jnp.exp2(spread(s8[j : j + 1], n) * a2)
            acc = acc + dec * (spread(d8[j : j + 1], n) * c)
        return dec, acc

    zero = jnp.zeros_like(a2)
    m.ends[1, :, lanes] = lax.fori_loop(0, m.step.shape[0] // 8, chunk, (zero + 1.0, zero))[1]


def scan_out(m, lanes):
    a2 = m.a2[:, lanes]
    n = a2.shape[0]

    def chunk(i, h):
        at = pl.ds(pl.multiple_of(i * 8, 8), 8)
        s8, u8 = m.step[at, lanes], m.u[at, lanes]
        ys = []
        for j in range(8):
            t = pl.ds(pl.multiple_of((i * 8 + j) * n, 8), n)
            b, c = wide(m.bb[t], a2.shape[1]), wide(m.cc[t], a2.shape[1])
            h = jnp.exp2(spread(s8[j : j + 1], n) * a2) * h + spread(u8[j : j + 1], n) * b
            ys.append(jnp.sum(c * h, axis=0, keepdims=True))
        m.y[at, lanes] = jnp.concatenate(ys, axis=0)
        return h

    lax.fori_loop(0, m.step.shape[0] // 8, chunk, m.edges[0, :, lanes])


def scan_again(m, lanes, first):
    a2 = m.a2[:, lanes]
    n = a2.shape[0]
    tokens = m.step.shape[0]

    def ahead(i, h):
        at = pl.ds(pl.multiple_of(i * 8, 8), 8)
        s8, u8, d8 = m.step[at, lanes], m.u[at, lanes], m.d_res[at, lanes]
        for j in range(8):
            t = pl.ds(pl.multiple_of((i * 8 + j) * n, 8), n)
            m.h[i * 8 + j] = h
            h = jnp.exp2(spread(s8[j : j + 1], n) * a2) * h + spread(u8[j : j + 1], n) * wide(m.bb[t])
            part = fold(spread(d8[j : j + 1], n) * h)
            m.cg[t] = part if first else m.cg[t] + part
        return h

    lax.fori_loop(0, tokens // 8, ahead, m.edges[0, :, lanes])


def scan_back(m, lanes, first):
    a2 = m.a2[:, lanes]
    n = a2.shape[0]
    tokens = m.step.shape[0]

    def behind(i, held):
        q, rate = held
        r = tokens // 8 - 1 - i
        at = pl.ds(pl.multiple_of(r * 8, 8), 8)
        s8, u8, d8 = m.step[at, lanes], m.u[at, lanes], m.d_res[at, lanes]
        sg, lb = [None] * 8, [None] * 8
        for j in reversed(range(8)):
            t = pl.ds(pl.multiple_of((r * 8 + j) * n, 8), n)
            st = spread(s8[j : j + 1], n)
            lam = spread(d8[j : j + 1], n) * wide(m.cc[t]) + q
            q = jnp.exp2(st * a2) * lam
            dec = q * m.h[r * 8 + j]
            lb[j] = jnp.sum(lam * wide(m.bb[t]), axis=0, keepdims=True)
            sg[j] = jnp.sum(dec * a2, axis=0, keepdims=True)
            rate = rate + dec * st
            part = fold(lam * spread(u8[j : j + 1], n))
            m.bg[t] = part if first else m.bg[t] + part
        lb8, sg8 = jnp.concatenate(lb, axis=0), jnp.concatenate(sg, axis=0)
        m.sg[at, lanes] = LN2 * sg8 + m.mixed[at, lanes] * lb8
        m.gate[at, lanes] = s8 * lb8
        return q, rate

    _, rate = lax.fori_loop(0, tokens // 8, behind, (m.edges[1, :, lanes], jnp.zeros_like(a2)))
    m.rate[:, lanes] = rate


class Refs:
    pass


FETCH = ["x", "gain", "g", "w_out", "conv_w", "conv_b", "x_proj", "step_proj", "step_b", "code", "a2", "skip"]
ARGS = [v + "_h" for v in FETCH] + ["w_in"]
OUTS = ["block_out", "input_grad", "in_sum", "out_sum", "small_sum", "gain_sum"]


UNITS = ["o0", "o1", "i0", "i1", "x0", "x1"]


def parts(unit):
    return [unit + "ab"[k] for k in range(PARTS.get(unit, 1))]


def recvs(sizes):
    bits, count = log2(sizes["seq"]), sizes["seq"]
    total = 2 + 2 + 2 * len(UNITS) + (6 if tiled(count) else 2 * bits)
    total += 2 * len(small_plan(sizes)) + sum(halvings(SMALL[0], len(small_plan(sizes))))
    for unit in UNITS:
        for p in parts(unit):
            total += bits + 4 + sum(halvings(LANES * 3 // len(parts(unit)), bits)) - 1
    return total


def scratch(sizes, tokens, width, inner, n, rank, taps):
    full = (tokens, inner)
    half, part = inner // 2, width // 2
    stages = log2(sizes["seq"])
    v = lambda *shape: pltpu.VMEM(shape, f32)
    sh = {name: v(*full) for name in ("gate", "d_res", "conv", "mixed", "pre", "step", "u", "y", "d_gate", "sg")}
    sh.update(
        x=v(tokens, width), g=v(tokens, width), vec=v(4, inner), gain=v(width // LANES, LANES),
        conv_b=v(inner // LANES, LANES), step_b=v(inner // LANES, LANES), skip=v(inner // LANES, LANES),
        code=pltpu.VMEM((inner // LANES, LANES), jnp.int32), conv_w=v(taps, inner), x_proj=v(rank + 2 * n, inner),
        step_proj=v(rank, inner), a2=v(n, inner), w_out=v(inner, width),
        normed=v(tokens, width), hid=v(8 + tokens, inner), cgr=v(tokens + 8, inner), proj=v(tokens, LANES),
        wbuf=v(SLOTS, width, WBLOCK), acc=v(tokens, width),
        bb=v(tokens * n, LANES), cc=v(tokens * n, LANES), bg=v(tokens * n, LANES), cg=v(tokens * n, LANES),
        h=v(tokens, n, SCAN), rate=v(n, inner), ends=v(2, n, inner), edges=v(2, n, inner), sums=v(1, inner),
        ng=v(4, tokens, part), gg=v(4, tokens, part),
        gains=v(8, LANES), gains_land=v(landing_rows(8, len(small_plan(sizes))), LANES),
        small=v(*SMALL), small_land=v(landing_rows(SMALL[0], len(small_plan(sizes))), SMALL[1]),
    )
    for unit in UNITS:
        sh["late_" + unit] = v(4, tokens, part)
        for p in parts(unit):
            rows = part // len(parts(unit))
            sh["tile_" + p] = v(rows, part)
            sh["land_" + p] = v(landing_rows(rows, stages), part)
    sh.update(carry_scratch(sizes["seq"], n, inner))
    sh["send"] = pltpu.SemaphoreType.DMA((SENDS,))
    sh["recv"] = pltpu.SemaphoreType.DMA((recvs(sizes),))
    sh["wsem"] = pltpu.SemaphoreType.DMA((SLOTS,))
    sh["isem"] = pltpu.SemaphoreType.DMA((len(FETCH),))
    return sh


def stream(m, first, last):
    def fetch(i, slot):
        cols = pl.ds(mult((first + i) * WBLOCK, WBLOCK), WBLOCK)
        return pltpu.make_async_copy(m.w_in.at[:, cols], m.wbuf.at[slot], m.wsem.at[slot])

    ahead = SLOTS - 1
    for k in range(ahead):
        fetch(k, k).start()

    def run(use):
        def body(i):
            slot = lax.rem(i, SLOTS)
            fetch(i, slot).wait()

            @pl.when(i + ahead < last - first)
            def _():
                fetch(i + ahead, lax.rem(i + ahead, SLOTS)).start()

            use(i, m.wbuf[slot])

        loop(last - first, body)

    return run


def late_chain(place, links, m, unit, value, left, right):
    late = getattr(m, "late_" + unit)
    width = late.shape[2]
    shift = int(unit[1]) * width
    mine = place.y if unit[0] == "o" else place.x
    to, _ = place.near(0, 1, 0) if unit[0] == "o" else place.near(1, 0, 0)
    core, _ = place.near(0, 0, 1)
    both = links.group()

    def cut(which):
        return value.at[:, pl.ds(mult(which * 2 * width + shift, LANES), width)]

    def pass_on(which):
        slot = late.at[which * 2 + place.c]
        return links.copy(slot, slot, core, group=both)

    sent = links.copy(cut(1 - mine), late.at[mine * 2 + place.c], to)
    late[mine * 2 + place.c] = cut(mine)[...]
    passed = [pass_on(mine)]
    yield
    sent.wait_recv()
    passed.append(pass_on(1 - mine))
    yield
    links.take(late.at[pl.ds(0, 2)], both)
    links.sent(sent, *passed)
    for i in range(2):
        cell = matmul(left(i), right(i), ((0,), (0,)))
        rows = cell.shape[0] // len(parts(unit))
        for k, p in enumerate(parts(unit)):
            tile = getattr(m, "tile_" + p)
            value = cell[k * rows : (k + 1) * rows]
            tile[...] = value if i == 0 else tile[...] + value


def piece_chain(place, links, m, p, zplan, out, base):
    acc, land = getattr(m, "tile_" + p), getattr(m, "land_" + p)
    rows, cols = acc.shape
    key, shift, r0 = p[0], int(p[1]) * m.x.shape[1] // 2, "ab".index(p[2]) * rows
    part = cols
    half = 2 * part
    bit = ("seq", 0) if key == "o" else ("batch", 1)
    x, y, c = place.x, place.y, place.c
    core, _ = place.near(0, 0, 1)

    def region(at, row, count):
        xx, yy = at
        if key == "o":
            top, side = yy * half + shift + r0 + xx * (rows // 2) + row, c * part
        else:
            top, side = c * part + r0 + yy * (rows // 2) + row, base + xx * half + shift
        return out.at[pl.ds(mult(top, 8), count), pl.ds(mult(side, LANES), cols)]

    kept = []
    off, count = yield from reduce_rows(place, links, [(bit, bit)] + zplan, acc, land, kept)
    edge = kept[0][2]
    place_rows(acc, off, count, lambda row, n: region((x, y), row - edge, n))
    row = off - edge
    held, across, to_core = [(x, y)], [], links.group()

    def give(at, to, group=None):
        ref = region(at, row, count)
        return links.copy(ref, ref, to, group=group)

    steps = list(reversed(kept[1:]))
    kind = SPREAD.get(p, "T1")
    steps.insert({"T1": len(steps), "T2": 0, "T3": 1}[kind], None)
    for i, step in enumerate(steps):
        last = i == len(steps) - 1
        if step is not None:
            to, parent, _, size = step
            step_copies = links.group()
            copies = [give(at, to, step_copies) for at in held]
            yield
            links.take(out.at[pl.ds(0, len(held) * count), pl.ds(0, cols)], step_copies)
            links.sent(*copies)
            row, count = parent - edge, 2 * size
            continue
        first, at_a = place.near(1 - c, c, 0)
        second, at_b = place.near(c, 1 - c, 0)
        _, at_d = place.near(1, 1, 0)
        a, b = give((x, y), first), give((x, y), second)
        held = [(x, y), at_a, at_b, at_d]

        def onward(at):
            if last:
                across.append(give(at, core, to_core))

        onward((x, y))
        yield
        a.wait_recv()
        d = give(at_a, second)
        onward(at_a)
        yield
        b.wait_recv()
        onward(at_b)
        yield
        d.wait_recv()
        links.sent(a, b)
        onward(at_d)
    if not across:
        across = [give(at, core, to_core) for at in held]
    yield
    links.take(out.at[pl.ds(0, 2 * rows), pl.ds(0, cols)], to_core)


def block_kernel(sizes, names, *refs):
    m = Refs()
    for name, ref in zip(ARGS + OUTS + names, refs):
        setattr(m, name, ref)
    place = Place(sizes)
    links = Links(m.send, m.recv)
    s, b, c = place.s, place.b, place.c
    count = sizes["seq"]
    tokens, width = m.x.shape
    inner, n = m.a2.shape[1], m.a2.shape[0]
    rank = m.step_proj.shape[0]
    taps = m.conv_w.shape[0]
    half, part = inner // 2, width // 2
    blocks_of_half = inner // WBLOCK
    last = s == count - 1

    fetched = {}
    for i, name in enumerate(FETCH):
        fetched[name] = pltpu.make_async_copy(getattr(m, name + "_h"), getattr(m, name), m.isem.at[i])
    for name in FETCH[:3]:
        fetched[name].start()
    to_hidden = stream(m, 0, blocks_of_half)
    for name in FETCH[3:]:
        fetched[name].start()
    bar = pltpu.get_barrier_semaphore()
    greet = [place.near(*d)[0] for d in GROUP[1:]] + [(p, b) for p in carry_peers(count, s)]
    if not tiled(count):
        greet += [(lax.rem(s + 1, count), b), (lax.rem(s + count - 1, count), b)]
    for to in greet:
        pl.semaphore_signal(bar, inc=1, device_id=to, device_id_type=MESH)

    fetched["x"].wait()
    fetched["gain"].wait()

    def to_row(name, k):
        ref = getattr(m, name)
        for j in range(ref.shape[0]):
            m.vec[k : k + 1, j * LANES : (j + 1) * LANES] = ref[j : j + 1]

    to_row("gain", 3)
    x = m.x[...]
    rms = lax.rsqrt(jnp.mean(x * x, axis=1, keepdims=True) + EPSILON)
    scaled = x * m.vec[3:4, :width]
    m.normed[...] = scaled * rms
    left = stacked(scaled)

    def hidden_block(i, w):
        m.hid[pl.ds(8, tokens), pl.ds(mult(i * WBLOCK, WBLOCK), WBLOCK)] = rms * rows_matmul(left, w, ((1,), (0,)))

    to_hidden(hidden_block)
    to_gate = stream(m, blocks_of_half, 2 * blocks_of_half)
    pl.semaphore_wait(bar, len(greet))
    halo = links.copy(m.hid.at[pl.ds(tokens, 8)], m.hid.at[pl.ds(0, 8)], (lax.rem(s + 1, count), b), start=False)

    @pl.when(jnp.logical_not(last))
    def _():
        halo.start()

    fetched["g"].wait()
    early, early_n, early_g = [], links.group(), links.group()
    for d in GROUP:
        to, _ = place.near(*d)
        cols = pl.ds(mult((c + d[2] * (1 - 2 * c)) * part, LANES), part)
        if not d[1]:
            early.append(links.copy(m.normed.at[:, cols], m.ng.at[place.x * 2 + c], to, group=early_n))
        if not d[0]:
            early.append(links.copy(m.g.at[:, cols], m.gg.at[place.y * 2 + c], to, group=early_g))
    own = pl.ds(mult(c * part, LANES), part)
    m.ng[place.x * 2 + c] = m.normed[:, own]
    m.gg[place.y * 2 + c] = m.g[:, own]


    for name in FETCH[3:]:
        fetched[name].wait()
    m.step_b[...] = m.step_b[...] - 0.5 * m.code[...].astype(f32)
    for k, name in enumerate(("conv_b", "step_b", "skip")):
        to_row(name, k)
    m.a2[...] = -LOG2E * jnp.exp(m.a2[...])
    def convolve(i):
        window = m.hid[pl.ds(mult(i * 8, 8), 16)]
        v = m.vec[0:1]
        for k in range(taps):
            o = 8 - taps + 1 + k
            v = v + m.conv_w[k : k + 1] * window[o : o + 8]
        at = pl.ds(mult(i * 8, 8), 8)
        m.conv[at] = v
        m.mixed[at] = v * sigmoid(v)

    loop(tokens // 8 - 1, lambda i: convolve(i + 1))

    @pl.when(s > 0)
    def _():
        halo.wait_recv()

    @pl.when(s == 0)
    def _():
        m.hid[pl.ds(0, 8)] = jnp.zeros((8, inner), f32)

    convolve(0)

    proj = matmul(m.mixed[...], m.x_proj[...], ((1,), (1,)))
    m.proj[:, : proj.shape[1]] = proj
    for j in range(n):
        at = pl.ds(j, tokens, stride=n)
        m.bb[at] = jnp.broadcast_to(proj[:, rank + j : rank + j + 1], (tokens, LANES))
    low_left = stacked(proj[:, :rank])

    def step_block(i):
        cols = pl.ds(mult(i * WBLOCK, WBLOCK), WBLOCK)
        pre = rows_matmul(low_left, m.step_proj[:, cols], ((1,), (0,))) + m.vec[1:2, cols]
        step = jnp.maximum(pre, 0.0) + jnp.log1p(jnp.exp(-jnp.abs(pre)))
        m.pre[:, cols] = pre
        m.step[:, cols] = step
        m.u[:, cols] = step * m.mixed[:, cols]
        m.sums[:, cols] = jnp.sum(step, axis=0, keepdims=True)

    loop(blocks_of_half, step_block)

    blocks = [slice(k, k + SCAN) for k in range(0, inner, SCAN)]
    for lanes in blocks:
        scan_ends(m, lanes)
    ahead = carry(place, links, m, 0)
    next(ahead)
    g_left = stacked(m.g[...])

    def d_gated_block(i):
        cols = pl.ds(mult(i * WBLOCK, WBLOCK), WBLOCK)
        m.d_res[:, cols] = rows_matmul(g_left, m.w_out[cols], ((1,), (1,)))

    loop(blocks_of_half, d_gated_block)
    for j in range(n):
        at = pl.ds(j, tokens, stride=n)
        m.cc[at] = jnp.broadcast_to(m.proj[:, rank + n + j : rank + n + j + 1], (tokens, LANES))

    def gate_block(i, w):
        cols = pl.ds(mult(i * WBLOCK, WBLOCK), WBLOCK)
        z = rms * rows_matmul(left, w, ((1,), (0,)))
        sg = sigmoid(z)
        act = z * sg
        d = m.d_res[:, cols]
        m.gate[:, cols] = act
        m.d_res[:, cols] = d * act
        m.d_gate[:, cols] = d * (sg * (1.0 + z * (1.0 - sg)))

    to_gate(gate_block)
    next(ahead)
    for lanes in blocks:
        scan_lams(m, lanes)
    behind = carry(place, links, m, 1)
    next(behind)
    for _ in ahead:
        pass
    def finish_quarters(k):
        for first in (k * part, half + k * part):
            cols = slice(first, first + part)
            scan_out(m, cols)

            def rows(i):
                at = pl.ds(mult(i * 8, 8), 8)
                result = m.y[at, cols] + m.vec[2:3, cols] * m.mixed[at, cols]
                m.y[at, cols] = result * m.gate[at, cols]
                m.d_gate[at, cols] = m.d_gate[at, cols] * result

            loop(tokens // 8, rows)

    s_bits, b_bits = all_bits(sizes)
    zplan = [(k, k) for k in s_bits[1:] + b_bits[2:]]
    chains, v = {}, Refs()

    def pair(ref):
        return lambda i: ref[pl.ds(2 * i, 2)].reshape(2 * tokens, ref.shape[2])

    def go(name):
        try:
            next(chains[name])
        except StopIteration:
            del chains[name]
            if name in UNITS:
                where = {"o": (m.out_sum, 0), "i": (m.in_sum, inner), "x": (m.in_sum, 0)}[name[0]]
                for p in parts(name):
                    chains[p] = piece_chain(place, links, m, p, zplan, *where)

    def late(key, value, left, right, which=(0, 1)):
        for unit in (key + str(k) for k in which):
            ref = getattr(m, "late_" + unit)
            chains[unit] = late_chain(place, links, m, unit, value, pair(ref if left is None else left), pair(ref if right is None else right))

    column = lax.broadcasted_iota(jnp.int32, (tokens, LANES), 1)
    zero = jnp.zeros((8, inner), f32)

    def collect(ref, base, total):
        for j in range(n):
            rows = jnp.sum(ref[pl.ds(j, tokens, stride=n)], axis=1, keepdims=True)
            total = total + jnp.where(column == base + j, rows, 0.0)
        return total

    def put_small(row, value):
        rows = value.shape[0]
        cut, top = SMALL[1], 80
        m.small[row : row + rows] = value[:, :cut]
        over = inner - cut
        if row < top:
            m.small[2 * top + row : 2 * top + row + rows, :over] = value[:, cut:]
        else:
            m.small[top + row : top + row + rows, over:] = value[:, cut:]

    def quarters(k):
        finish_quarters(k)
        late("o", m.y, None, m.gg, (k,))
        late("i", m.d_gate, m.ng, None, (k,))
        if k == 0:
            next(behind)

    def again(k):
        scan_again(m, blocks[k], k == 0)

    def back(k):
        if k == 0:
            for _ in behind:
                pass
            links.take(m.ng.at[pl.ds(0, 3)], early_n)
            links.take(m.gg.at[pl.ds(0, 3)], early_g)
            links.sent(*early)
        scan_back(m, blocks[k], k == 0)

    def pre():
        bc_grad = collect(m.cg, rank + n, collect(m.bg, rank, jnp.zeros((tokens, LANES), f32)))

        def rows(i, total):
            at = pl.ds(pl.multiple_of(i * 8, 8), 8)
            p = m.sg[at] * sigmoid(m.pre[at])
            m.sg[at] = p
            return total[0] + p, total[1] + m.d_res[at] * m.mixed[at]

        total = lax.fori_loop(0, tokens // 8, rows, (zero, zero))
        v.bias_grad, v.skip_grad = (jnp.sum(t, axis=0, keepdims=True) for t in total)
        low_grad = matmul(m.sg[...], m.step_proj[...], ((1,), (1,)))
        v.proj_grad = jnp.concatenate([low_grad, bc_grad[:, rank : rank + 2 * n]], axis=1)

    def mixg():
        pg_left = stacked(v.proj_grad)

        def block(i):
            cols = pl.ds(mult(i * WBLOCK, WBLOCK), WBLOCK)
            d = rows_matmul(pg_left, m.x_proj[:, cols], ((1,), (0,)))
            z = m.conv[:, cols]
            sg = sigmoid(z)
            d = d + m.gate[:, cols] + m.d_res[:, cols] * m.vec[2:3, cols]
            m.cgr[pl.ds(0, tokens), cols] = d * (sg * (1.0 + z * (1.0 - sg)))

        loop(blocks_of_half, block)
        v.halo_back = links.copy(
            m.cgr.at[pl.ds(0, 8)], m.cgr.at[pl.ds(tokens, 8)], (lax.rem(s + count - 1, count), b), start=False)

        @pl.when(s > 0)
        def _():
            v.halo_back.start()

    def xg():
        @pl.when(jnp.logical_not(last))
        def _():
            v.halo_back.wait_recv()

        @pl.when(last)
        def _():
            m.cgr[pl.ds(tokens, 8)] = jnp.zeros((8, inner), f32)

        def rows(i):
            window = m.cgr[pl.ds(mult(i * 8, 8), 16)]
            z = m.conv_w[0:1] * window[taps - 1 : taps + 7]
            for k in range(1, taps):
                o = taps - 1 - k
                z = z + m.conv_w[k : k + 1] * window[o : o + 8]
            m.gate[pl.ds(mult(i * 8, 8), 8)] = z

        loop(tokens // 8, rows)
        late("x", m.gate, m.ng, None)

    def taps_():
        def rows(i, total):
            at = pl.ds(pl.multiple_of(i * 8, 8), 8)
            window = m.hid[pl.ds(pl.multiple_of(i * 8, 8), 16)]
            z = m.cgr[at]
            o = 8 - taps + 1
            return tuple(t + z * window[o + k : o + k + 8] for k, t in enumerate(total[:-1])) + (total[-1] + z,)

        total = lax.fori_loop(0, tokens // 8, rows, (zero,) * (taps + 1))
        v.tap_rows = [jnp.sum(t, axis=0, keepdims=True) for t in total]

    def mid():
        put_small(0, matmul(v.proj_grad, m.mixed[...], ((0,), (0,))))
        put_small(rank + 2 * n, matmul(m.proj[:, :rank], m.sg[...], ((0,), (0,))))
        put_small(2 * rank + 2 * n, m.rate[...] * m.a2[...] * LN2)
        rows = v.tap_rows + [v.bias_grad, v.skip_grad, zero[:1]]
        put_small(2 * rank + 3 * n, jnp.concatenate(rows, axis=0))
        end = 2 * rank + 3 * n + 8
        m.small[end:160] = jnp.zeros((160 - end, SMALL[1]), f32)
        m.small[240:256] = jnp.zeros((16, SMALL[1]), f32)
        m.small[80 + end : 240, SMALL[1] // 2 :] = jnp.zeros((160 - end, SMALL[1] // 2), f32)
        chains["s"] = small_chain(place, links, small_plan(sizes), m.small, m.small_land, m.small_sum)

    def normed_block(ref):
        def use(i, w):
            d = stacked(ref[:, pl.ds(mult(i * WBLOCK, WBLOCK), WBLOCK)])
            m.acc[...] = m.acc[...] + rows_matmul(d, w, ((1,), (1,)))

        return use

    def ng0():
        m.acc[...] = jnp.zeros_like(m.acc)
        stream(m, blocks_of_half, 2 * blocks_of_half)(normed_block(m.d_gate))

    def ng1():
        stream(m, 0, blocks_of_half)(normed_block(m.gate))

    def inp():
        x = m.x[...]
        rms = lax.rsqrt(jnp.mean(x * x, axis=1, keepdims=True) + EPSILON)
        normed_grad = m.acc[...]
        gain_grad = jnp.sum(normed_grad * x * rms, axis=0, keepdims=True)
        weighted = normed_grad * m.vec[3:4, :width]
        m.input_grad[...] = rms * weighted - rms * rms * rms * x * jnp.mean(weighted * x, axis=1, keepdims=True) + m.g[...]
        for k in range(width // LANES):
            m.gains[k : k + 1] = gain_grad[:, k * LANES : (k + 1) * LANES]
        m.gains[width // LANES :] = jnp.zeros((8 - width // LANES, LANES), f32)
        chains["n"] = small_chain(place, links, small_plan(sizes), m.gains, m.gains_land, m.gain_sum)

    def bo():
        gl = stacked(m.y[...])

        def block(i):
            cols = pl.ds(mult(i * WBLOCK, WBLOCK), WBLOCK)
            m.block_out[:, cols] = m.x[:, cols] + rows_matmul(gl, m.w_out[:, cols], ((1,), (0,)))

        loop(width // WBLOCK, block)

    work = {
        "g0": lambda: quarters(0), "g1": lambda: quarters(1), "a0": lambda: again(0), "b0": lambda: back(0), "a1": lambda: again(1), "b1": lambda: back(1),
        "a2": lambda: again(2), "b2": lambda: back(2), "pre": pre, "mixg": mixg,
        "xg": xg, "taps": taps_, "mid": mid, "ng0": ng0, "ng1": ng1, "inp": inp, "bo": bo,
    }
    for name in ORDER:
        if name in work:
            work.pop(name)()
        elif name in chains:
            go(name)
    assert not work
    while chains:
        for name in list(chains):
            go(name)

    @pl.when(jnp.logical_not(last))
    def _():
        halo.wait_send()

    @pl.when(s > 0)
    def _():
        v.halo_back.wait_send()

    links.drain()


def unpack_kernel(rank, n, a_v, b_v, c_v, d_v, small, gains, a_o, b_o, c_o, d_o, x_proj_o, step_proj_o, decay_o, taps_o, *rest):
    row_os, sems = rest[:-1], rest[-1]
    copies = []
    for v, o, cuts in ((c_v, c_o, 8), (d_v, d_o, 4), (a_v, a_o, 1), (b_v, b_o, 1)):
        rows = v.shape[0] // cuts
        for k in range(cuts):
            at = pl.ds(k * rows, rows)
            copies.append(pltpu.make_async_copy(v.at[at], o.at[at], sems.at[len(copies)]))
    for c in copies:
        c.start()

    def take(row, rows):
        over = SMALL[1] // 2
        if row < 80:
            tail = small[160 + row : 160 + row + rows, :over]
        else:
            tail = small[80 + row : 80 + row + rows, over:]
        return jnp.concatenate([small[row : row + rows], tail], axis=1)

    x_proj_o[...] = take(0, rank + 2 * n)
    step_proj_o[...] = take(rank + 2 * n, rank)
    decay_o[...] = take(2 * rank + 2 * n, n)
    rows = take(2 * rank + 3 * n, 8)
    taps = taps_o.shape[0]
    taps_o[...] = rows[:taps]
    row_os[3][...] = gains[: row_os[3].shape[0]]
    for k, ref in enumerate(row_os[:3]):
        for j in range(ref.shape[0]):
            ref[j : j + 1] = rows[taps + k : taps + k + 1, j * LANES : (j + 1) * LANES]
    for c in copies:
        c.wait()


VMEM = pl.BlockSpec(memory_space=pltpu.VMEM)
ANY = pl.BlockSpec(memory_space=pl.ANY)


def shards(sizes, inputs, norm_gain, w_in, conv_weight, conv_bias, x_proj, step_proj, step_bias, decay_code, decay_log,
           skip_gain, w_out, cotangent):
    seqs, tokens, width = inputs.shape
    assert seqs == 1 and sizes["batch"] == 4 and sizes["seq"] % 2 == 0
    inner = w_in.shape[1] // 2
    rank, n, taps = step_proj.shape[0], decay_log.shape[1], conv_weight.shape[0]
    sh = scratch(sizes, tokens, width, inner, n, rank, taps)
    tall = lambda u: u.reshape(-1, LANES)
    args = dict(
        x=inputs[0], g=cotangent[0], gain=tall(norm_gain), conv_w=conv_weight, conv_b=tall(conv_bias), x_proj=x_proj.T,
        step_proj=step_proj, step_b=tall(step_bias), code=tall(decay_code), a2=decay_log.T, skip=tall(skip_gain), w_out=w_out)
    held = [pltpu.VMEM(v, f32) for v in ((tokens, width), (tokens, width), (width, 2 * inner), (inner, width), SMALL, (8, LANES))]
    sums = pl.pallas_call(
        functools.partial(block_kernel, sizes, list(sh)),
        in_specs=[ANY] * len(ARGS),
        out_specs=[VMEM] * 6,
        out_shape=held,
        scratch_shapes=list(sh.values()),
        compiler_params=pltpu.CompilerParams(collective_id=1, has_side_effects=True, vmem_limit_bytes=VLIMIT << 19),
        name="block",
    )(*(args[a] for a in FETCH), w_in)
    wanted = [v.shape for v in sums[:4]] + [(rank + 2 * n, inner), (rank, inner), (n, inner), (taps, inner)]
    wanted += [(inner // LANES, LANES)] * 3 + [(width // LANES, LANES)]
    block_out, input_grad, in_sum, out_sum, x_proj_sum, step_proj_sum, decay_sum, taps_sum, *rows = pl.pallas_call(
        functools.partial(unpack_kernel, rank, n),
        in_specs=[VMEM] * 6,
        out_specs=[ANY] * 4 + [VMEM] * 8,
        out_shape=[jax.ShapeDtypeStruct(v, f32) for v in wanted],
        scratch_shapes=[pltpu.SemaphoreType.DMA((14,))],
        compiler_params=pltpu.CompilerParams(vmem_limit_bytes=VLIMIT2 << 19),
        name="unpack",
    )(*sums)
    conv_b_sum, step_b_sum, skip_sum, gain_sum = (v.reshape(-1) for v in rows)
    return (block_out[None], input_grad[None], gain_sum, in_sum, taps_sum, conv_b_sum, x_proj_sum.T, step_proj_sum, step_b_sum,
            decay_sum.T, skip_sum, out_sum)


VLIMIT, VLIMIT2 = 97, 16


def solution(mesh):
    rows = P("batch", "seq", None)
    return jax.shard_map(
        functools.partial(shards, dict(mesh.shape)),
        mesh=mesh,
        in_specs=(rows,) + (P(),) * 11 + (rows,),
        out_specs=(rows, rows) + (P(),) * 10,
        check_vma=False,
    )
```

```python
import functools

import jax
import jax.numpy as jnp
from jax import lax
from jax.experimental import pallas as pl
from jax.experimental.pallas import tpu as pltpu
from jax.sharding import PartitionSpec as P

f32 = jnp.float32
bf16 = jnp.bfloat16
MESH = pl.DeviceIdType.MESH
EPSILON = 1e-05
LOG2E = 1.4426950408889634
LN2 = 0.6931471805599453
LANES = 128
SCAN = 512
WBLOCK = 256
SLOTS = 4
SMALL = (256, 1024)
PARTS = {"o0": 2, "i0": 2, "i1": 2, "x0": 2, "x1": 2}
SPREAD = {"i0a": "T3", "x0b": "T3", "x1b": "T2"}
SENDS = 72
ORDER = [
    "g0", "o0", "i0", "g1", "a0", "i1", "o1", "b0", "a1", "i0", "o0", "b1", "i0", "i0b", "o0", "a2",
    "o0b", "i0a", "o1", "b2", "o1", "i1", "o1a", "i0b", "pre", "i0a", "mixg", "o0b", "i1", "o0a", "i1a", "i0b",
    "taps", "o1a", "xg", "x0", "i0a", "i1b", "mid", "s", "o0b", "i0b", "i1a", "ng0", "s", "i0a", "x0", "o0a",
    "o0b", "o1a", "x0", "x0b", "i0b", "x1", "s", "i1a", "i0a", "o0b", "x0a", "o0a", "i1b", "i0b", "o1a", "x0b",
    "ng1", "i1a", "x1", "o0b", "s", "x1", "x0b", "o1a", "x1b", "i1a", "inp", "i0a", "s", "x1a", "x0b", "i0b",
    "x1b", "o0a", "i1b", "i1a", "i0a", "s", "o1a", "x0a", "x1a", "x1b", "i1b", "s", "x0a", "o0a", "x1b", "i0a",
    "i1a", "x1a", "o0b", "x0a", "s", "i1b", "x1b", "o1a", "o0a", "x1b", "x1a", "x0b", "x1b", "s", "o0b", "x0b",
    "i0b", "x1a", "o0a", "o0a", "x0a", "i1a", "n", "n", "o0b", "x1b", "i0a", "i1b", "o1a", "x0a", "n", "bo",
    "x0b", "o1a", "s", "x1a", "o0a", "x0b", "o0a", "x1b", "i1a", "i1b", "n", "x0a", "i1a", "i1b", "x0a", "s",
    "x1a", "x1a", "n", "i0b", "x1b", "i1b", "x0b", "o1a", "o0b", "x0a", "n", "i1b", "i0a", "x1a", "i0b", "x0b",
    "x0a", "x1a",
]


def mult(value, by):
    return value if isinstance(value, int) else pl.multiple_of(value, by)


def split(value):
    high = value.astype(bf16)
    return high, (value - high.astype(f32)).astype(bf16)


def dot(a, b, dims):
    return lax.dot_general(a, b, (dims, ((), ())), preferred_element_type=f32)


def matmul(a, b, dims=((1,), (0,))):
    (ah, al), (bh, bl) = split(a), split(b)
    return dot(ah, bh, dims) + dot(al, bh, dims) + dot(ah, bl, dims)


def stacked(value):
    return jnp.concatenate(split(value), axis=0)


def rows_matmul(both, b, dims):
    rows = both.shape[0] // 2
    bh, bl = split(b)
    wide = dot(both, bh, dims)
    return wide[:rows] + wide[rows:] + dot(both[:rows], bl, dims)


def sigmoid(v):
    return 1.0 / (1.0 + jnp.exp(-v))


def loop(count, body):
    def step(i, _):
        body(i)
        return 0

    lax.fori_loop(0, count, step, 0)


class Place:
    def __init__(self, sizes):
        self.sizes = sizes
        self.s, self.b = lax.axis_index("seq"), lax.axis_index("batch")
        self.at = {"seq": self.s, "batch": self.b}
        self.x, self.c, self.y = self.s % 2, self.b % 2, self.b // 2
        self.odd = self.c

    def near(self, dx, dy, dc):
        dx, dy = dx * (1 - 2 * self.x), dy * (1 - 2 * self.y)
        return (self.s + dx, self.b + dc * (1 - 2 * self.c) + 2 * dy), (self.x + dx, self.y + dy)

    def bit(self, d):
        return self.at[d[0]] // (1 << d[1]) % 2

    def stage(self, pair):
        to = dict(self.at)
        first, second = pair
        if first == second:
            v = self.bit(first)
            to[first[0]] = to[first[0]] + (1 - 2 * v) * (1 << first[1])
        else:
            va, vb = self.bit(first), self.bit(second)
            to[first[0]] = to[first[0]] + (1 - self.odd) * (1 - 2 * va) * (1 << first[1])
            to[second[0]] = to[second[0]] + self.odd * (1 - 2 * vb) * (1 << second[1])
            v = (1 - self.odd) * va + self.odd * vb
        return (to["seq"], to["batch"]), v


class Links:
    def __init__(self, send, recv):
        self.send, self.recv, self.used, self.made, self.free, self.open = send, recv, 0, 0, [], []

    def group(self):
        self.used += 1
        return self.used - 1

    def copy(self, src, dst, to, start=True, group=None):
        i = self.group() if group is None else group
        if self.free:
            k = self.free.pop()
        else:
            k = self.made
            self.made += 1
        assert self.used <= self.recv.shape[0] and self.made <= self.send.shape[0]
        c = pltpu.make_async_remote_copy(
            src_ref=src, dst_ref=dst, send_sem=self.send.at[k], recv_sem=self.recv.at[i], device_id=to, device_id_type=MESH
        )
        if start:
            c.start()
            self.open.append((c, k))
        return c

    def take(self, like, group):
        pltpu.make_async_copy(like, like, self.recv.at[group]).wait()

    def sent(self, *copies):
        for copy in copies:
            copy.wait_send()
            self.free += [k for c, k in self.open if c is copy]
            self.open = [(c, k) for c, k in self.open if c is not copy]

    def drain(self):
        self.sent(*(c for c, _ in self.open))


GROUP = [(1, 0, 0), (1, 0, 1), (0, 1, 0), (0, 1, 1), (0, 0, 1)]


def log2(size):
    return size.bit_length() - 1


def all_bits(sizes):
    s = [("seq", k) for k in range(log2(sizes["seq"]))]
    b = [("batch", k) for k in range(log2(sizes["batch"]))]
    return s, b


def small_plan(sizes):
    s, b = all_bits(sizes)
    return [(b[0], b[0]), (s[0], b[1]), (b[1], s[0])] + [(q, q) for q in s[1:] + b[2:]]


def halvings(rows, stages):
    out = []
    for _ in range(stages):
        ok = rows % 16 == 0
        out.append(ok)
        rows = rows // 2 if ok else rows
    return out


def landing_rows(rows, stages):
    total = 0
    for ok in halvings(rows, stages):
        rows = rows // 2 if ok else rows
        total += rows
    return total


def reduce_rows(place, links, plan, acc, land, kept):
    rows = acc.shape[0]
    off, base, before = 0, 0, []
    for pair, ok in zip(plan, halvings(rows, len(plan))):
        to, v = place.stage(pair)
        parent = off
        if ok:
            rows //= 2
            off, give = off + v * rows, off + (1 - v) * rows
        else:
            give = off
        copy = links.copy(acc.at[pl.ds(mult(give, 8), rows)], land.at[pl.ds(base, rows)], to)
        yield
        copy.wait_recv()
        links.sent(*before)
        before = [copy]
        if not ok:
            links.sent(copy)
            before = []

        def add(i, off=off, base=base):
            at = pl.ds(mult(off + i * 8, 8), 8)
            acc[at] = acc[at] + land[pl.ds(mult(base + i * 8, 8), 8)]

        loop(rows // 8, add)
        base += rows
        if ok:
            kept.append((to, parent, off, rows))
    links.sent(*before)
    return off, rows


def place_rows(acc, off, rows, whole):
    def one(i):
        whole(off + i * 8, 8)[...] = acc[pl.ds(mult(off + i * 8, 8), 8)]

    loop(rows // 8, one)


def small_chain(place, links, plan, acc, land, out):
    whole = lambda row, rows: out.at[pl.ds(mult(row, 8), rows)]
    kept = []
    off, rows = yield from reduce_rows(place, links, plan, acc, land, kept)
    place_rows(acc, off, rows, whole)
    for to, _, off, rows in reversed(kept):
        copy = links.copy(whole(off, rows), whole(off, rows), to)
        yield
        copy.wait_recv()


def tiled(count):
    return count in (2, 4, 6, 8, 12, 24)


def carry_peers(count, s):
    if tiled(count):
        return [lax.rem(s + i, count) for i in range(1, count)]
    return [s + (1 - 2 * (s // (1 << k) % 2)) * (1 << k) for k in range(log2(count))]


def carry_scratch(count, n, inner):
    v = lambda *shape: pltpu.VMEM(shape, f32)
    if tiled(count):
        w = inner // (count // 2)
        return dict(got=v(count, 2, 8, w), back=v(count, 2, 8, w), got_sum=v(count, 1, w), tile_dec=v(count, 8, w))
    return dict(got=v(2 * log2(count), 2, n, inner), back=v(2, n, inner), tot=v(2, n, inner))


def carry(place, links, m, way):
    return (carry_tiles if tiled(place.sizes["seq"]) else carry_doubling)(place, links, m, way)


def carry_doubling(place, links, m, way):
    bits = log2(place.sizes["seq"])
    m.edges[way] = jnp.zeros_like(m.edges[way])
    m.back[way] = jnp.ones_like(m.back[way])
    m.tot[0] = m.ends[way]
    m.tot[1] = jnp.exp2(m.a2[...] * m.sums[...])
    for k, p in enumerate(carry_peers(place.sizes["seq"], place.s)):
        got = m.got.at[way * bits + k]
        copy = links.copy(m.tot, got, (p, place.b))
        copy.wait_recv()
        links.sent(copy)
        later = place.bit(("seq", k))

        @pl.when(later == 1 - way)
        def _():
            m.edges[way] += m.back[way] * got[0]
            m.back[way] *= got[1]
            m.tot[0] += m.tot[1] * got[0]

        @pl.when(later == way)
        def _():
            m.tot[0] = got[0] + got[1] * m.tot[0]

        m.tot[1] *= got[1]
    yield
    yield


def carry_tiles(place, links, m, way):
    count, s, b = place.sizes["seq"], place.s, place.b
    across = count // 2
    width = m.ends.shape[2] // across
    peers = carry_peers(count, s)

    def cut(ref, p):
        return ref.at[pl.ds(mult(p // across * 8, 8), 8), pl.ds(mult(p % across * width, LANES), width)]

    def cut_sum(p):
        return m.sums.at[:, pl.ds(mult(p % across * width, LANES), width)]

    one, two, three = links.group(), links.group(), links.group()
    others = pl.ds(0, count - 1)
    first = [links.copy(cut(m.ends.at[way], p), m.got.at[s, way], (p, b), group=one) for p in peers]
    m.got[s, way] = cut(m.ends.at[way], s)[...]
    if way == 0:
        first += [links.copy(cut_sum(p), m.got_sum.at[s], (p, b), group=three) for p in peers]
        m.got_sum[s] = cut_sum(s)[...]
    yield
    links.take(m.got.at[others, way], one)
    if way == 0:
        links.take(m.got_sum.at[others], three)
        a2 = cut(m.a2, s)[...]
        for p in range(count):
            m.tile_dec[p] = jnp.exp2(a2 * m.got_sum[p])
    value = jnp.zeros((8, width), f32)
    for p in reversed(range(count)) if way else range(count):
        m.back[p, way] = value
        value = m.got[p, way] + m.tile_dec[p] * value
    second = [links.copy(m.back.at[p, way], cut(m.edges.at[way], s), (p, b), group=two) for p in peers]
    cut(m.edges.at[way], s)[...] = m.back[s, way]
    links.sent(*first)
    yield
    links.take(m.back.at[others, way], two)
    links.sent(*second)


def wide(tile, width=SCAN):
    return jnp.concatenate([tile] * (width // LANES), axis=1)


def spread(row, n):
    return jnp.broadcast_to(row, (n, row.shape[1]))


def fold(value):
    return sum(value[:, k : k + LANES] for k in range(0, value.shape[1], LANES))


def scan_ends(m, lanes):
    a2 = m.a2[:, lanes]
    n = a2.shape[0]

    def chunk(i, h):
        at = pl.ds(pl.multiple_of(i * 8, 8), 8)
        s8, u8 = m.step[at, lanes], m.u[at, lanes]
        for j in range(8):
            b = wide(m.bb[pl.ds(pl.multiple_of((i * 8 + j) * n, 8), n)])
            h = jnp.exp2(spread(s8[j : j + 1], n) * a2) * h + spread(u8[j : j + 1], n) * b
        return h

    m.ends[0, :, lanes] = lax.fori_loop(0, m.step.shape[0] // 8, chunk, jnp.zeros_like(a2))


def scan_lams(m, lanes):
    a2 = m.a2[:, lanes]
    n = a2.shape[0]

    def chunk(i, held):
        dec, acc = held
        at = pl.ds(pl.multiple_of(i * 8, 8), 8)
        s8, d8 = m.step[at, lanes], m.d_res[at, lanes]
        for j in range(8):
            c = wide(m.cc[pl.ds(pl.multiple_of((i * 8 + j) * n, 8), n)])
            dec = dec * jnp.exp2(spread(s8[j : j + 1], n) * a2)
            acc = acc + dec * (spread(d8[j : j + 1], n) * c)
        return dec, acc

    zero = jnp.zeros_like(a2)
    m.ends[1, :, lanes] = lax.fori_loop(0, m.step.shape[0] // 8, chunk, (zero + 1.0, zero))[1]


def scan_out(m, lanes):
    a2 = m.a2[:, lanes]
    n = a2.shape[0]

    def chunk(i, h):
        at = pl.ds(pl.multiple_of(i * 8, 8), 8)
        s8, u8 = m.step[at, lanes], m.u[at, lanes]
        ys = []
        for j in range(8):
            t = pl.ds(pl.multiple_of((i * 8 + j) * n, 8), n)
            b, c = wide(m.bb[t], a2.shape[1]), wide(m.cc[t], a2.shape[1])
            h = jnp.exp2(spread(s8[j : j + 1], n) * a2) * h + spread(u8[j : j + 1], n) * b
            ys.append(jnp.sum(c * h, axis=0, keepdims=True))
        m.y[at, lanes] = jnp.concatenate(ys, axis=0)
        return h

    lax.fori_loop(0, m.step.shape[0] // 8, chunk, m.edges[0, :, lanes])


def scan_again(m, lanes, first):
    a2 = m.a2[:, lanes]
    n = a2.shape[0]
    tokens = m.step.shape[0]

    def ahead(i, h):
        at = pl.ds(pl.multiple_of(i * 8, 8), 8)
        s8, u8, d8 = m.step[at, lanes], m.u[at, lanes], m.d_res[at, lanes]
        for j in range(8):
            t = pl.ds(pl.multiple_of((i * 8 + j) * n, 8), n)
            m.h[i * 8 + j] = h
            h = jnp.exp2(spread(s8[j : j + 1], n) * a2) * h + spread(u8[j : j + 1], n) * wide(m.bb[t])
            part = fold(spread(d8[j : j + 1], n) * h)
            m.cg[t] = part if first else m.cg[t] + part
        return h

    lax.fori_loop(0, tokens // 8, ahead, m.edges[0, :, lanes])


def scan_back(m, lanes, first):
    a2 = m.a2[:, lanes]
    n = a2.shape[0]
    tokens = m.step.shape[0]

    def behind(i, held):
        q, rate = held
        r = tokens // 8 - 1 - i
        at = pl.ds(pl.multiple_of(r * 8, 8), 8)
        s8, u8, d8 = m.step[at, lanes], m.u[at, lanes], m.d_res[at, lanes]
        sg, lb = [None] * 8, [None] * 8
        for j in reversed(range(8)):
            t = pl.ds(pl.multiple_of((r * 8 + j) * n, 8), n)
            st = spread(s8[j : j + 1], n)
            lam = spread(d8[j : j + 1], n) * wide(m.cc[t]) + q
            q = jnp.exp2(st * a2) * lam
            dec = q * m.h[r * 8 + j]
            lb[j] = jnp.sum(lam * wide(m.bb[t]), axis=0, keepdims=True)
            sg[j] = jnp.sum(dec * a2, axis=0, keepdims=True)
            rate = rate + dec * st
            part = fold(lam * spread(u8[j : j + 1], n))
            m.bg[t] = part if first else m.bg[t] + part
        lb8, sg8 = jnp.concatenate(lb, axis=0), jnp.concatenate(sg, axis=0)
        m.sg[at, lanes] = LN2 * sg8 + m.mixed[at, lanes] * lb8
        m.gate[at, lanes] = s8 * lb8
        return q, rate

    _, rate = lax.fori_loop(0, tokens // 8, behind, (m.edges[1, :, lanes], jnp.zeros_like(a2)))
    m.rate[:, lanes] = rate


class Refs:
    pass


FETCH = ["x", "gain", "g", "w_out", "conv_w", "conv_b", "x_proj", "step_proj", "step_b", "code", "a2", "skip"]
ARGS = [v + "_h" for v in FETCH] + ["w_in"]
OUTS = ["block_out", "input_grad", "in_sum", "out_sum", "small_sum", "gain_sum"]


UNITS = ["o0", "o1", "i0", "i1", "x0", "x1"]


def parts(unit):
    return [unit + "ab"[k] for k in range(PARTS.get(unit, 1))]


def recvs(sizes):
    bits, count = log2(sizes["seq"]), sizes["seq"]
    total = 2 + 2 + 2 * len(UNITS) + (6 if tiled(count) else 2 * bits)
    total += 2 * len(small_plan(sizes)) + sum(halvings(SMALL[0], len(small_plan(sizes))))
    for unit in UNITS:
        for p in parts(unit):
            total += bits + 4 + sum(halvings(LANES * 3 // len(parts(unit)), bits)) - 1
    return total


def scratch(sizes, tokens, width, inner, n, rank, taps):
    full = (tokens, inner)
    half, part = inner // 2, width // 2
    stages = log2(sizes["seq"])
    v = lambda *shape: pltpu.VMEM(shape, f32)
    sh = {name: v(*full) for name in ("gate", "d_res", "conv", "mixed", "pre", "step", "u", "y", "d_gate", "sg")}
    sh.update(
        x=v(tokens, width), g=v(tokens, width), vec=v(4, inner), gain=v(width // LANES, LANES),
        conv_b=v(inner // LANES, LANES), step_b=v(inner // LANES, LANES), skip=v(inner // LANES, LANES),
        code=pltpu.VMEM((inner // LANES, LANES), jnp.int32), conv_w=v(taps, inner), x_proj=v(rank + 2 * n, inner),
        step_proj=v(rank, inner), a2=v(n, inner), w_out=v(inner, width),
        normed=v(tokens, width), hid=v(8 + tokens, inner), cgr=v(tokens + 8, inner), proj=v(tokens, LANES),
        wbuf=v(SLOTS, width, WBLOCK), acc=v(tokens, width),
        bb=v(tokens * n, LANES), cc=v(tokens * n, LANES), bg=v(tokens * n, LANES), cg=v(tokens * n, LANES),
        h=v(tokens, n, SCAN), rate=v(n, inner), ends=v(2, n, inner), edges=v(2, n, inner), sums=v(1, inner),
        ng=v(4, tokens, part), gg=v(4, tokens, part),
        gains=v(8, LANES), gains_land=v(landing_rows(8, len(small_plan(sizes))), LANES),
        small=v(*SMALL), small_land=v(landing_rows(SMALL[0], len(small_plan(sizes))), SMALL[1]),
    )
    for unit in UNITS:
        sh["late_" + unit] = v(4, tokens, part)
        for p in parts(unit):
            rows = part // len(parts(unit))
            sh["tile_" + p] = v(rows, part)
            sh["land_" + p] = v(landing_rows(rows, stages), part)
    sh.update(carry_scratch(sizes["seq"], n, inner))
    sh["send"] = pltpu.SemaphoreType.DMA((SENDS,))
    sh["recv"] = pltpu.SemaphoreType.DMA((recvs(sizes),))
    sh["wsem"] = pltpu.SemaphoreType.DMA((SLOTS,))
    sh["isem"] = pltpu.SemaphoreType.DMA((len(FETCH),))
    return sh


def stream(m, first, last):
    def fetch(i, slot):
        cols = pl.ds(mult((first + i) * WBLOCK, WBLOCK), WBLOCK)
        return pltpu.make_async_copy(m.w_in.at[:, cols], m.wbuf.at[slot], m.wsem.at[slot])

    ahead = SLOTS - 1
    for k in range(ahead):
        fetch(k, k).start()

    def run(use):
        def body(i):
            slot = lax.rem(i, SLOTS)
            fetch(i, slot).wait()

            @pl.when(i + ahead < last - first)
            def _():
                fetch(i + ahead, lax.rem(i + ahead, SLOTS)).start()

            use(i, m.wbuf[slot])

        loop(last - first, body)

    return run


def late_chain(place, links, m, unit, value, left, right):
    late = getattr(m, "late_" + unit)
    width = late.shape[2]
    shift = int(unit[1]) * width
    mine = place.y if unit[0] == "o" else place.x
    to, _ = place.near(0, 1, 0) if unit[0] == "o" else place.near(1, 0, 0)
    core, _ = place.near(0, 0, 1)
    both = links.group()

    def cut(which):
        return value.at[:, pl.ds(mult(which * 2 * width + shift, LANES), width)]

    def pass_on(which):
        slot = late.at[which * 2 + place.c]
        return links.copy(slot, slot, core, group=both)

    sent = links.copy(cut(1 - mine), late.at[mine * 2 + place.c], to)
    late[mine * 2 + place.c] = cut(mine)[...]
    passed = [pass_on(mine)]
    yield
    sent.wait_recv()
    passed.append(pass_on(1 - mine))
    yield
    links.take(late.at[pl.ds(0, 2)], both)
    links.sent(sent, *passed)
    for i in range(2):
        cell = matmul(left(i), right(i), ((0,), (0,)))
        rows = cell.shape[0] // len(parts(unit))
        for k, p in enumerate(parts(unit)):
            tile = getattr(m, "tile_" + p)
            value = cell[k * rows : (k + 1) * rows]
            tile[...] = value if i == 0 else tile[...] + value


def piece_chain(place, links, m, p, zplan, out, base):
    acc, land = getattr(m, "tile_" + p), getattr(m, "land_" + p)
    rows, cols = acc.shape
    key, shift, r0 = p[0], int(p[1]) * m.x.shape[1] // 2, "ab".index(p[2]) * rows
    part = cols
    half = 2 * part
    bit = ("seq", 0) if key == "o" else ("batch", 1)
    x, y, c = place.x, place.y, place.c
    core, _ = place.near(0, 0, 1)

    def region(at, row, count):
        xx, yy = at
        if key == "o":
            top, side = yy * half + shift + r0 + xx * (rows // 2) + row, c * part
        else:
            top, side = c * part + r0 + yy * (rows // 2) + row, base + xx * half + shift
        return out.at[pl.ds(mult(top, 8), count), pl.ds(mult(side, LANES), cols)]

    kept = []
    off, count = yield from reduce_rows(place, links, [(bit, bit)] + zplan, acc, land, kept)
    edge = kept[0][2]
    place_rows(acc, off, count, lambda row, n: region((x, y), row - edge, n))
    row = off - edge
    held, across, to_core = [(x, y)], [], links.group()

    def give(at, to, group=None):
        ref = region(at, row, count)
        return links.copy(ref, ref, to, group=group)

    steps = list(reversed(kept[1:]))
    kind = SPREAD.get(p, "T1")
    steps.insert({"T1": len(steps), "T2": 0, "T3": 1}[kind], None)
    for i, step in enumerate(steps):
        last = i == len(steps) - 1
        if step is not None:
            to, parent, _, size = step
            step_copies = links.group()
            copies = [give(at, to, step_copies) for at in held]
            yield
            links.take(out.at[pl.ds(0, len(held) * count), pl.ds(0, cols)], step_copies)
            links.sent(*copies)
            row, count = parent - edge, 2 * size
            continue
        first, at_a = place.near(1 - c, c, 0)
        second, at_b = place.near(c, 1 - c, 0)
        _, at_d = place.near(1, 1, 0)
        a, b = give((x, y), first), give((x, y), second)
        held = [(x, y), at_a, at_b, at_d]

        def onward(at):
            if last:
                across.append(give(at, core, to_core))

        onward((x, y))
        yield
        a.wait_recv()
        d = give(at_a, second)
        onward(at_a)
        yield
        b.wait_recv()
        onward(at_b)
        yield
        d.wait_recv()
        links.sent(a, b)
        onward(at_d)
    if not across:
        across = [give(at, core, to_core) for at in held]
    yield
    links.take(out.at[pl.ds(0, 2 * rows), pl.ds(0, cols)], to_core)


def block_kernel(sizes, names, *refs):
    m = Refs()
    for name, ref in zip(ARGS + OUTS + names, refs):
        setattr(m, name, ref)
    place = Place(sizes)
    links = Links(m.send, m.recv)
    s, b, c = place.s, place.b, place.c
    count = sizes["seq"]
    tokens, width = m.x.shape
    inner, n = m.a2.shape[1], m.a2.shape[0]
    rank = m.step_proj.shape[0]
    taps = m.conv_w.shape[0]
    half, part = inner // 2, width // 2
    blocks_of_half = inner // WBLOCK
    last = s == count - 1

    fetched = {}
    for i, name in enumerate(FETCH):
        fetched[name] = pltpu.make_async_copy(getattr(m, name + "_h"), getattr(m, name), m.isem.at[i])
    for name in FETCH[:3]:
        fetched[name].start()
    to_hidden = stream(m, 0, blocks_of_half)
    for name in FETCH[3:]:
        fetched[name].start()
    bar = pltpu.get_barrier_semaphore()
    greet = [place.near(*d)[0] for d in GROUP[1:]] + [(p, b) for p in carry_peers(count, s)]
    if not tiled(count):
        greet += [(lax.rem(s + 1, count), b), (lax.rem(s + count - 1, count), b)]
    for to in greet:
        pl.semaphore_signal(bar, inc=1, device_id=to, device_id_type=MESH)

    fetched["x"].wait()
    fetched["gain"].wait()

    def to_row(name, k):
        ref = getattr(m, name)
        for j in range(ref.shape[0]):
            m.vec[k : k + 1, j * LANES : (j + 1) * LANES] = ref[j : j + 1]

    to_row("gain", 3)
    x = m.x[...]
    rms = lax.rsqrt(jnp.mean(x * x, axis=1, keepdims=True) + EPSILON)
    scaled = x * m.vec[3:4, :width]
    m.normed[...] = scaled * rms
    left = stacked(scaled)

    def hidden_block(i, w):
        m.hid[pl.ds(8, tokens), pl.ds(mult(i * WBLOCK, WBLOCK), WBLOCK)] = rms * rows_matmul(left, w, ((1,), (0,)))

    to_hidden(hidden_block)
    to_gate = stream(m, blocks_of_half, 2 * blocks_of_half)
    pl.semaphore_wait(bar, len(greet))
    halo = links.copy(m.hid.at[pl.ds(tokens, 8)], m.hid.at[pl.ds(0, 8)], (lax.rem(s + 1, count), b), start=False)

    @pl.when(jnp.logical_not(last))
    def _():
        halo.start()

    fetched["g"].wait()
    early, early_n, early_g = [], links.group(), links.group()
    for d in GROUP:
        to, _ = place.near(*d)
        cols = pl.ds(mult((c + d[2] * (1 - 2 * c)) * part, LANES), part)
        if not d[1]:
            early.append(links.copy(m.normed.at[:, cols], m.ng.at[place.x * 2 + c], to, group=early_n))
        if not d[0]:
            early.append(links.copy(m.g.at[:, cols], m.gg.at[place.y * 2 + c], to, group=early_g))
    own = pl.ds(mult(c * part, LANES), part)
    m.ng[place.x * 2 + c] = m.normed[:, own]
    m.gg[place.y * 2 + c] = m.g[:, own]


    for name in FETCH[3:]:
        fetched[name].wait()
    m.step_b[...] = m.step_b[...] - 0.5 * m.code[...].astype(f32)
    for k, name in enumerate(("conv_b", "step_b", "skip")):
        to_row(name, k)
    m.a2[...] = -LOG2E * jnp.exp(m.a2[...])
    def convolve(i):
        window = m.hid[pl.ds(mult(i * 8, 8), 16)]
        v = m.vec[0:1]
        for k in range(taps):
            o = 8 - taps + 1 + k
            v = v + m.conv_w[k : k + 1] * window[o : o + 8]
        at = pl.ds(mult(i * 8, 8), 8)
        m.conv[at] = v
        m.mixed[at] = v * sigmoid(v)

    loop(tokens // 8 - 1, lambda i: convolve(i + 1))

    @pl.when(s > 0)
    def _():
        halo.wait_recv()

    @pl.when(s == 0)
    def _():
        m.hid[pl.ds(0, 8)] = jnp.zeros((8, inner), f32)

    convolve(0)

    proj = matmul(m.mixed[...], m.x_proj[...], ((1,), (1,)))
    m.proj[:, : proj.shape[1]] = proj
    for j in range(n):
        at = pl.ds(j, tokens, stride=n)
        m.bb[at] = jnp.broadcast_to(proj[:, rank + j : rank + j + 1], (tokens, LANES))
    low_left = stacked(proj[:, :rank])

    def step_block(i):
        cols = pl.ds(mult(i * WBLOCK, WBLOCK), WBLOCK)
        pre = rows_matmul(low_left, m.step_proj[:, cols], ((1,), (0,))) + m.vec[1:2, cols]
        step = jnp.maximum(pre, 0.0) + jnp.log1p(jnp.exp(-jnp.abs(pre)))
        m.pre[:, cols] = pre
        m.step[:, cols] = step
        m.u[:, cols] = step * m.mixed[:, cols]
        m.sums[:, cols] = jnp.sum(step, axis=0, keepdims=True)

    loop(blocks_of_half, step_block)

    blocks = [slice(k, k + SCAN) for k in range(0, inner, SCAN)]
    for lanes in blocks:
        scan_ends(m, lanes)
    ahead = carry(place, links, m, 0)
    next(ahead)
    g_left = stacked(m.g[...])

    def d_gated_block(i):
        cols = pl.ds(mult(i * WBLOCK, WBLOCK), WBLOCK)
        m.d_res[:, cols] = rows_matmul(g_left, m.w_out[cols], ((1,), (1,)))

    loop(blocks_of_half, d_gated_block)
    for j in range(n):
        at = pl.ds(j, tokens, stride=n)
        m.cc[at] = jnp.broadcast_to(m.proj[:, rank + n + j : rank + n + j + 1], (tokens, LANES))

    def gate_block(i, w):
        cols = pl.ds(mult(i * WBLOCK, WBLOCK), WBLOCK)
        z = rms * rows_matmul(left, w, ((1,), (0,)))
        sg = sigmoid(z)
        act = z * sg
        d = m.d_res[:, cols]
        m.gate[:, cols] = act
        m.d_res[:, cols] = d * act
        m.d_gate[:, cols] = d * (sg * (1.0 + z * (1.0 - sg)))

    to_gate(gate_block)
    next(ahead)
    for lanes in blocks:
        scan_lams(m, lanes)
    behind = carry(place, links, m, 1)
    next(behind)
    for _ in ahead:
        pass
    def finish_quarters(k):
        for first in (k * part, half + k * part):
            cols = slice(first, first + part)
            scan_out(m, cols)

            def rows(i):
                at = pl.ds(mult(i * 8, 8), 8)
                result = m.y[at, cols] + m.vec[2:3, cols] * m.mixed[at, cols]
                m.y[at, cols] = result * m.gate[at, cols]
                m.d_gate[at, cols] = m.d_gate[at, cols] * result

            loop(tokens // 8, rows)

    s_bits, b_bits = all_bits(sizes)
    zplan = [(k, k) for k in s_bits[1:] + b_bits[2:]]
    chains, v = {}, Refs()

    def pair(ref):
        return lambda i: ref[pl.ds(2 * i, 2)].reshape(2 * tokens, ref.shape[2])

    def go(name):
        try:
            next(chains[name])
        except StopIteration:
            del chains[name]
            if name in UNITS:
                where = {"o": (m.out_sum, 0), "i": (m.in_sum, inner), "x": (m.in_sum, 0)}[name[0]]
                for p in parts(name):
                    chains[p] = piece_chain(place, links, m, p, zplan, *where)

    def late(key, value, left, right, which=(0, 1)):
        for unit in (key + str(k) for k in which):
            ref = getattr(m, "late_" + unit)
            chains[unit] = late_chain(place, links, m, unit, value, pair(ref if left is None else left), pair(ref if right is None else right))

    column = lax.broadcasted_iota(jnp.int32, (tokens, LANES), 1)
    zero = jnp.zeros((8, inner), f32)

    def collect(ref, base, total):
        for j in range(n):
            rows = jnp.sum(ref[pl.ds(j, tokens, stride=n)], axis=1, keepdims=True)
            total = total + jnp.where(column == base + j, rows, 0.0)
        return total

    def put_small(row, value):
        rows = value.shape[0]
        cut, top = SMALL[1], 80
        m.small[row : row + rows] = value[:, :cut]
        over = inner - cut
        if row < top:
            m.small[2 * top + row : 2 * top + row + rows, :over] = value[:, cut:]
        else:
            m.small[top + row : top + row + rows, over:] = value[:, cut:]

    def quarters(k):
        finish_quarters(k)
        late("o", m.y, None, m.gg, (k,))
        late("i", m.d_gate, m.ng, None, (k,))
        if k == 0:
            next(behind)

    def again(k):
        scan_again(m, blocks[k], k == 0)

    def back(k):
        if k == 0:
            for _ in behind:
                pass
            links.take(m.ng.at[pl.ds(0, 3)], early_n)
            links.take(m.gg.at[pl.ds(0, 3)], early_g)
            links.sent(*early)
        scan_back(m, blocks[k], k == 0)

    def pre():
        bc_grad = collect(m.cg, rank + n, collect(m.bg, rank, jnp.zeros((tokens, LANES), f32)))

        def rows(i, total):
            at = pl.ds(pl.multiple_of(i * 8, 8), 8)
            p = m.sg[at] * sigmoid(m.pre[at])
            m.sg[at] = p
            return total[0] + p, total[1] + m.d_res[at] * m.mixed[at]

        total = lax.fori_loop(0, tokens // 8, rows, (zero, zero))
        v.bias_grad, v.skip_grad = (jnp.sum(t, axis=0, keepdims=True) for t in total)
        low_grad = matmul(m.sg[...], m.step_proj[...], ((1,), (1,)))
        v.proj_grad = jnp.concatenate([low_grad, bc_grad[:, rank : rank + 2 * n]], axis=1)

    def mixg():
        pg_left = stacked(v.proj_grad)

        def block(i):
            cols = pl.ds(mult(i * WBLOCK, WBLOCK), WBLOCK)
            d = rows_matmul(pg_left, m.x_proj[:, cols], ((1,), (0,)))
            z = m.conv[:, cols]
            sg = sigmoid(z)
            d = d + m.gate[:, cols] + m.d_res[:, cols] * m.vec[2:3, cols]
            m.cgr[pl.ds(0, tokens), cols] = d * (sg * (1.0 + z * (1.0 - sg)))

        loop(blocks_of_half, block)
        v.halo_back = links.copy(
            m.cgr.at[pl.ds(0, 8)], m.cgr.at[pl.ds(tokens, 8)], (lax.rem(s + count - 1, count), b), start=False)

        @pl.when(s > 0)
        def _():
            v.halo_back.start()

    def xg():
        @pl.when(jnp.logical_not(last))
        def _():
            v.halo_back.wait_recv()

        @pl.when(last)
        def _():
            m.cgr[pl.ds(tokens, 8)] = jnp.zeros((8, inner), f32)

        def rows(i):
            window = m.cgr[pl.ds(mult(i * 8, 8), 16)]
            z = m.conv_w[0:1] * window[taps - 1 : taps + 7]
            for k in range(1, taps):
                o = taps - 1 - k
                z = z + m.conv_w[k : k + 1] * window[o : o + 8]
            m.gate[pl.ds(mult(i * 8, 8), 8)] = z

        loop(tokens // 8, rows)
        late("x", m.gate, m.ng, None)

    def taps_():
        def rows(i, total):
            at = pl.ds(pl.multiple_of(i * 8, 8), 8)
            window = m.hid[pl.ds(pl.multiple_of(i * 8, 8), 16)]
            z = m.cgr[at]
            o = 8 - taps + 1
            return tuple(t + z * window[o + k : o + k + 8] for k, t in enumerate(total[:-1])) + (total[-1] + z,)

        total = lax.fori_loop(0, tokens // 8, rows, (zero,) * (taps + 1))
        v.tap_rows = [jnp.sum(t, axis=0, keepdims=True) for t in total]

    def mid():
        put_small(0, matmul(v.proj_grad, m.mixed[...], ((0,), (0,))))
        put_small(rank + 2 * n, matmul(m.proj[:, :rank], m.sg[...], ((0,), (0,))))
        put_small(2 * rank + 2 * n, m.rate[...] * m.a2[...] * LN2)
        rows = v.tap_rows + [v.bias_grad, v.skip_grad, zero[:1]]
        put_small(2 * rank + 3 * n, jnp.concatenate(rows, axis=0))
        end = 2 * rank + 3 * n + 8
        m.small[end:160] = jnp.zeros((160 - end, SMALL[1]), f32)
        m.small[240:256] = jnp.zeros((16, SMALL[1]), f32)
        m.small[80 + end : 240, SMALL[1] // 2 :] = jnp.zeros((160 - end, SMALL[1] // 2), f32)
        chains["s"] = small_chain(place, links, small_plan(sizes), m.small, m.small_land, m.small_sum)

    def normed_block(ref):
        def use(i, w):
            d = stacked(ref[:, pl.ds(mult(i * WBLOCK, WBLOCK), WBLOCK)])
            m.acc[...] = m.acc[...] + rows_matmul(d, w, ((1,), (1,)))

        return use

    def ng0():
        m.acc[...] = jnp.zeros_like(m.acc)
        stream(m, blocks_of_half, 2 * blocks_of_half)(normed_block(m.d_gate))

    def ng1():
        stream(m, 0, blocks_of_half)(normed_block(m.gate))

    def inp():
        x = m.x[...]
        rms = lax.rsqrt(jnp.mean(x * x, axis=1, keepdims=True) + EPSILON)
        normed_grad = m.acc[...]
        gain_grad = jnp.sum(normed_grad * x * rms, axis=0, keepdims=True)
        weighted = normed_grad * m.vec[3:4, :width]
        m.input_grad[...] = rms * weighted - rms * rms * rms * x * jnp.mean(weighted * x, axis=1, keepdims=True) + m.g[...]
        for k in range(width // LANES):
            m.gains[k : k + 1] = gain_grad[:, k * LANES : (k + 1) * LANES]
        m.gains[width // LANES :] = jnp.zeros((8 - width // LANES, LANES), f32)
        chains["n"] = small_chain(place, links, small_plan(sizes), m.gains, m.gains_land, m.gain_sum)

    def bo():
        gl = stacked(m.y[...])

        def block(i):
            cols = pl.ds(mult(i * WBLOCK, WBLOCK), WBLOCK)
            m.block_out[:, cols] = m.x[:, cols] + rows_matmul(gl, m.w_out[:, cols], ((1,), (0,)))

        loop(width // WBLOCK, block)

    work = {
        "g0": lambda: quarters(0), "g1": lambda: quarters(1), "a0": lambda: again(0), "b0": lambda: back(0), "a1": lambda: again(1), "b1": lambda: back(1),
        "a2": lambda: again(2), "b2": lambda: back(2), "pre": pre, "mixg": mixg,
        "xg": xg, "taps": taps_, "mid": mid, "ng0": ng0, "ng1": ng1, "inp": inp, "bo": bo,
    }
    for name in ORDER:
        if name in work:
            work.pop(name)()
        elif name in chains:
            go(name)
    assert not work
    while chains:
        for name in list(chains):
            go(name)

    @pl.when(jnp.logical_not(last))
    def _():
        halo.wait_send()

    @pl.when(s > 0)
    def _():
        v.halo_back.wait_send()

    links.drain()


def unpack_kernel(rank, n, a_v, b_v, c_v, d_v, small, gains, a_o, b_o, c_o, d_o, x_proj_o, step_proj_o, decay_o, taps_o, *rest):
    row_os, sems = rest[:-1], rest[-1]
    copies = []
    for v, o, cuts in ((c_v, c_o, 8), (d_v, d_o, 4), (a_v, a_o, 1), (b_v, b_o, 1)):
        rows = v.shape[0] // cuts
        for k in range(cuts):
            at = pl.ds(k * rows, rows)
            copies.append(pltpu.make_async_copy(v.at[at], o.at[at], sems.at[len(copies)]))
    for c in copies:
        c.start()

    def take(row, rows):
        over = SMALL[1] // 2
        if row < 80:
            tail = small[160 + row : 160 + row + rows, :over]
        else:
            tail = small[80 + row : 80 + row + rows, over:]
        return jnp.concatenate([small[row : row + rows], tail], axis=1)

    x_proj_o[...] = take(0, rank + 2 * n)
    step_proj_o[...] = take(rank + 2 * n, rank)
    decay_o[...] = take(2 * rank + 2 * n, n)
    rows = take(2 * rank + 3 * n, 8)
    taps = taps_o.shape[0]
    taps_o[...] = rows[:taps]
    row_os[3][...] = gains[: row_os[3].shape[0]]
    for k, ref in enumerate(row_os[:3]):
        for j in range(ref.shape[0]):
            ref[j : j + 1] = rows[taps + k : taps + k + 1, j * LANES : (j + 1) * LANES]
    for c in copies:
        c.wait()


VMEM = pl.BlockSpec(memory_space=pltpu.VMEM)
ANY = pl.BlockSpec(memory_space=pl.ANY)


def shards(sizes, inputs, norm_gain, w_in, conv_weight, conv_bias, x_proj, step_proj, step_bias, decay_code, decay_log,
           skip_gain, w_out, cotangent):
    seqs, tokens, width = inputs.shape
    assert seqs == 1 and sizes["batch"] == 4 and sizes["seq"] % 2 == 0
    inner = w_in.shape[1] // 2
    rank, n, taps = step_proj.shape[0], decay_log.shape[1], conv_weight.shape[0]
    sh = scratch(sizes, tokens, width, inner, n, rank, taps)
    tall = lambda u: u.reshape(-1, LANES)
    args = dict(
        x=inputs[0], g=cotangent[0], gain=tall(norm_gain), conv_w=conv_weight, conv_b=tall(conv_bias), x_proj=x_proj.T,
        step_proj=step_proj, step_b=tall(step_bias), code=tall(decay_code), a2=decay_log.T, skip=tall(skip_gain), w_out=w_out)
    held = [pltpu.VMEM(v, f32) for v in ((tokens, width), (tokens, width), (width, 2 * inner), (inner, width), SMALL, (8, LANES))]
    sums = pl.pallas_call(
        functools.partial(block_kernel, sizes, list(sh)),
        in_specs=[ANY] * len(ARGS),
        out_specs=[VMEM] * 6,
        out_shape=held,
        scratch_shapes=list(sh.values()),
        compiler_params=pltpu.CompilerParams(collective_id=1, has_side_effects=True, vmem_limit_bytes=VLIMIT << 19),
        name="block",
    )(*(args[a] for a in FETCH), w_in)
    wanted = [v.shape for v in sums[:4]] + [(rank + 2 * n, inner), (rank, inner), (n, inner), (taps, inner)]
    wanted += [(inner // LANES, LANES)] * 3 + [(width // LANES, LANES)]
    block_out, input_grad, in_sum, out_sum, x_proj_sum, step_proj_sum, decay_sum, taps_sum, *rows = pl.pallas_call(
        functools.partial(unpack_kernel, rank, n),
        in_specs=[VMEM] * 6,
        out_specs=[ANY] * 4 + [VMEM] * 8,
        out_shape=[jax.ShapeDtypeStruct(v, f32) for v in wanted],
        scratch_shapes=[pltpu.SemaphoreType.DMA((14,))],
        compiler_params=pltpu.CompilerParams(vmem_limit_bytes=VLIMIT2 << 19),
        name="unpack",
    )(*sums)
    conv_b_sum, step_b_sum, skip_sum, gain_sum = (v.reshape(-1) for v in rows)
    return (block_out[None], input_grad[None], gain_sum, in_sum, taps_sum, conv_b_sum, x_proj_sum.T, step_proj_sum, step_b_sum,
            decay_sum.T, skip_sum, out_sum)


VLIMIT, VLIMIT2 = 97, 16


def solution(mesh):
    rows = P("batch", "seq", None)
    return jax.shard_map(
        functools.partial(shards, dict(mesh.shape)),
        mesh=mesh,
        in_specs=(rows,) + (P(),) * 11 + (rows,),
        out_specs=(rows, rows) + (P(),) * 10,
        check_vma=False,
    )
```
